256 devices in a mesh: src: 8 (over z_hi, core), gx: 8 (over x, z_lo), gy: 4 (over y).
Axes of the slice: x: 4, y: 4, z: 8 (z_hi: 4, z_lo: 2; z = z_hi * 2 + z_lo), core: 2. Of those that a mesh axis runs over, the one named last changes fastest.
Arguments:
- labels: int32 [64, 128, 128], P('gx', 'gy'), may hold values from 0 to 15
- kappa_table: float32 [16], replicated, may hold values from 0.5 to 2
- absorb_table: float32 [16], replicated, may hold values from 0.02 to 0.1
- background: float32 [32, 64, 128, 128], P('src', 'gx', 'gy'), may hold values from 0.1 to 10
- det_cells: int32 [1024], replicated, may hold values from 0 to 1048575
- v_kappa: float32 [64, 128, 128], P('gx', 'gy', 'src'), may hold values from -6 to 6
- v_absorb: float32 [64, 128, 128], P('gx', 'gy', 'src'), may hold values from -6 to 6
- q_kappa: float32 [64, 128, 128], P('gx', 'gy', 'src'), may hold values from -6 to 6
- q_absorb: float32 [64, 128, 128], P('gx', 'gy', 'src'), may hold values from -6 to 6
- beta_prev: float32 [1], replicated, may hold values from 0.2 to 2
Outputs:
- next_kappa: float32 [64, 128, 128], P('gx', 'gy', 'src')
- next_absorb: float32 [64, 128, 128], P('gx', 'gy', 'src')
- coefs: float32 [2], replicated
The draws below stay inside these ranges and needn't reach their ends.
Inputs may be any that keep to these rules, and one draw needn't show every extreme that they name: `labels`: a region number for every cell. `det_cells`: flat index (x * 128 + y) * 128 + z of a grid cell; indices may repeat.
All inputs are finite; a program needn't handle non-finite values.
Results may differ from the reference program's by a relative error of at most 0.0001.
Values sent between devices are 32-bit elements; how exact they have to be, the bound alone decides.
A program may use at most 128 MiB of HBM per device.

```python
import math
import jax
import jax.numpy as jnp
from jax import lax

DETS = 1024
REGIONS = 16
ITERS = 6
NX = 64
NY = 128
NZ = 128
SOURCES = 32
CELLS = 1048576


def place_ends(values, stream_key, smallest, largest):
    dims = values.shape
    index_at = [jax.random.randint(jax.random.fold_in(stream_key, axis), (), 0, dims[axis]) for axis in range(len(dims))]
    values = values.at[tuple(index_at)].set(smallest)
    longest = dims.index(max(dims))
    index_at[longest] = (index_at[longest] + 1) % dims[longest]
    return values.at[tuple(index_at)].set(largest)


def steps_of(key, shape, pieces, least, top_value):
    level, own = 1.0, jax.random.fold_in(key, 6)
    for axis_at, parts in pieces:
        steps = jnp.exp(jax.random.uniform(jax.random.fold_in(own, axis_at), (parts,), jnp.float32, least / len(pieces), top_value / len(pieces)))
        level = level * jnp.repeat(steps, shape[axis_at] // parts).reshape([-1 if axis == axis_at else 1 for axis in range(len(shape))])
    return level


def normal_values(rng, dims, width, most, shards=(), dtype=jnp.bfloat16):
    drawn = jax.random.normal(rng, dims, jnp.float32) * width
    if len(shards) > 0:
        drawn = steps_of(rng, dims, shards, -0.22, 0.18) * drawn
    return jnp.clip(drawn, min=-most, max=most).astype(dtype)


def setup_inputs(seed: int = 0) -> dict:
    keys = jax.random.split(jax.random.key(seed), 11)
    labels = place_ends(jax.random.randint(keys[0], (NX, NY, NZ), 0, REGIONS), jax.random.fold_in(keys[0], 1), 0, REGIONS - 1).astype(jnp.int32)
    kappa_table = jnp.clip(jnp.exp(jax.random.uniform(keys[1], (REGIONS,), jnp.float32, math.log(0.5), math.log(2.0))), 0.5, 2.0)
    absorb_table = jnp.clip(jnp.exp(jax.random.uniform(keys[2], (REGIONS,), jnp.float32, math.log(0.02), math.log(0.1))), 0.02, 0.1)
    background = jnp.clip(jnp.exp(math.log(10.0) - 4.6051702 * jax.random.uniform(keys[3], (SOURCES, NX, NY, NZ), jnp.float32) ** steps_of(keys[3], (SOURCES, NX, NY, NZ), ((0, 8), (1, 8), (2, 4)), -0.2, 0.2)), 0.1, 10.0)
    det_cells = place_ends(jax.random.randint(keys[4], (DETS,), 0, NX * NY * NZ), jax.random.fold_in(keys[4], 1), 0, (NX * NY * NZ) - 1).astype(jnp.int32)
    v_kappa = normal_values(keys[5], (NX, NY, NZ), 1.0, 6.0, ((0, 8), (1, 4), (2, 8)), jnp.float32)
    v_absorb = normal_values(keys[6], (NX, NY, NZ), 1.0, 6.0, ((0, 8), (1, 4), (2, 8)), jnp.float32)
    q_kappa = normal_values(keys[7], (NX, NY, NZ), 1.0, 6.0, ((0, 8), (1, 4), (2, 8)), jnp.float32)
    q_absorb = normal_values(keys[8], (NX, NY, NZ), 1.0, 6.0, ((0, 8), (1, 4), (2, 8)), jnp.float32)
    beta_prev = jnp.clip(jnp.exp(jax.random.uniform(keys[9], (1,), jnp.float32, math.log(0.2), math.log(2.0))), 0.2, 2.0)
    return dict(labels=labels, kappa_table=kappa_table, absorb_table=absorb_table, background=background, det_cells=det_cells, v_kappa=v_kappa, v_absorb=v_absorb, q_kappa=q_kappa, q_absorb=q_absorb, beta_prev=beta_prev)


lam_low = 0.02
lam_high = 24.1
eps_norm = 1e-06

def regional(labels, table):
    field = jnp.zeros(labels.shape, jnp.float32)
    for region in range(REGIONS):
        field = field + jnp.where(labels == region, table[region], 0.0)
    return field

def beside(field):
    padded = jnp.pad(field, 1)
    return [padded[2:, 1:-1, 1:-1], padded[:-2, 1:-1, 1:-1], padded[1:-1, 2:, 1:-1], padded[1:-1, :-2, 1:-1], padded[1:-1, 1:-1, 2:], padded[1:-1, 1:-1, :-2]]

def chebyshev(rhs, apply_op):
    theta = 0.5 * (lam_high + lam_low)
    delta = 0.5 * (lam_high - lam_low)
    sigma = theta / delta
    rho = 1.0 / sigma
    solution = jnp.zeros_like(rhs)
    remain = rhs
    step_dir = rhs / theta
    for step in range(ITERS):
        solution = solution + step_dir
        if step + 1 < ITERS:
            remain = remain - apply_op(step_dir)
            rho_next = 1.0 / (2.0 * sigma - rho)
            step_dir = rho_next * rho * step_dir + 2.0 * rho_next / delta * remain
            rho = rho_next
    return solution

def reference(labels, kappa_table, absorb_table, background, det_cells, v_kappa, v_absorb, q_kappa, q_absorb, beta_prev):
    kappa = regional(labels, kappa_table)
    absorb = regional(labels, absorb_table)
    kappa_faces = [0.5 * (kappa + near) for near in beside(kappa)]
    vk_faces = [0.5 * (v_kappa + near) for near in beside(v_kappa)]

    def apply_op(field):
        result = absorb * field
        for face, near in zip(kappa_faces, beside(field)):
            result = result + face * (field - near)
        return result

    def one_source(carry, phi):
        rhs = v_absorb * phi
        for face, near in zip(vk_faces, beside(phi)):
            rhs = rhs + face * (phi - near)
        rhs = -rhs
        change = chebyshev(rhs, apply_op)
        seen = change.reshape(-1)[det_cells]
        base = phi.reshape(-1)[det_cells]
        total = jnp.sum(base)
        mean_base = total / DETS
        ratio = base / total
        jv_vals = (seen - ratio * jnp.sum(seen)) / mean_base
        weight = (jv_vals - jnp.sum(ratio * jv_vals)) / mean_base
        source = jnp.zeros((CELLS,), jnp.float32).at[det_cells].add(weight).reshape(phi.shape)
        dual = chebyshev(source, apply_op)
        grad_a = -phi * dual
        grad_k = jnp.zeros_like(phi)
        for near_phi, near_dual in zip(beside(phi), beside(dual)):
            grad_k = grad_k - 0.5 * (phi - near_phi) * (dual - near_dual)
        return ((carry[0] + grad_k, carry[1] + grad_a), None)
    zero_field = jnp.zeros_like(kappa)
    (hv_k, hv_a), _ = lax.scan(one_source, (zero_field, zero_field), background)
    w_k = hv_k - beta_prev[0] * q_kappa
    w_a = hv_a - beta_prev[0] * q_absorb
    wv_mean = (jnp.sum(w_k * v_kappa) + jnp.sum(w_a * v_absorb)) / CELLS
    vv_mean = (jnp.sum(v_kappa * v_kappa) + jnp.sum(v_absorb * v_absorb)) / CELLS
    alpha = wv_mean / (vv_mean + eps_norm)
    r_k = w_k - alpha * v_kappa
    r_a = w_a - alpha * v_absorb
    rr_mean = (jnp.sum(r_k * r_k) + jnp.sum(r_a * r_a)) / CELLS
    beta = jnp.sqrt(rr_mean + eps_norm)
    return (r_k / beta, r_a / beta, jnp.stack([alpha, beta]))
```

```python
import functools

import jax
import jax.numpy as jnp
from jax import lax
from jax.experimental import pallas as pl
from jax.experimental.pallas import tpu as pltpu
from jax.sharding import PartitionSpec as P

ITERS = 6
MESH = pl.DeviceIdType.MESH


lam_low = 0.02
lam_high = 24.1
eps_norm = 1e-06


def _exchange_kernel(axis, n, scatter, x_ref, o_ref, slots, send_sem, recv_sem, local_sem):
    me = lax.axis_index(axis)
    barrier = pltpu.get_barrier_semaphore()
    for k in range(1, n):
        peer = lax.rem(me + k, n)
        pl.semaphore_signal(barrier, inc=1, device_id={axis: peer}, device_id_type=MESH)
    pl.semaphore_wait(barrier, n - 1)
    copies = []
    for k in range(1, n):
        peer = lax.rem(me + k, n)
        copy = pltpu.make_async_remote_copy(
            src_ref=x_ref.at[peer] if scatter else x_ref,
            dst_ref=slots.at[me],
            send_sem=send_sem.at[k - 1],
            recv_sem=recv_sem.at[k - 1],
            device_id={axis: peer},
            device_id_type=MESH,
        )
        copy.start()
        copies.append(copy)
    local = pltpu.make_async_copy(x_ref.at[me] if scatter else x_ref, slots.at[me], local_sem)
    local.start()
    local.wait()
    for copy in copies:
        copy.wait()
    o_ref[...] = slots[...]


def exchange(x, axis, cid, scatter=False):
    n = lax.axis_size(axis)
    block = x.shape[1:] if scatter else x.shape
    return pl.pallas_call(
        functools.partial(_exchange_kernel, axis, n, scatter),
        out_shape=jax.ShapeDtypeStruct((n,) + block, x.dtype),
        in_specs=[pl.BlockSpec(memory_space=pltpu.VMEM)],
        out_specs=pl.BlockSpec(memory_space=pltpu.VMEM),
        scratch_shapes=[
            pltpu.VMEM((n,) + block, x.dtype),
            pltpu.SemaphoreType.DMA((n - 1,)),
            pltpu.SemaphoreType.DMA((n - 1,)),
            pltpu.SemaphoreType.DMA,
        ],
        compiler_params=pltpu.CompilerParams(collective_id=cid, has_side_effects=True),
    )(x)


def small_sum(values, axes, first_id):
    count = values.shape[0]
    packed = jnp.pad(values, (0, 1024 - count)).reshape(8, 128)
    for i, axis in enumerate(axes):
        packed = jnp.sum(exchange(packed, axis, first_id + i), axis=0)
    return packed.reshape(-1)[:count]


def padded_2(block, sides, width):
    for axis, dim in sides:
        count = lax.axis_size(axis)
        forward = [(i, i + 1) for i in range(count - 1)]
        backward = [(target, source) for source, target in forward]
        low = lax.ppermute(
            lax.slice_in_dim(block, block.shape[dim] - width, None, axis=dim), axis, forward
        )
        high = lax.ppermute(lax.slice_in_dim(block, 0, width, axis=dim), axis, backward)
        block = jnp.concatenate([low, block, high], axis=dim)
    return block


def regional(labels, table):
    field = jnp.zeros(labels.shape, jnp.float32)
    for region in range(table.shape[0]):
        field = field + jnp.where(labels == region, table[region], 0.0)
    return field


def beside(padded):
    widths = [(0, 0)] * (padded.ndim - 1) + [(1, 1)]
    full = jnp.pad(padded, widths)
    return [
        full[..., 2:, 1:-1, 1:-1],
        full[..., :-2, 1:-1, 1:-1],
        full[..., 1:-1, 2:, 1:-1],
        full[..., 1:-1, :-2, 1:-1],
        full[..., 1:-1, 1:-1, 2:],
        full[..., 1:-1, 1:-1, :-2],
    ]


def chebyshev(rhs, apply_op):
    theta = 0.5 * (lam_high + lam_low)
    delta = 0.5 * (lam_high - lam_low)
    sigma = theta / delta
    rho = 1.0 / sigma
    solution = jnp.zeros_like(rhs)
    remain = rhs
    step_dir = rhs / theta
    for step in range(ITERS):
        solution = solution + step_dir
        if step + 1 < ITERS:
            remain = remain - apply_op(step_dir)
            rho_next = 1.0 / (2.0 * sigma - rho)
            step_dir = rho_next * rho * step_dir + 2.0 * rho_next / delta * remain
            rho = rho_next
    return solution


def per_device(
    labels,
    kappa_table,
    absorb_table,
    background,
    det_cells,
    v_kappa,
    v_absorb,
    q_kappa,
    q_absorb,
    beta_prev,
):
    sources, cx, cy, cz = background.shape
    kappa = regional(labels, kappa_table)
    absorb = regional(labels, absorb_table)
    n_src = lax.axis_size("src")
    slab = v_kappa.shape[2]
    pair = jnp.stack([v_kappa, v_absorb]).reshape(-1, 128)
    gathered = exchange(pair, "src", 0).reshape((n_src, 2, cx, cy, slab))
    full_k, full_a = jnp.transpose(gathered, (1, 2, 3, 0, 4)).reshape(2, cx, cy, cz)
    stacked = jnp.concatenate([background, kappa[None], full_k[None]], axis=0)
    rims = padded_2(stacked, (("gx", 1), ("gy", 2)), 1)
    near_all = beside(rims)
    kappa_faces = [0.5 * (kappa + near[sources]) for near in near_all]
    vk_faces = [0.5 * (full_k + near[sources + 1]) for near in near_all]
    phi_near = [near[:sources] for near in near_all]

    def apply_op(field):
        padded = padded_2(field, (("gx", 1), ("gy", 2)), 1)
        result = absorb * field
        for face, near in zip(kappa_faces, beside(padded)):
            result = result + face * (field - near)
        return result

    rhs = full_a * background
    for face, near in zip(vk_faces, phi_near):
        rhs = rhs + face * (background - near)
    rhs = -rhs
    change = chebyshev(rhs, apply_op)
    span_y = cy * lax.axis_size("gy")
    ix = det_cells // (span_y * cz)
    iy = det_cells // cz % span_y
    iz = det_cells % cz
    anchor_x = lax.axis_index("gx") * cx
    anchor_y = lax.axis_index("gy") * cy
    owned = (ix >= anchor_x) & (ix < anchor_x + cx) & (iy >= anchor_y) & (iy < anchor_y + cy)
    local = jnp.where(owned, ((ix - anchor_x) * cy + (iy - anchor_y)) * cz + iz, 0)
    seen = jnp.where(owned[None, :], change.reshape(sources, -1)[:, local], 0.0)
    base = jnp.where(owned[None, :], background.reshape(sources, -1)[:, local], 0.0)
    partial = jnp.stack(
        [
            jnp.sum(base, axis=1),
            jnp.sum(seen, axis=1),
            jnp.sum(base * seen, axis=1),
            jnp.sum(base * base, axis=1),
        ],
        axis=1,
    )
    sums = small_sum(partial.reshape(-1), ("gy", "gx"), 1).reshape(sources, 4, 1)
    total, seen_sum, cross, square = sums[:, 0], sums[:, 1], sums[:, 2], sums[:, 3]
    mean_base = total / det_cells.shape[0]
    ratio = base / total
    jv_vals = (seen - ratio * seen_sum) / mean_base
    ratio_jv = (cross / total - seen_sum * (square / (total * total))) / mean_base
    weight = (jv_vals - ratio_jv) / mean_base
    deposit = jnp.where(owned[None, :], weight, 0.0)
    source = (
        jnp.zeros((sources, cx * cy * cz), jnp.float32)
        .at[:, local]
        .add(deposit)
        .reshape(change.shape)
    )
    dual = chebyshev(source, apply_op)
    dual_rims = padded_2(dual, (("gx", 1), ("gy", 2)), 1)
    grad_a = -jnp.sum(background * dual, axis=0)
    grad_k = jnp.zeros_like(kappa)
    for near_phi, near_dual in zip(phi_near, beside(dual_rims)):
        grad_k = grad_k - 0.5 * jnp.sum((background - near_phi) * (dual - near_dual), axis=0)
    grads = jnp.stack([grad_k, grad_a]).reshape(2, cx, cy, n_src, slab)
    grads = jnp.transpose(grads, (3, 0, 1, 2, 4)).reshape(n_src, -1, 128)
    hv = jnp.sum(exchange(grads, "src", 3, scatter=True), axis=0).reshape(2, cx, cy, slab)
    hv_k, hv_a = hv[0], hv[1]
    cell_count = cx * lax.axis_size("gx") * cy * lax.axis_size("gy") * cz
    w_k = hv_k - beta_prev[0] * q_kappa
    w_a = hv_a - beta_prev[0] * q_absorb
    local_wv = jnp.sum(w_k * v_kappa) + jnp.sum(w_a * v_absorb)
    local_vv = jnp.sum(v_kappa * v_kappa) + jnp.sum(v_absorb * v_absorb)
    wv_sum, vv_sum = small_sum(jnp.stack([local_wv, local_vv]), ("gy", "gx", "src"), 4)
    alpha = wv_sum / cell_count / (vv_sum / cell_count + eps_norm)
    r_k = w_k - alpha * v_kappa
    r_a = w_a - alpha * v_absorb
    rr_sum = small_sum((jnp.sum(r_k * r_k) + jnp.sum(r_a * r_a))[None], ("gy", "gx", "src"), 7)[0]
    beta = jnp.sqrt(rr_sum / cell_count + eps_norm)
    return (r_k / beta, r_a / beta, jnp.stack([alpha, beta]))


def solution(mesh):
    return jax.shard_map(
        per_device,
        mesh=mesh,
        in_specs=(
            P("gx", "gy", None),
            P(),
            P(),
            P("src", "gx", "gy", None),
            P(),
            P("gx", "gy", "src"),
            P("gx", "gy", "src"),
            P("gx", "gy", "src"),
            P("gx", "gy", "src"),
            P(),
        ),
        out_specs=(P("gx", "gy", "src"), P("gx", "gy", "src"), P()),
        check_vma=False,
    )
```

```python
import functools

import jax
import jax.numpy as jnp
from jax import lax
from jax.experimental import pallas as pl
from jax.experimental.pallas import tpu as pltpu
from jax.sharding import PartitionSpec as P

ITERS = 6
MESH = pl.DeviceIdType.MESH


lam_low = 0.02
lam_high = 24.1
eps_norm = 1e-06


def _exchange_kernel(axis, n, scatter, x_ref, o_ref, slots, send_sem, recv_sem, local_sem):
    me = lax.axis_index(axis)
    barrier = pltpu.get_barrier_semaphore()
    for k in range(1, n):
        peer = lax.rem(me + k, n)
        pl.semaphore_signal(barrier, inc=1, device_id={axis: peer}, device_id_type=MESH)
    pl.semaphore_wait(barrier, n - 1)
    copies = []
    for k in range(1, n):
        peer = lax.rem(me + k, n)
        copy = pltpu.make_async_remote_copy(
            src_ref=x_ref.at[peer] if scatter else x_ref,
            dst_ref=slots.at[me],
            send_sem=send_sem.at[k - 1],
            recv_sem=recv_sem.at[k - 1],
            device_id={axis: peer},
            device_id_type=MESH,
        )
        copy.start()
        copies.append(copy)
    local = pltpu.make_async_copy(x_ref.at[me] if scatter else x_ref, slots.at[me], local_sem)
    local.start()
    local.wait()
    for copy in copies:
        copy.wait()
    o_ref[...] = slots[...]


def exchange(x, axis, cid, scatter=False):
    n = lax.axis_size(axis)
    block = x.shape[1:] if scatter else x.shape
    return pl.pallas_call(
        functools.partial(_exchange_kernel, axis, n, scatter),
        out_shape=jax.ShapeDtypeStruct((n,) + block, x.dtype),
        in_specs=[pl.BlockSpec(memory_space=pltpu.VMEM)],
        out_specs=pl.BlockSpec(memory_space=pltpu.VMEM),
        scratch_shapes=[
            pltpu.VMEM((n,) + block, x.dtype),
            pltpu.SemaphoreType.DMA((n - 1,)),
            pltpu.SemaphoreType.DMA((n - 1,)),
            pltpu.SemaphoreType.DMA,
        ],
        compiler_params=pltpu.CompilerParams(collective_id=cid, has_side_effects=True),
    )(x)


def small_sum(values, axes, first_id):
    count = values.shape[0]
    packed = jnp.pad(values, (0, 1024 - count)).reshape(8, 128)
    for i, axis in enumerate(axes):
        packed = jnp.sum(exchange(packed, axis, first_id + i), axis=0)
    return packed.reshape(-1)[:count]


def padded_2(block, sides, width):
    for axis, dim in sides:
        count = lax.axis_size(axis)
        forward = [(i, i + 1) for i in range(count - 1)]
        backward = [(target, source) for source, target in forward]
        low = lax.ppermute(
            lax.slice_in_dim(block, block.shape[dim] - width, None, axis=dim), axis, forward
        )
        high = lax.ppermute(lax.slice_in_dim(block, 0, width, axis=dim), axis, backward)
        block = jnp.concatenate([low, block, high], axis=dim)
    return block


def regional(labels, table):
    field = jnp.zeros(labels.shape, jnp.float32)
    for region in range(table.shape[0]):
        field = field + jnp.where(labels == region, table[region], 0.0)
    return field


def beside(padded):
    widths = [(0, 0)] * (padded.ndim - 1) + [(1, 1)]
    full = jnp.pad(padded, widths)
    return [
        full[..., 2:, 1:-1, 1:-1],
        full[..., :-2, 1:-1, 1:-1],
        full[..., 1:-1, 2:, 1:-1],
        full[..., 1:-1, :-2, 1:-1],
        full[..., 1:-1, 1:-1, 2:],
        full[..., 1:-1, 1:-1, :-2],
    ]


def around(field):
    widths = [(0, 0)] * (field.ndim - 3) + [(1, 1)] * 3
    full = jnp.pad(field, widths)
    return [
        full[..., 2:, 1:-1, 1:-1],
        full[..., :-2, 1:-1, 1:-1],
        full[..., 1:-1, 2:, 1:-1],
        full[..., 1:-1, :-2, 1:-1],
        full[..., 1:-1, 1:-1, 2:],
        full[..., 1:-1, 1:-1, :-2],
    ]


def chebyshev(rhs, apply_op):
    theta = 0.5 * (lam_high + lam_low)
    delta = 0.5 * (lam_high - lam_low)
    sigma = theta / delta
    rho = 1.0 / sigma
    solution = jnp.zeros_like(rhs)
    remain = rhs
    step_dir = rhs / theta
    for step in range(ITERS):
        solution = solution + step_dir
        if step + 1 < ITERS:
            remain = remain - apply_op(step_dir)
            rho_next = 1.0 / (2.0 * sigma - rho)
            step_dir = rho_next * rho * step_dir + 2.0 * rho_next / delta * remain
            rho = rho_next
    return solution


def per_device(
    labels,
    kappa_table,
    absorb_table,
    background,
    det_cells,
    v_kappa,
    v_absorb,
    q_kappa,
    q_absorb,
    beta_prev,
):
    sources, cx, cy, cz = background.shape
    kappa = regional(labels, kappa_table)
    absorb = regional(labels, absorb_table)
    n_src = lax.axis_size("src")
    slab = v_kappa.shape[2]
    pair = jnp.stack([v_kappa, v_absorb]).reshape(-1, 128)
    gathered = exchange(pair, "src", 0).reshape((n_src, 2, cx, cy, slab))
    full_k, full_a = jnp.transpose(gathered, (1, 2, 3, 0, 4)).reshape(2, cx, cy, cz)
    width = ITERS
    stacked = jnp.concatenate([background, kappa[None], absorb[None], full_k[None], full_a[None]], axis=0)
    wide = padded_2(stacked, (("gx", 1), ("gy", 2)), width)
    phi_w, kappa_w, absorb_w, vk_w, va_w = (
        wide[:sources], wide[sources], wide[sources + 1], wide[sources + 2], wide[sources + 3]
    )
    wx = cx + 2 * width
    wy = cy + 2 * width
    gx_at = lax.axis_index("gx") * cx - width + jnp.arange(wx)
    gy_at = lax.axis_index("gy") * cy - width + jnp.arange(wy)
    inside = ((gx_at >= 0) & (gx_at < cx * lax.axis_size("gx")))[:, None, None] & (
        (gy_at >= 0) & (gy_at < cy * lax.axis_size("gy"))
    )[None, :, None]
    mask = inside.astype(jnp.float32)
    kappa_faces = [mask * (0.5 * (kappa_w + near)) for near in around(kappa_w)]
    vk_faces = [mask * (0.5 * (vk_w + near)) for near in around(vk_w)]

    def apply_op(field):
        result = absorb_w * field
        for face, near in zip(kappa_faces, around(field)):
            result = result + face * (field - near)
        return result

    rhs = va_w * phi_w
    for face, near in zip(vk_faces, around(phi_w)):
        rhs = rhs + face * (phi_w - near)
    rhs = -rhs
    change = chebyshev(rhs, apply_op)[:, width : width + cx, width : width + cy, :]
    span_y = cy * lax.axis_size("gy")
    ix = det_cells // (span_y * cz)
    iy = det_cells // cz % span_y
    iz = det_cells % cz
    anchor_x = lax.axis_index("gx") * cx
    anchor_y = lax.axis_index("gy") * cy
    owned = (ix >= anchor_x) & (ix < anchor_x + cx) & (iy >= anchor_y) & (iy < anchor_y + cy)
    local = jnp.where(owned, ((ix - anchor_x) * cy + (iy - anchor_y)) * cz + iz, 0)
    seen = jnp.where(owned[None, :], change.reshape(sources, -1)[:, local], 0.0)
    base = jnp.where(owned[None, :], background.reshape(sources, -1)[:, local], 0.0)
    partial = jnp.stack(
        [
            jnp.sum(base, axis=1),
            jnp.sum(seen, axis=1),
            jnp.sum(base * seen, axis=1),
            jnp.sum(base * base, axis=1),
        ],
        axis=1,
    )
    sums = small_sum(partial.reshape(-1), ("gy", "gx"), 1).reshape(sources, 4, 1)
    total, seen_sum, cross, square = sums[:, 0], sums[:, 1], sums[:, 2], sums[:, 3]
    mean_base = total / det_cells.shape[0]
    ratio = base / total
    jv_vals = (seen - ratio * seen_sum) / mean_base
    ratio_jv = (cross / total - seen_sum * (square / (total * total))) / mean_base
    weight = (jv_vals - ratio_jv) / mean_base
    deposit = jnp.where(owned[None, :], weight, 0.0)
    source = (
        jnp.zeros((sources, cx * cy * cz), jnp.float32)
        .at[:, local]
        .add(deposit)
        .reshape(change.shape)
    )
    dual_w = chebyshev(padded_2(source, (("gx", 1), ("gy", 2)), width), apply_op)
    ring = (slice(None), slice(width - 1, width + cx + 1), slice(width - 1, width + cy + 1))
    phi_near = beside(phi_w[ring])
    dual_near = beside(dual_w[ring])
    dual = dual_w[:, width : width + cx, width : width + cy, :]
    grad_a = -jnp.sum(background * dual, axis=0)
    grad_k = jnp.zeros_like(kappa)
    for near_phi, near_dual in zip(phi_near, dual_near):
        grad_k = grad_k - 0.5 * jnp.sum((background - near_phi) * (dual - near_dual), axis=0)
    grads = jnp.stack([grad_k, grad_a]).reshape(2, cx, cy, n_src, slab)
    grads = jnp.transpose(grads, (3, 0, 1, 2, 4)).reshape(n_src, -1, 128)
    hv = jnp.sum(exchange(grads, "src", 3, scatter=True), axis=0).reshape(2, cx, cy, slab)
    hv_k, hv_a = hv[0], hv[1]
    cell_count = cx * lax.axis_size("gx") * cy * lax.axis_size("gy") * cz
    w_k = hv_k - beta_prev[0] * q_kappa
    w_a = hv_a - beta_prev[0] * q_absorb
    local_wv = jnp.sum(w_k * v_kappa) + jnp.sum(w_a * v_absorb)
    local_vv = jnp.sum(v_kappa * v_kappa) + jnp.sum(v_absorb * v_absorb)
    wv_sum, vv_sum = small_sum(jnp.stack([local_wv, local_vv]), ("gy", "gx", "src"), 4)
    alpha = wv_sum / cell_count / (vv_sum / cell_count + eps_norm)
    r_k = w_k - alpha * v_kappa
    r_a = w_a - alpha * v_absorb
    rr_sum = small_sum((jnp.sum(r_k * r_k) + jnp.sum(r_a * r_a))[None], ("gy", "gx", "src"), 7)[0]
    beta = jnp.sqrt(rr_sum / cell_count + eps_norm)
    return (r_k / beta, r_a / beta, jnp.stack([alpha, beta]))


def solution(mesh):
    return jax.shard_map(
        per_device,
        mesh=mesh,
        in_specs=(
            P("gx", "gy", None),
            P(),
            P(),
            P("src", "gx", "gy", None),
            P(),
            P("gx", "gy", "src"),
            P("gx", "gy", "src"),
            P("gx", "gy", "src"),
            P("gx", "gy", "src"),
            P(),
        ),
        out_specs=(P("gx", "gy", "src"), P("gx", "gy", "src"), P()),
        check_vma=False,
    )
```

```python
import functools

import jax
import jax.numpy as jnp
from jax import lax
from jax.experimental import pallas as pl
from jax.experimental.pallas import tpu as pltpu
from jax.sharding import PartitionSpec as P

ITERS = 6
MESH = pl.DeviceIdType.MESH


lam_low = 0.02
lam_high = 24.1
eps_norm = 1e-06


def _exchange_kernel(axis, n, scatter, x_ref, o_ref, slots, send_sem, recv_sem, local_sem):
    me = lax.axis_index(axis)
    barrier = pltpu.get_barrier_semaphore()
    for k in range(1, n):
        peer = lax.rem(me + k, n)
        pl.semaphore_signal(barrier, inc=1, device_id={axis: peer}, device_id_type=MESH)
    pl.semaphore_wait(barrier, n - 1)
    copies = []
    for k in range(1, n):
        peer = lax.rem(me + k, n)
        copy = pltpu.make_async_remote_copy(
            src_ref=x_ref.at[peer] if scatter else x_ref,
            dst_ref=slots.at[me],
            send_sem=send_sem.at[k - 1],
            recv_sem=recv_sem.at[k - 1],
            device_id={axis: peer},
            device_id_type=MESH,
        )
        copy.start()
        copies.append(copy)
    local = pltpu.make_async_copy(x_ref.at[me] if scatter else x_ref, slots.at[me], local_sem)
    local.start()
    local.wait()
    for copy in copies:
        copy.wait()
    o_ref[...] = slots[...]


def exchange(x, axis, cid, scatter=False):
    n = lax.axis_size(axis)
    block = x.shape[1:] if scatter else x.shape
    return pl.pallas_call(
        functools.partial(_exchange_kernel, axis, n, scatter),
        out_shape=jax.ShapeDtypeStruct((n,) + block, x.dtype),
        in_specs=[pl.BlockSpec(memory_space=pltpu.VMEM)],
        out_specs=pl.BlockSpec(memory_space=pltpu.VMEM),
        scratch_shapes=[
            pltpu.VMEM((n,) + block, x.dtype),
            pltpu.SemaphoreType.DMA((n - 1,)),
            pltpu.SemaphoreType.DMA((n - 1,)),
            pltpu.SemaphoreType.DMA,
        ],
        compiler_params=pltpu.CompilerParams(collective_id=cid, has_side_effects=True),
    )(x)


def small_sum(values, axes, first_id):
    count = values.shape[0]
    packed = jnp.pad(values, (0, 1024 - count)).reshape(8, 128)
    for i, axis in enumerate(axes):
        packed = jnp.sum(exchange(packed, axis, first_id + i), axis=0)
    return packed.reshape(-1)[:count]


def padded_2(block, sides, width):
    for axis, dim in sides:
        count = lax.axis_size(axis)
        forward = [(i, i + 1) for i in range(count - 1)]
        backward = [(target, source) for source, target in forward]
        low = lax.ppermute(
            lax.slice_in_dim(block, block.shape[dim] - width, None, axis=dim), axis, forward
        )
        high = lax.ppermute(lax.slice_in_dim(block, 0, width, axis=dim), axis, backward)
        block = jnp.concatenate([low, block, high], axis=dim)
    return block


def regional(labels, table):
    field = jnp.zeros(labels.shape, jnp.float32)
    for region in range(table.shape[0]):
        field = field + jnp.where(labels == region, table[region], 0.0)
    return field


def beside(padded):
    widths = [(0, 0)] * (padded.ndim - 1) + [(1, 1)]
    full = jnp.pad(padded, widths)
    return [
        full[..., 2:, 1:-1, 1:-1],
        full[..., :-2, 1:-1, 1:-1],
        full[..., 1:-1, 2:, 1:-1],
        full[..., 1:-1, :-2, 1:-1],
        full[..., 1:-1, 1:-1, 2:],
        full[..., 1:-1, 1:-1, :-2],
    ]


def around(field):
    widths = [(0, 0)] * (field.ndim - 3) + [(1, 1)] * 3
    full = jnp.pad(field, widths)
    return [
        full[..., 2:, 1:-1, 1:-1],
        full[..., :-2, 1:-1, 1:-1],
        full[..., 1:-1, 2:, 1:-1],
        full[..., 1:-1, :-2, 1:-1],
        full[..., 1:-1, 1:-1, 2:],
        full[..., 1:-1, 1:-1, :-2],
    ]


def chebyshev(rhs, apply_op):
    theta = 0.5 * (lam_high + lam_low)
    delta = 0.5 * (lam_high - lam_low)
    sigma = theta / delta
    rho = 1.0 / sigma
    solution = jnp.zeros_like(rhs)
    remain = rhs
    step_dir = rhs / theta
    for step in range(ITERS):
        solution = solution + step_dir
        if step + 1 < ITERS:
            remain = remain - apply_op(step_dir)
            rho_next = 1.0 / (2.0 * sigma - rho)
            step_dir = rho_next * rho * step_dir + 2.0 * rho_next / delta * remain
            rho = rho_next
    return solution


def per_device(
    labels,
    kappa_table,
    absorb_table,
    background,
    det_cells,
    v_kappa,
    v_absorb,
    q_kappa,
    q_absorb,
    beta_prev,
):
    sources, cx, cy, cz = background.shape
    regions = kappa_table.shape[0]
    label_hot = (labels.reshape(1, -1) == jnp.arange(regions)[:, None]).astype(jnp.float32)
    tables = jnp.stack([kappa_table, absorb_table])
    fields = jnp.dot(tables, label_hot, precision=lax.Precision.HIGHEST).reshape(2, cx, cy, cz)
    kappa, absorb = fields[0], fields[1]
    n_src = lax.axis_size("src")
    slab = v_kappa.shape[2]
    pair = jnp.stack([v_kappa, v_absorb]).reshape(-1, 128)
    gathered = exchange(pair, "src", 0).reshape((n_src, 2, cx, cy, slab))
    full_k, full_a = jnp.transpose(gathered, (1, 2, 3, 0, 4)).reshape(2, cx, cy, cz)
    width = ITERS
    stacked = jnp.concatenate([background, kappa[None], absorb[None], full_k[None], full_a[None]], axis=0)
    wide = padded_2(stacked, (("gx", 1), ("gy", 2)), width)
    phi_w, kappa_w, absorb_w, vk_w, va_w = (
        wide[:sources], wide[sources], wide[sources + 1], wide[sources + 2], wide[sources + 3]
    )
    wx = cx + 2 * width
    wy = cy + 2 * width
    gx_at = lax.axis_index("gx") * cx - width + jnp.arange(wx)
    gy_at = lax.axis_index("gy") * cy - width + jnp.arange(wy)
    inside = ((gx_at >= 0) & (gx_at < cx * lax.axis_size("gx")))[:, None, None] & (
        (gy_at >= 0) & (gy_at < cy * lax.axis_size("gy"))
    )[None, :, None]
    mask = inside.astype(jnp.float32)
    kappa_faces = [mask * (0.5 * (kappa_w + near)) for near in around(kappa_w)]
    vk_faces = [mask * (0.5 * (vk_w + near)) for near in around(vk_w)]

    def apply_op(field):
        result = absorb_w * field
        for face, near in zip(kappa_faces, around(field)):
            result = result + face * (field - near)
        return result

    rhs = va_w * phi_w
    for face, near in zip(vk_faces, around(phi_w)):
        rhs = rhs + face * (phi_w - near)
    rhs = -rhs
    change = chebyshev(rhs, apply_op)[:, width : width + cx, width : width + cy, :]
    span_y = cy * lax.axis_size("gy")
    ix = det_cells // (span_y * cz)
    iy = det_cells // cz % span_y
    iz = det_cells % cz
    anchor_x = lax.axis_index("gx") * cx
    anchor_y = lax.axis_index("gy") * cy
    owned = (ix >= anchor_x) & (ix < anchor_x + cx) & (iy >= anchor_y) & (iy < anchor_y + cy)
    plane = (ix - anchor_x) * cy + (iy - anchor_y)
    plane_hot = (jnp.arange(cx * cy)[:, None] == plane[None, :]) & owned[None, :]
    depth_hot = (jnp.arange(cz)[:, None] == iz[None, :]).astype(jnp.float32)
    both = jnp.concatenate([change, background], axis=0).reshape(-1, cz)
    picked = jnp.dot(both, depth_hot, precision=lax.Precision.HIGHEST).reshape(2 * sources, cx * cy, -1)
    picked = jnp.sum(jnp.where(plane_hot[None], picked, 0.0), axis=1)
    seen, base = picked[:sources], picked[sources:]
    partial = jnp.stack(
        [
            jnp.sum(base, axis=1),
            jnp.sum(seen, axis=1),
            jnp.sum(base * seen, axis=1),
            jnp.sum(base * base, axis=1),
        ],
        axis=1,
    )
    sums = small_sum(partial.reshape(-1), ("gy", "gx"), 1).reshape(sources, 4, 1)
    total, seen_sum, cross, square = sums[:, 0], sums[:, 1], sums[:, 2], sums[:, 3]
    mean_base = total / det_cells.shape[0]
    ratio = base / total
    jv_vals = (seen - ratio * seen_sum) / mean_base
    ratio_jv = (cross / total - seen_sum * (square / (total * total))) / mean_base
    weight = (jv_vals - ratio_jv) / mean_base
    spread = jnp.where(plane_hot[None], weight[:, None, :], 0.0).reshape(sources * cx * cy, -1)
    source = jnp.dot(spread, depth_hot.T, precision=lax.Precision.HIGHEST).reshape(change.shape)
    dual_w = chebyshev(padded_2(source, (("gx", 1), ("gy", 2)), width), apply_op)
    ring = (slice(None), slice(width - 1, width + cx + 1), slice(width - 1, width + cy + 1))
    phi_near = beside(phi_w[ring])
    dual_near = beside(dual_w[ring])
    dual = dual_w[:, width : width + cx, width : width + cy, :]
    grad_a = -jnp.sum(background * dual, axis=0)
    grad_k = jnp.zeros_like(kappa)
    for near_phi, near_dual in zip(phi_near, dual_near):
        grad_k = grad_k - 0.5 * jnp.sum((background - near_phi) * (dual - near_dual), axis=0)
    grads = jnp.stack([grad_k, grad_a]).reshape(2, cx, cy, n_src, slab)
    grads = jnp.transpose(grads, (3, 0, 1, 2, 4)).reshape(n_src, -1, 128)
    hv = jnp.sum(exchange(grads, "src", 3, scatter=True), axis=0).reshape(2, cx, cy, slab)
    hv_k, hv_a = hv[0], hv[1]
    cell_count = cx * lax.axis_size("gx") * cy * lax.axis_size("gy") * cz
    w_k = hv_k - beta_prev[0] * q_kappa
    w_a = hv_a - beta_prev[0] * q_absorb
    local_wv = jnp.sum(w_k * v_kappa) + jnp.sum(w_a * v_absorb)
    local_vv = jnp.sum(v_kappa * v_kappa) + jnp.sum(v_absorb * v_absorb)
    wv_sum, vv_sum = small_sum(jnp.stack([local_wv, local_vv]), ("gy", "gx", "src"), 4)
    alpha = wv_sum / cell_count / (vv_sum / cell_count + eps_norm)
    r_k = w_k - alpha * v_kappa
    r_a = w_a - alpha * v_absorb
    rr_sum = small_sum((jnp.sum(r_k * r_k) + jnp.sum(r_a * r_a))[None], ("gy", "gx", "src"), 7)[0]
    beta = jnp.sqrt(rr_sum / cell_count + eps_norm)
    return (r_k / beta, r_a / beta, jnp.stack([alpha, beta]))


def solution(mesh):
    return jax.shard_map(
        per_device,
        mesh=mesh,
        in_specs=(
            P("gx", "gy", None),
            P(),
            P(),
            P("src", "gx", "gy", None),
            P(),
            P("gx", "gy", "src"),
            P("gx", "gy", "src"),
            P("gx", "gy", "src"),
            P("gx", "gy", "src"),
            P(),
        ),
        out_specs=(P("gx", "gy", "src"), P("gx", "gy", "src"), P()),
        check_vma=False,
    )
```

```python
import functools

import jax
import jax.numpy as jnp
from jax import lax
from jax.experimental import pallas as pl
from jax.experimental.pallas import tpu as pltpu
from jax.sharding import PartitionSpec as P

ITERS = 6
MESH = pl.DeviceIdType.MESH


lam_low = 0.02
lam_high = 24.1
eps_norm = 1e-06


def _exchange_kernel(axis, n, scatter, x_ref, o_ref, slots, send_sem, recv_sem, local_sem):
    me = lax.axis_index(axis)
    barrier = pltpu.get_barrier_semaphore()
    for k in range(1, n):
        peer = lax.rem(me + k, n)
        pl.semaphore_signal(barrier, inc=1, device_id={axis: peer}, device_id_type=MESH)
    pl.semaphore_wait(barrier, n - 1)
    copies = []
    for k in range(1, n):
        peer = lax.rem(me + k, n)
        copy = pltpu.make_async_remote_copy(
            src_ref=x_ref.at[peer] if scatter else x_ref,
            dst_ref=slots.at[me],
            send_sem=send_sem.at[k - 1],
            recv_sem=recv_sem.at[k - 1],
            device_id={axis: peer},
            device_id_type=MESH,
        )
        copy.start()
        copies.append(copy)
    local = pltpu.make_async_copy(x_ref.at[me] if scatter else x_ref, slots.at[me], local_sem)
    local.start()
    local.wait()
    for copy in copies:
        copy.wait()
    o_ref[...] = slots[...]


def exchange(x, axis, cid, scatter=False):
    n = lax.axis_size(axis)
    block = x.shape[1:] if scatter else x.shape
    return pl.pallas_call(
        functools.partial(_exchange_kernel, axis, n, scatter),
        out_shape=jax.ShapeDtypeStruct((n,) + block, x.dtype),
        in_specs=[pl.BlockSpec(memory_space=pltpu.VMEM)],
        out_specs=pl.BlockSpec(memory_space=pltpu.VMEM),
        scratch_shapes=[
            pltpu.VMEM((n,) + block, x.dtype),
            pltpu.SemaphoreType.DMA((n - 1,)),
            pltpu.SemaphoreType.DMA((n - 1,)),
            pltpu.SemaphoreType.DMA,
        ],
        compiler_params=pltpu.CompilerParams(collective_id=cid, has_side_effects=True),
    )(x)


def _halo_kernel(hx, hy, x_ref, o_ref, wide, send_sem, recv_sem, local_sem):
    fields, cx, cy, cz = x_ref.shape
    ax, ay = lax.axis_index("gx"), lax.axis_index("gy")
    nx, ny = lax.axis_size("gx"), lax.axis_size("gy")
    wide[...] = jnp.zeros_like(wide)
    steps = [(dx, dy) for dx in (-1, 0, 1) for dy in (-1, 0, 1) if (dx, dy) != (0, 0)]

    def exists(dx, dy):
        return (ax + dx >= 0) & (ax + dx < nx) & (ay + dy >= 0) & (ay + dy < ny)

    def window(d, block, halo):
        if d < 0:
            return pl.ds(0, halo), pl.ds(block + halo, halo)
        if d > 0:
            return pl.ds(block - halo, halo), pl.ds(0, halo)
        return pl.ds(0, block), pl.ds(halo, block)

    barrier = pltpu.get_barrier_semaphore()
    for dx, dy in steps:
        @pl.when(exists(dx, dy))
        def _():
            pl.semaphore_signal(
                barrier, inc=1, device_id={"gx": ax + dx, "gy": ay + dy}, device_id_type=MESH
            )
    across = 1 + (ax + nx - 1) // nx + (2 * nx - 2 - ax) // nx
    along = 1 + (ay + ny - 1) // ny + (2 * ny - 2 - ay) // ny
    pl.semaphore_wait(barrier, across * along - 1)

    local = pltpu.make_async_copy(
        x_ref, wide.at[:, pl.ds(hx, cx), pl.ds(hy, cy), :], local_sem
    )
    local.start()
    copies = []
    for k, (dx, dy) in enumerate(steps):
        src_x, dst_x = window(dx, cx, hx)
        src_y, dst_y = window(dy, cy, hy)
        tx = jnp.clip(ax + dx, 0, nx - 1)
        ty = jnp.clip(ay + dy, 0, ny - 1)
        copy = pltpu.make_async_remote_copy(
            src_ref=x_ref.at[:, src_x, src_y, :],
            dst_ref=wide.at[:, dst_x, dst_y, :],
            send_sem=send_sem.at[k],
            recv_sem=recv_sem.at[k],
            device_id={"gx": tx, "gy": ty},
            device_id_type=MESH,
        )
        copies.append(copy)

        @pl.when(exists(dx, dy))
        def _():
            copy.start()

    local.wait()
    for copy, (dx, dy) in zip(copies, steps):
        @pl.when(exists(dx, dy))
        def _():
            copy.wait_send()

        @pl.when(exists(-dx, -dy))
        def _():
            copy.wait_recv()

    o_ref[...] = wide[...]


def halo_block(x, hx, hy, cid):
    fields, cx, cy, cz = x.shape
    shape = (fields, cx + 2 * hx, cy + 2 * hy, cz)
    return pl.pallas_call(
        functools.partial(_halo_kernel, hx, hy),
        out_shape=jax.ShapeDtypeStruct(shape, x.dtype),
        in_specs=[pl.BlockSpec(memory_space=pltpu.VMEM)],
        out_specs=pl.BlockSpec(memory_space=pltpu.VMEM),
        scratch_shapes=[
            pltpu.VMEM(shape, x.dtype),
            pltpu.SemaphoreType.DMA((8,)),
            pltpu.SemaphoreType.DMA((8,)),
            pltpu.SemaphoreType.DMA,
        ],
        compiler_params=pltpu.CompilerParams(
            collective_id=cid, has_side_effects=True, vmem_limit_bytes=48 * 1024 * 1024
        ),
    )(x)


def small_sum(values, axes, first_id):
    count = values.shape[0]
    packed = jnp.pad(values, (0, 1024 - count)).reshape(8, 128)
    for i, axis in enumerate(axes):
        packed = jnp.sum(exchange(packed, axis, first_id + i), axis=0)
    return packed.reshape(-1)[:count]


def padded_2(block, sides, width):
    for axis, dim in sides:
        count = lax.axis_size(axis)
        forward = [(i, i + 1) for i in range(count - 1)]
        backward = [(target, source) for source, target in forward]
        low = lax.ppermute(
            lax.slice_in_dim(block, block.shape[dim] - width, None, axis=dim), axis, forward
        )
        high = lax.ppermute(lax.slice_in_dim(block, 0, width, axis=dim), axis, backward)
        block = jnp.concatenate([low, block, high], axis=dim)
    return block


def regional(labels, table):
    field = jnp.zeros(labels.shape, jnp.float32)
    for region in range(table.shape[0]):
        field = field + jnp.where(labels == region, table[region], 0.0)
    return field


def beside(padded):
    widths = [(0, 0)] * (padded.ndim - 1) + [(1, 1)]
    full = jnp.pad(padded, widths)
    return [
        full[..., 2:, 1:-1, 1:-1],
        full[..., :-2, 1:-1, 1:-1],
        full[..., 1:-1, 2:, 1:-1],
        full[..., 1:-1, :-2, 1:-1],
        full[..., 1:-1, 1:-1, 2:],
        full[..., 1:-1, 1:-1, :-2],
    ]


def around(field):
    widths = [(0, 0)] * (field.ndim - 3) + [(1, 1)] * 3
    full = jnp.pad(field, widths)
    return [
        full[..., 2:, 1:-1, 1:-1],
        full[..., :-2, 1:-1, 1:-1],
        full[..., 1:-1, 2:, 1:-1],
        full[..., 1:-1, :-2, 1:-1],
        full[..., 1:-1, 1:-1, 2:],
        full[..., 1:-1, 1:-1, :-2],
    ]


def chebyshev(rhs, apply_op):
    theta = 0.5 * (lam_high + lam_low)
    delta = 0.5 * (lam_high - lam_low)
    sigma = theta / delta
    rho = 1.0 / sigma
    solution = jnp.zeros_like(rhs)
    remain = rhs
    step_dir = rhs / theta
    for step in range(ITERS):
        solution = solution + step_dir
        if step + 1 < ITERS:
            remain = remain - apply_op(step_dir)
            rho_next = 1.0 / (2.0 * sigma - rho)
            step_dir = rho_next * rho * step_dir + 2.0 * rho_next / delta * remain
            rho = rho_next
    return solution


def per_device(
    labels,
    kappa_table,
    absorb_table,
    background,
    det_cells,
    v_kappa,
    v_absorb,
    q_kappa,
    q_absorb,
    beta_prev,
):
    sources, cx, cy, cz = background.shape
    regions = kappa_table.shape[0]
    label_hot = (labels.reshape(1, -1) == jnp.arange(regions)[:, None]).astype(jnp.float32)
    tables = jnp.stack([kappa_table, absorb_table])
    fields = jnp.dot(tables, label_hot, precision=lax.Precision.HIGHEST).reshape(2, cx, cy, cz)
    kappa, absorb = fields[0], fields[1]
    n_src = lax.axis_size("src")
    slab = v_kappa.shape[2]
    pair = jnp.stack([v_kappa, v_absorb]).reshape(-1, 128)
    gathered = exchange(pair, "src", 0).reshape((n_src, 2, cx, cy, slab))
    full_k, full_a = jnp.transpose(gathered, (1, 2, 3, 0, 4)).reshape(2, cx, cy, cz)
    width = ITERS
    width_y = 8
    stacked = jnp.concatenate([background, kappa[None], absorb[None], full_k[None], full_a[None]], axis=0)
    wide = halo_block(stacked, width, width_y, 10)
    phi_w, kappa_w, absorb_w, vk_w, va_w = (
        wide[:sources], wide[sources], wide[sources + 1], wide[sources + 2], wide[sources + 3]
    )
    wx = cx + 2 * width
    wy = cy + 2 * width_y
    gx_at = lax.axis_index("gx") * cx - width + jnp.arange(wx)
    gy_at = lax.axis_index("gy") * cy - width_y + jnp.arange(wy)
    inside = ((gx_at >= 0) & (gx_at < cx * lax.axis_size("gx")))[:, None, None] & (
        (gy_at >= 0) & (gy_at < cy * lax.axis_size("gy"))
    )[None, :, None]
    mask = inside.astype(jnp.float32)
    kappa_faces = [mask * (0.5 * (kappa_w + near)) for near in around(kappa_w)]
    vk_faces = [mask * (0.5 * (vk_w + near)) for near in around(vk_w)]

    def apply_op(field):
        result = absorb_w * field
        for face, near in zip(kappa_faces, around(field)):
            result = result + face * (field - near)
        return result

    rhs = va_w * phi_w
    for face, near in zip(vk_faces, around(phi_w)):
        rhs = rhs + face * (phi_w - near)
    rhs = -rhs
    change = chebyshev(rhs, apply_op)[:, width : width + cx, width_y : width_y + cy, :]
    span_y = cy * lax.axis_size("gy")
    ix = det_cells // (span_y * cz)
    iy = det_cells // cz % span_y
    iz = det_cells % cz
    anchor_x = lax.axis_index("gx") * cx
    anchor_y = lax.axis_index("gy") * cy
    owned = (ix >= anchor_x) & (ix < anchor_x + cx) & (iy >= anchor_y) & (iy < anchor_y + cy)
    plane = (ix - anchor_x) * cy + (iy - anchor_y)
    plane_hot = (jnp.arange(cx * cy)[:, None] == plane[None, :]) & owned[None, :]
    depth_hot = (jnp.arange(cz)[:, None] == iz[None, :]).astype(jnp.float32)
    both = jnp.concatenate([change, background], axis=0).reshape(-1, cz)
    picked = jnp.dot(both, depth_hot, precision=lax.Precision.HIGHEST).reshape(2 * sources, cx * cy, -1)
    picked = jnp.sum(jnp.where(plane_hot[None], picked, 0.0), axis=1)
    seen, base = picked[:sources], picked[sources:]
    partial = jnp.stack(
        [
            jnp.sum(base, axis=1),
            jnp.sum(seen, axis=1),
            jnp.sum(base * seen, axis=1),
            jnp.sum(base * base, axis=1),
        ],
        axis=1,
    )
    sums = small_sum(partial.reshape(-1), ("gy", "gx"), 1).reshape(sources, 4, 1)
    total, seen_sum, cross, square = sums[:, 0], sums[:, 1], sums[:, 2], sums[:, 3]
    mean_base = total / det_cells.shape[0]
    ratio = base / total
    jv_vals = (seen - ratio * seen_sum) / mean_base
    ratio_jv = (cross / total - seen_sum * (square / (total * total))) / mean_base
    weight = (jv_vals - ratio_jv) / mean_base
    spread = jnp.where(plane_hot[None], weight[:, None, :], 0.0).reshape(sources * cx * cy, -1)
    source = jnp.dot(spread, depth_hot.T, precision=lax.Precision.HIGHEST).reshape(change.shape)
    dual_w = chebyshev(halo_block(source, width, width_y, 11), apply_op)
    ring = (slice(None), slice(width - 1, width + cx + 1), slice(width_y - 1, width_y + cy + 1))
    phi_near = beside(phi_w[ring])
    dual_near = beside(dual_w[ring])
    dual = dual_w[:, width : width + cx, width_y : width_y + cy, :]
    grad_a = -jnp.sum(background * dual, axis=0)
    grad_k = jnp.zeros_like(kappa)
    for near_phi, near_dual in zip(phi_near, dual_near):
        grad_k = grad_k - 0.5 * jnp.sum((background - near_phi) * (dual - near_dual), axis=0)
    grads = jnp.stack([grad_k, grad_a]).reshape(2, cx, cy, n_src, slab)
    grads = jnp.transpose(grads, (3, 0, 1, 2, 4)).reshape(n_src, -1, 128)
    hv = jnp.sum(exchange(grads, "src", 3, scatter=True), axis=0).reshape(2, cx, cy, slab)
    hv_k, hv_a = hv[0], hv[1]
    cell_count = cx * lax.axis_size("gx") * cy * lax.axis_size("gy") * cz
    w_k = hv_k - beta_prev[0] * q_kappa
    w_a = hv_a - beta_prev[0] * q_absorb
    local_wv = jnp.sum(w_k * v_kappa) + jnp.sum(w_a * v_absorb)
    local_vv = jnp.sum(v_kappa * v_kappa) + jnp.sum(v_absorb * v_absorb)
    wv_sum, vv_sum = small_sum(jnp.stack([local_wv, local_vv]), ("gy", "gx", "src"), 4)
    alpha = wv_sum / cell_count / (vv_sum / cell_count + eps_norm)
    r_k = w_k - alpha * v_kappa
    r_a = w_a - alpha * v_absorb
    rr_sum = small_sum((jnp.sum(r_k * r_k) + jnp.sum(r_a * r_a))[None], ("gy", "gx", "src"), 7)[0]
    beta = jnp.sqrt(rr_sum / cell_count + eps_norm)
    return (r_k / beta, r_a / beta, jnp.stack([alpha, beta]))


def solution(mesh):
    return jax.shard_map(
        per_device,
        mesh=mesh,
        in_specs=(
            P("gx", "gy", None),
            P(),
            P(),
            P("src", "gx", "gy", None),
            P(),
            P("gx", "gy", "src"),
            P("gx", "gy", "src"),
            P("gx", "gy", "src"),
            P("gx", "gy", "src"),
            P(),
        ),
        out_specs=(P("gx", "gy", "src"), P("gx", "gy", "src"), P()),
        check_vma=False,
    )
```

```python
import functools

import jax
import jax.numpy as jnp
from jax import lax
from jax.experimental import pallas as pl
from jax.experimental.pallas import tpu as pltpu
from jax.sharding import PartitionSpec as P

ITERS = 6
MESH = pl.DeviceIdType.MESH


lam_low = 0.02
lam_high = 24.1
eps_norm = 1e-06


def _exchange_kernel(axis, n, scatter, x_ref, o_ref, slots, send_sem, recv_sem, local_sem):
    me = lax.axis_index(axis)
    barrier = pltpu.get_barrier_semaphore()
    for k in range(1, n):
        peer = lax.rem(me + k, n)
        pl.semaphore_signal(barrier, inc=1, device_id={axis: peer}, device_id_type=MESH)
    pl.semaphore_wait(barrier, n - 1)
    copies = []
    for k in range(1, n):
        peer = lax.rem(me + k, n)
        copy = pltpu.make_async_remote_copy(
            src_ref=x_ref.at[peer] if scatter else x_ref,
            dst_ref=slots.at[me],
            send_sem=send_sem.at[k - 1],
            recv_sem=recv_sem.at[k - 1],
            device_id={axis: peer},
            device_id_type=MESH,
        )
        copy.start()
        copies.append(copy)
    local = pltpu.make_async_copy(x_ref.at[me] if scatter else x_ref, slots.at[me], local_sem)
    local.start()
    local.wait()
    for copy in copies:
        copy.wait()
    o_ref[...] = slots[...]


def exchange(x, axis, cid, scatter=False):
    n = lax.axis_size(axis)
    block = x.shape[1:] if scatter else x.shape
    return pl.pallas_call(
        functools.partial(_exchange_kernel, axis, n, scatter),
        out_shape=jax.ShapeDtypeStruct((n,) + block, x.dtype),
        in_specs=[pl.BlockSpec(memory_space=pltpu.VMEM)],
        out_specs=pl.BlockSpec(memory_space=pltpu.VMEM),
        scratch_shapes=[
            pltpu.VMEM((n,) + block, x.dtype),
            pltpu.SemaphoreType.DMA((n - 1,)),
            pltpu.SemaphoreType.DMA((n - 1,)),
            pltpu.SemaphoreType.DMA,
        ],
        compiler_params=pltpu.CompilerParams(collective_id=cid, has_side_effects=True),
    )(x)


def _halo_kernel(hx, hy, x_ref, o_ref, wide, send_sem, recv_sem, local_sem):
    fields, cx, cy, cz = x_ref.shape
    ax, ay = lax.axis_index("gx"), lax.axis_index("gy")
    nx, ny = lax.axis_size("gx"), lax.axis_size("gy")
    wide[...] = jnp.zeros_like(wide)
    steps = [(dx, dy) for dx in (-1, 0, 1) for dy in (-1, 0, 1) if (dx, dy) != (0, 0)]

    def exists(dx, dy):
        return (ax + dx >= 0) & (ax + dx < nx) & (ay + dy >= 0) & (ay + dy < ny)

    def window(d, block, halo):
        if d < 0:
            return pl.ds(0, halo), pl.ds(block + halo, halo)
        if d > 0:
            return pl.ds(block - halo, halo), pl.ds(0, halo)
        return pl.ds(0, block), pl.ds(halo, block)

    barrier = pltpu.get_barrier_semaphore()
    for dx, dy in steps:
        @pl.when(exists(dx, dy))
        def _():
            pl.semaphore_signal(
                barrier, inc=1, device_id={"gx": ax + dx, "gy": ay + dy}, device_id_type=MESH
            )
    across = 1 + (ax + nx - 1) // nx + (2 * nx - 2 - ax) // nx
    along = 1 + (ay + ny - 1) // ny + (2 * ny - 2 - ay) // ny
    pl.semaphore_wait(barrier, across * along - 1)

    local = pltpu.make_async_copy(
        x_ref, wide.at[:, pl.ds(hx, cx), pl.ds(hy, cy), :], local_sem
    )
    local.start()
    copies = []
    for k, (dx, dy) in enumerate(steps):
        src_x, dst_x = window(dx, cx, hx)
        src_y, dst_y = window(dy, cy, hy)
        tx = jnp.clip(ax + dx, 0, nx - 1)
        ty = jnp.clip(ay + dy, 0, ny - 1)
        copy = pltpu.make_async_remote_copy(
            src_ref=x_ref.at[:, src_x, src_y, :],
            dst_ref=wide.at[:, dst_x, dst_y, :],
            send_sem=send_sem.at[k],
            recv_sem=recv_sem.at[k],
            device_id={"gx": tx, "gy": ty},
            device_id_type=MESH,
        )
        copies.append(copy)

        @pl.when(exists(dx, dy))
        def _():
            copy.start()

    local.wait()
    for copy, (dx, dy) in zip(copies, steps):
        @pl.when(exists(dx, dy))
        def _():
            copy.wait_send()

        @pl.when(exists(-dx, -dy))
        def _():
            copy.wait_recv()

    o_ref[...] = wide[...]


def halo_block(x, hx, hy, cid):
    fields, cx, cy, cz = x.shape
    shape = (fields, cx + 2 * hx, cy + 2 * hy, cz)
    return pl.pallas_call(
        functools.partial(_halo_kernel, hx, hy),
        out_shape=jax.ShapeDtypeStruct(shape, x.dtype),
        in_specs=[pl.BlockSpec(memory_space=pltpu.VMEM)],
        out_specs=pl.BlockSpec(memory_space=pltpu.VMEM),
        scratch_shapes=[
            pltpu.VMEM(shape, x.dtype),
            pltpu.SemaphoreType.DMA((8,)),
            pltpu.SemaphoreType.DMA((8,)),
            pltpu.SemaphoreType.DMA,
        ],
        compiler_params=pltpu.CompilerParams(
            collective_id=cid, has_side_effects=True, vmem_limit_bytes=48 * 1024 * 1024
        ),
    )(x)


def _reduce_kernel(axes, x_ref, o_ref, *scratch):
    stages = len(axes)
    slots, sends, recvs = scratch[:stages], scratch[stages : 2 * stages], scratch[2 * stages : 3 * stages]
    held = scratch[3 * stages :]
    barrier = pltpu.get_barrier_semaphore()
    peers = 0
    for axis in axes:
        n = lax.axis_size(axis)
        me = lax.axis_index(axis)
        for k in range(1, n):
            pl.semaphore_signal(
                barrier, inc=1, device_id={axis: lax.rem(me + k, n)}, device_id_type=MESH
            )
        peers += n - 1
    pl.semaphore_wait(barrier, peers)
    value = x_ref
    for i, axis in enumerate(axes):
        n = lax.axis_size(axis)
        me = lax.axis_index(axis)
        copies = []
        for k in range(1, n):
            copy = pltpu.make_async_remote_copy(
                src_ref=value,
                dst_ref=slots[i].at[me],
                send_sem=sends[i].at[k - 1],
                recv_sem=recvs[i].at[k - 1],
                device_id={axis: lax.rem(me + k, n)},
                device_id_type=MESH,
            )
            copy.start()
            copies.append(copy)
        slots[i][me] = value[...]
        for copy in copies:
            copy.wait()
        total = slots[i][0]
        for j in range(1, n):
            total = total + slots[i][j]
        if i + 1 < stages:
            held[i][...] = total
            value = held[i]
        else:
            o_ref[...] = total


def small_sum(values, axes, cid):
    count = values.shape[0]
    packed = jnp.pad(values, (0, 1024 - count)).reshape(8, 128)
    sizes = [lax.axis_size(axis) for axis in axes]
    scratch = (
        [pltpu.VMEM((n, 8, 128), jnp.float32) for n in sizes]
        + [pltpu.SemaphoreType.DMA((n - 1,)) for n in sizes]
        + [pltpu.SemaphoreType.DMA((n - 1,)) for n in sizes]
        + [pltpu.VMEM((8, 128), jnp.float32) for n in sizes[:-1]]
    )
    total = pl.pallas_call(
        functools.partial(_reduce_kernel, tuple(axes)),
        out_shape=jax.ShapeDtypeStruct((8, 128), jnp.float32),
        in_specs=[pl.BlockSpec(memory_space=pltpu.VMEM)],
        out_specs=pl.BlockSpec(memory_space=pltpu.VMEM),
        scratch_shapes=scratch,
        compiler_params=pltpu.CompilerParams(collective_id=cid, has_side_effects=True),
    )(packed)
    return total.reshape(-1)[:count]


def padded_2(block, sides, width):
    for axis, dim in sides:
        count = lax.axis_size(axis)
        forward = [(i, i + 1) for i in range(count - 1)]
        backward = [(target, source) for source, target in forward]
        low = lax.ppermute(
            lax.slice_in_dim(block, block.shape[dim] - width, None, axis=dim), axis, forward
        )
        high = lax.ppermute(lax.slice_in_dim(block, 0, width, axis=dim), axis, backward)
        block = jnp.concatenate([low, block, high], axis=dim)
    return block


def regional(labels, table):
    field = jnp.zeros(labels.shape, jnp.float32)
    for region in range(table.shape[0]):
        field = field + jnp.where(labels == region, table[region], 0.0)
    return field


def beside(padded):
    widths = [(0, 0)] * (padded.ndim - 1) + [(1, 1)]
    full = jnp.pad(padded, widths)
    return [
        full[..., 2:, 1:-1, 1:-1],
        full[..., :-2, 1:-1, 1:-1],
        full[..., 1:-1, 2:, 1:-1],
        full[..., 1:-1, :-2, 1:-1],
        full[..., 1:-1, 1:-1, 2:],
        full[..., 1:-1, 1:-1, :-2],
    ]


def around(field):
    widths = [(0, 0)] * (field.ndim - 3) + [(1, 1)] * 3
    full = jnp.pad(field, widths)
    return [
        full[..., 2:, 1:-1, 1:-1],
        full[..., :-2, 1:-1, 1:-1],
        full[..., 1:-1, 2:, 1:-1],
        full[..., 1:-1, :-2, 1:-1],
        full[..., 1:-1, 1:-1, 2:],
        full[..., 1:-1, 1:-1, :-2],
    ]


def chebyshev(rhs, apply_op):
    theta = 0.5 * (lam_high + lam_low)
    delta = 0.5 * (lam_high - lam_low)
    sigma = theta / delta
    rho = 1.0 / sigma
    solution = jnp.zeros_like(rhs)
    remain = rhs
    step_dir = rhs / theta
    for step in range(ITERS):
        solution = solution + step_dir
        if step + 1 < ITERS:
            remain = remain - apply_op(step_dir)
            rho_next = 1.0 / (2.0 * sigma - rho)
            step_dir = rho_next * rho * step_dir + 2.0 * rho_next / delta * remain
            rho = rho_next
    return solution


def per_device(
    labels,
    kappa_table,
    absorb_table,
    background,
    det_cells,
    v_kappa,
    v_absorb,
    q_kappa,
    q_absorb,
    beta_prev,
):
    sources, cx, cy, cz = background.shape
    regions = kappa_table.shape[0]
    label_hot = (labels.reshape(1, -1) == jnp.arange(regions)[:, None]).astype(jnp.float32)
    tables = jnp.stack([kappa_table, absorb_table])
    fields = jnp.dot(tables, label_hot, precision=lax.Precision.HIGHEST).reshape(2, cx, cy, cz)
    kappa, absorb = fields[0], fields[1]
    n_src = lax.axis_size("src")
    slab = v_kappa.shape[2]
    pair = jnp.stack([v_kappa, v_absorb]).reshape(-1, 128)
    gathered = exchange(pair, "src", 0).reshape((n_src, 2, cx, cy, slab))
    full_k, full_a = jnp.transpose(gathered, (1, 2, 3, 0, 4)).reshape(2, cx, cy, cz)
    width = ITERS
    width_y = 8
    stacked = jnp.concatenate([background, kappa[None], absorb[None], full_k[None], full_a[None]], axis=0)
    wide = halo_block(stacked, width, width_y, 10)
    phi_w, kappa_w, absorb_w, vk_w, va_w = (
        wide[:sources], wide[sources], wide[sources + 1], wide[sources + 2], wide[sources + 3]
    )
    wx = cx + 2 * width
    wy = cy + 2 * width_y
    gx_at = lax.axis_index("gx") * cx - width + jnp.arange(wx)
    gy_at = lax.axis_index("gy") * cy - width_y + jnp.arange(wy)
    inside = ((gx_at >= 0) & (gx_at < cx * lax.axis_size("gx")))[:, None, None] & (
        (gy_at >= 0) & (gy_at < cy * lax.axis_size("gy"))
    )[None, :, None]
    mask = inside.astype(jnp.float32)
    kappa_faces = [mask * (0.5 * (kappa_w + near)) for near in around(kappa_w)]
    vk_faces = [mask * (0.5 * (vk_w + near)) for near in around(vk_w)]

    def apply_op(field):
        result = absorb_w * field
        for face, near in zip(kappa_faces, around(field)):
            result = result + face * (field - near)
        return result

    rhs = va_w * phi_w
    for face, near in zip(vk_faces, around(phi_w)):
        rhs = rhs + face * (phi_w - near)
    rhs = -rhs
    change = chebyshev(rhs, apply_op)[:, width : width + cx, width_y : width_y + cy, :]
    span_y = cy * lax.axis_size("gy")
    ix = det_cells // (span_y * cz)
    iy = det_cells // cz % span_y
    iz = det_cells % cz
    anchor_x = lax.axis_index("gx") * cx
    anchor_y = lax.axis_index("gy") * cy
    owned = (ix >= anchor_x) & (ix < anchor_x + cx) & (iy >= anchor_y) & (iy < anchor_y + cy)
    plane = (ix - anchor_x) * cy + (iy - anchor_y)
    plane_hot = (jnp.arange(cx * cy)[:, None] == plane[None, :]) & owned[None, :]
    depth_hot = (jnp.arange(cz)[:, None] == iz[None, :]).astype(jnp.float32)
    both = jnp.concatenate([change, background], axis=0).reshape(-1, cz)
    picked = jnp.dot(both, depth_hot, precision=lax.Precision.HIGHEST).reshape(2 * sources, cx * cy, -1)
    picked = jnp.sum(jnp.where(plane_hot[None], picked, 0.0), axis=1)
    seen, base = picked[:sources], picked[sources:]
    partial = jnp.stack(
        [
            jnp.sum(base, axis=1),
            jnp.sum(seen, axis=1),
            jnp.sum(base * seen, axis=1),
            jnp.sum(base * base, axis=1),
        ],
        axis=1,
    )
    sums = small_sum(partial.reshape(-1), ("gy", "gx"), 1).reshape(sources, 4, 1)
    total, seen_sum, cross, square = sums[:, 0], sums[:, 1], sums[:, 2], sums[:, 3]
    mean_base = total / det_cells.shape[0]
    ratio = base / total
    jv_vals = (seen - ratio * seen_sum) / mean_base
    ratio_jv = (cross / total - seen_sum * (square / (total * total))) / mean_base
    weight = (jv_vals - ratio_jv) / mean_base
    spread = jnp.where(plane_hot[None], weight[:, None, :], 0.0).reshape(sources * cx * cy, -1)
    source = jnp.dot(spread, depth_hot.T, precision=lax.Precision.HIGHEST).reshape(change.shape)
    dual_w = chebyshev(halo_block(source, width, width_y, 11), apply_op)
    ring = (slice(None), slice(width - 1, width + cx + 1), slice(width_y - 1, width_y + cy + 1))
    phi_near = beside(phi_w[ring])
    dual_near = beside(dual_w[ring])
    dual = dual_w[:, width : width + cx, width_y : width_y + cy, :]
    grad_a = -jnp.sum(background * dual, axis=0)
    grad_k = jnp.zeros_like(kappa)
    for near_phi, near_dual in zip(phi_near, dual_near):
        grad_k = grad_k - 0.5 * jnp.sum((background - near_phi) * (dual - near_dual), axis=0)
    grads = jnp.stack([grad_k, grad_a]).reshape(2, cx, cy, n_src, slab)
    grads = jnp.transpose(grads, (3, 0, 1, 2, 4)).reshape(n_src, -1, 128)
    hv = jnp.sum(exchange(grads, "src", 3, scatter=True), axis=0).reshape(2, cx, cy, slab)
    hv_k, hv_a = hv[0], hv[1]
    cell_count = cx * lax.axis_size("gx") * cy * lax.axis_size("gy") * cz
    w_k = hv_k - beta_prev[0] * q_kappa
    w_a = hv_a - beta_prev[0] * q_absorb
    local_wv = jnp.sum(w_k * v_kappa) + jnp.sum(w_a * v_absorb)
    local_vv = jnp.sum(v_kappa * v_kappa) + jnp.sum(v_absorb * v_absorb)
    wv_sum, vv_sum = small_sum(jnp.stack([local_wv, local_vv]), ("gy", "gx", "src"), 4)
    alpha = wv_sum / cell_count / (vv_sum / cell_count + eps_norm)
    r_k = w_k - alpha * v_kappa
    r_a = w_a - alpha * v_absorb
    rr_sum = small_sum((jnp.sum(r_k * r_k) + jnp.sum(r_a * r_a))[None], ("gy", "gx", "src"), 7)[0]
    beta = jnp.sqrt(rr_sum / cell_count + eps_norm)
    return (r_k / beta, r_a / beta, jnp.stack([alpha, beta]))


def solution(mesh):
    return jax.shard_map(
        per_device,
        mesh=mesh,
        in_specs=(
            P("gx", "gy", None),
            P(),
            P(),
            P("src", "gx", "gy", None),
            P(),
            P("gx", "gy", "src"),
            P("gx", "gy", "src"),
            P("gx", "gy", "src"),
            P("gx", "gy", "src"),
            P(),
        ),
        out_specs=(P("gx", "gy", "src"), P("gx", "gy", "src"), P()),
        check_vma=False,
    )
```

```python
import functools

import jax
import jax.numpy as jnp
from jax import lax
from jax.experimental import pallas as pl
from jax.experimental.pallas import tpu as pltpu
from jax.sharding import PartitionSpec as P

ITERS = 6
MESH = pl.DeviceIdType.MESH


lam_low = 0.02
lam_high = 24.1
eps_norm = 1e-06


def _exchange_kernel(axis, n, scatter, x_ref, o_ref, slots, send_sem, recv_sem, local_sem):
    me = lax.axis_index(axis)
    barrier = pltpu.get_barrier_semaphore()
    for k in range(1, n):
        peer = lax.rem(me + k, n)
        pl.semaphore_signal(barrier, inc=1, device_id={axis: peer}, device_id_type=MESH)
    pl.semaphore_wait(barrier, n - 1)
    copies = []
    for k in range(1, n):
        peer = lax.rem(me + k, n)
        copy = pltpu.make_async_remote_copy(
            src_ref=x_ref.at[peer] if scatter else x_ref,
            dst_ref=slots.at[me],
            send_sem=send_sem.at[k - 1],
            recv_sem=recv_sem.at[k - 1],
            device_id={axis: peer},
            device_id_type=MESH,
        )
        copy.start()
        copies.append(copy)
    local = pltpu.make_async_copy(x_ref.at[me] if scatter else x_ref, slots.at[me], local_sem)
    local.start()
    local.wait()
    for copy in copies:
        copy.wait()
    o_ref[...] = slots[...]


def exchange(x, axis, cid, scatter=False):
    n = lax.axis_size(axis)
    block = x.shape[1:] if scatter else x.shape
    return pl.pallas_call(
        functools.partial(_exchange_kernel, axis, n, scatter),
        out_shape=jax.ShapeDtypeStruct((n,) + block, x.dtype),
        in_specs=[pl.BlockSpec(memory_space=pltpu.VMEM)],
        out_specs=pl.BlockSpec(memory_space=pltpu.VMEM),
        scratch_shapes=[
            pltpu.VMEM((n,) + block, x.dtype),
            pltpu.SemaphoreType.DMA((n - 1,)),
            pltpu.SemaphoreType.DMA((n - 1,)),
            pltpu.SemaphoreType.DMA,
        ],
        compiler_params=pltpu.CompilerParams(collective_id=cid, has_side_effects=True),
    )(x)


def _halo_kernel(hx, hy, x_ref, o_ref, wide, send_sem, recv_sem, local_sem):
    fields, cx, cy, cz = x_ref.shape
    ax, ay = lax.axis_index("gx"), lax.axis_index("gy")
    nx, ny = lax.axis_size("gx"), lax.axis_size("gy")
    wide[...] = jnp.zeros_like(wide)
    steps = [(dx, dy) for dx in (-1, 0, 1) for dy in (-1, 0, 1) if (dx, dy) != (0, 0)]

    def exists(dx, dy):
        return (ax + dx >= 0) & (ax + dx < nx) & (ay + dy >= 0) & (ay + dy < ny)

    def window(d, block, halo):
        if d < 0:
            return pl.ds(0, halo), pl.ds(block + halo, halo)
        if d > 0:
            return pl.ds(block - halo, halo), pl.ds(0, halo)
        return pl.ds(0, block), pl.ds(halo, block)

    barrier = pltpu.get_barrier_semaphore()
    for dx, dy in steps:
        @pl.when(exists(dx, dy))
        def _():
            pl.semaphore_signal(
                barrier, inc=1, device_id={"gx": ax + dx, "gy": ay + dy}, device_id_type=MESH
            )
    across = 1 + (ax + nx - 1) // nx + (2 * nx - 2 - ax) // nx
    along = 1 + (ay + ny - 1) // ny + (2 * ny - 2 - ay) // ny
    pl.semaphore_wait(barrier, across * along - 1)

    local = pltpu.make_async_copy(
        x_ref, wide.at[:, pl.ds(hx, cx), pl.ds(hy, cy), :], local_sem
    )
    local.start()
    copies = []
    for k, (dx, dy) in enumerate(steps):
        src_x, dst_x = window(dx, cx, hx)
        src_y, dst_y = window(dy, cy, hy)
        tx = jnp.clip(ax + dx, 0, nx - 1)
        ty = jnp.clip(ay + dy, 0, ny - 1)
        copy = pltpu.make_async_remote_copy(
            src_ref=x_ref.at[:, src_x, src_y, :],
            dst_ref=wide.at[:, dst_x, dst_y, :],
            send_sem=send_sem.at[k],
            recv_sem=recv_sem.at[k],
            device_id={"gx": tx, "gy": ty},
            device_id_type=MESH,
        )
        copies.append(copy)

        @pl.when(exists(dx, dy))
        def _():
            copy.start()

    local.wait()
    for copy, (dx, dy) in zip(copies, steps):
        @pl.when(exists(dx, dy))
        def _():
            copy.wait_send()

        @pl.when(exists(-dx, -dy))
        def _():
            copy.wait_recv()

    o_ref[...] = wide[...]


def halo_block(x, hx, hy, cid):
    fields, cx, cy, cz = x.shape
    shape = (fields, cx + 2 * hx, cy + 2 * hy, cz)
    return pl.pallas_call(
        functools.partial(_halo_kernel, hx, hy),
        out_shape=jax.ShapeDtypeStruct(shape, x.dtype),
        in_specs=[pl.BlockSpec(memory_space=pltpu.VMEM)],
        out_specs=pl.BlockSpec(memory_space=pltpu.VMEM),
        scratch_shapes=[
            pltpu.VMEM(shape, x.dtype),
            pltpu.SemaphoreType.DMA((8,)),
            pltpu.SemaphoreType.DMA((8,)),
            pltpu.SemaphoreType.DMA,
        ],
        compiler_params=pltpu.CompilerParams(
            collective_id=cid, has_side_effects=True, vmem_limit_bytes=48 * 1024 * 1024
        ),
    )(x)


def _reduce_kernel(axes, x_ref, o_ref, *scratch):
    stages = len(axes)
    slots, sends, recvs = scratch[:stages], scratch[stages : 2 * stages], scratch[2 * stages : 3 * stages]
    held = scratch[3 * stages :]
    barrier = pltpu.get_barrier_semaphore()
    peers = 0
    for axis in axes:
        n = lax.axis_size(axis)
        me = lax.axis_index(axis)
        for k in range(1, n):
            pl.semaphore_signal(
                barrier, inc=1, device_id={axis: lax.rem(me + k, n)}, device_id_type=MESH
            )
        peers += n - 1
    pl.semaphore_wait(barrier, peers)
    value = x_ref
    for i, axis in enumerate(axes):
        n = lax.axis_size(axis)
        me = lax.axis_index(axis)
        copies = []
        for k in range(1, n):
            copy = pltpu.make_async_remote_copy(
                src_ref=value,
                dst_ref=slots[i].at[me],
                send_sem=sends[i].at[k - 1],
                recv_sem=recvs[i].at[k - 1],
                device_id={axis: lax.rem(me + k, n)},
                device_id_type=MESH,
            )
            copy.start()
            copies.append(copy)
        slots[i][me] = value[...]
        for copy in copies:
            copy.wait()
        total = slots[i][0]
        for j in range(1, n):
            total = total + slots[i][j]
        if i + 1 < stages:
            held[i][...] = total
            value = held[i]
        else:
            o_ref[...] = total


def small_sum(values, axes, cid):
    count = values.shape[0]
    packed = jnp.pad(values, (0, 1024 - count)).reshape(8, 128)
    sizes = [lax.axis_size(axis) for axis in axes]
    scratch = (
        [pltpu.VMEM((n, 8, 128), jnp.float32) for n in sizes]
        + [pltpu.SemaphoreType.DMA((n - 1,)) for n in sizes]
        + [pltpu.SemaphoreType.DMA((n - 1,)) for n in sizes]
        + [pltpu.VMEM((8, 128), jnp.float32) for n in sizes[:-1]]
    )
    total = pl.pallas_call(
        functools.partial(_reduce_kernel, tuple(axes)),
        out_shape=jax.ShapeDtypeStruct((8, 128), jnp.float32),
        in_specs=[pl.BlockSpec(memory_space=pltpu.VMEM)],
        out_specs=pl.BlockSpec(memory_space=pltpu.VMEM),
        scratch_shapes=scratch,
        compiler_params=pltpu.CompilerParams(collective_id=cid, has_side_effects=True),
    )(packed)
    return total.reshape(-1)[:count]


def padded_2(block, sides, width):
    for axis, dim in sides:
        count = lax.axis_size(axis)
        forward = [(i, i + 1) for i in range(count - 1)]
        backward = [(target, source) for source, target in forward]
        low = lax.ppermute(
            lax.slice_in_dim(block, block.shape[dim] - width, None, axis=dim), axis, forward
        )
        high = lax.ppermute(lax.slice_in_dim(block, 0, width, axis=dim), axis, backward)
        block = jnp.concatenate([low, block, high], axis=dim)
    return block


def regional(labels, table):
    field = jnp.zeros(labels.shape, jnp.float32)
    for region in range(table.shape[0]):
        field = field + jnp.where(labels == region, table[region], 0.0)
    return field


def beside(padded):
    widths = [(0, 0)] * (padded.ndim - 1) + [(1, 1)]
    full = jnp.pad(padded, widths)
    return [
        full[..., 2:, 1:-1, 1:-1],
        full[..., :-2, 1:-1, 1:-1],
        full[..., 1:-1, 2:, 1:-1],
        full[..., 1:-1, :-2, 1:-1],
        full[..., 1:-1, 1:-1, 2:],
        full[..., 1:-1, 1:-1, :-2],
    ]


def around(field):
    widths = [(0, 0)] * (field.ndim - 3) + [(1, 1)] * 3
    full = jnp.pad(field, widths)
    return [
        full[..., 2:, 1:-1, 1:-1],
        full[..., :-2, 1:-1, 1:-1],
        full[..., 1:-1, 2:, 1:-1],
        full[..., 1:-1, :-2, 1:-1],
        full[..., 1:-1, 1:-1, 2:],
        full[..., 1:-1, 1:-1, :-2],
    ]


def chebyshev(rhs, apply_op):
    theta = 0.5 * (lam_high + lam_low)
    delta = 0.5 * (lam_high - lam_low)
    sigma = theta / delta
    rho = 1.0 / sigma
    solution = jnp.zeros_like(rhs)
    remain = rhs
    step_dir = rhs / theta
    for step in range(ITERS):
        solution = solution + step_dir
        if step + 1 < ITERS:
            remain = remain - apply_op(step_dir)
            rho_next = 1.0 / (2.0 * sigma - rho)
            step_dir = rho_next * rho * step_dir + 2.0 * rho_next / delta * remain
            rho = rho_next
    return solution


def per_device(
    labels,
    kappa_table,
    absorb_table,
    background,
    det_cells,
    v_kappa,
    v_absorb,
    q_kappa,
    q_absorb,
    beta_prev,
):
    sources, cx, cy, cz = background.shape
    n_src = lax.axis_size("src")
    slab = v_kappa.shape[2]
    pair = jnp.stack([v_kappa, v_absorb]).reshape(-1, 128)
    gathered = exchange(pair, "src", 0).reshape((n_src, 2, cx, cy, slab))
    full_k, full_a = jnp.transpose(gathered, (1, 2, 3, 0, 4)).reshape(2, cx, cy, cz)
    width = ITERS
    width_y = 8
    region_of = labels.astype(jnp.float32)[None]
    stacked = jnp.concatenate([background, region_of, full_k[None], full_a[None]], axis=0)
    wide = halo_block(stacked, width, width_y, 10)
    phi_w, region_w, vk_w, va_w = wide[:sources], wide[sources], wide[sources + 1], wide[sources + 2]
    wx = cx + 2 * width
    wy = cy + 2 * width_y
    gx_at = lax.axis_index("gx") * cx - width + jnp.arange(wx)
    gy_at = lax.axis_index("gy") * cy - width_y + jnp.arange(wy)
    inside = ((gx_at >= 0) & (gx_at < cx * lax.axis_size("gx")))[:, None, None] & (
        (gy_at >= 0) & (gy_at < cy * lax.axis_size("gy"))
    )[None, :, None]
    mask = inside.astype(jnp.float32)
    regions = kappa_table.shape[0]
    label_hot = (region_w.reshape(1, -1) == jnp.arange(regions, dtype=jnp.float32)[:, None]).astype(jnp.float32)
    tables = jnp.stack([kappa_table, absorb_table])
    fields = jnp.dot(tables, label_hot, precision=lax.Precision.HIGHEST).reshape(2, wx, wy, cz)
    kappa_w, absorb_w = mask * fields[0], mask * fields[1]
    kappa_faces = [mask * (0.5 * (kappa_w + near)) for near in around(kappa_w)]
    vk_faces = [mask * (0.5 * (vk_w + near)) for near in around(vk_w)]

    def apply_op(field):
        result = absorb_w * field
        for face, near in zip(kappa_faces, around(field)):
            result = result + face * (field - near)
        return result

    rhs = va_w * phi_w
    for face, near in zip(vk_faces, around(phi_w)):
        rhs = rhs + face * (phi_w - near)
    rhs = -rhs
    change = chebyshev(rhs, apply_op)[:, width : width + cx, width_y : width_y + cy, :]
    span_y = cy * lax.axis_size("gy")
    ix = det_cells // (span_y * cz)
    iy = det_cells // cz % span_y
    iz = det_cells % cz
    anchor_x = lax.axis_index("gx") * cx
    anchor_y = lax.axis_index("gy") * cy
    owned = (ix >= anchor_x) & (ix < anchor_x + cx) & (iy >= anchor_y) & (iy < anchor_y + cy)
    plane = (ix - anchor_x) * cy + (iy - anchor_y)
    plane_hot = (jnp.arange(cx * cy)[:, None] == plane[None, :]) & owned[None, :]
    depth_hot = (jnp.arange(cz)[:, None] == iz[None, :]).astype(jnp.float32)
    both = jnp.concatenate([change, background], axis=0).reshape(-1, cz)
    picked = jnp.dot(both, depth_hot, precision=lax.Precision.HIGHEST).reshape(2 * sources, cx * cy, -1)
    picked = jnp.sum(jnp.where(plane_hot[None], picked, 0.0), axis=1)
    seen, base = picked[:sources], picked[sources:]
    partial = jnp.stack(
        [
            jnp.sum(base, axis=1),
            jnp.sum(seen, axis=1),
            jnp.sum(base * seen, axis=1),
            jnp.sum(base * base, axis=1),
        ],
        axis=1,
    )
    sums = small_sum(partial.reshape(-1), ("gy", "gx"), 1).reshape(sources, 4, 1)
    total, seen_sum, cross, square = sums[:, 0], sums[:, 1], sums[:, 2], sums[:, 3]
    mean_base = total / det_cells.shape[0]
    ratio = base / total
    jv_vals = (seen - ratio * seen_sum) / mean_base
    ratio_jv = (cross / total - seen_sum * (square / (total * total))) / mean_base
    weight = (jv_vals - ratio_jv) / mean_base
    spread = jnp.where(plane_hot[None], weight[:, None, :], 0.0).reshape(sources * cx * cy, -1)
    source = jnp.dot(spread, depth_hot.T, precision=lax.Precision.HIGHEST).reshape(change.shape)
    dual_w = chebyshev(halo_block(source, width, width_y, 11), apply_op)
    ring = (slice(None), slice(width - 1, width + cx + 1), slice(width_y - 1, width_y + cy + 1))
    phi_near = beside(phi_w[ring])
    dual_near = beside(dual_w[ring])
    dual = dual_w[:, width : width + cx, width_y : width_y + cy, :]
    grad_a = -jnp.sum(background * dual, axis=0)
    grad_k = jnp.zeros_like(background[0])
    for near_phi, near_dual in zip(phi_near, dual_near):
        grad_k = grad_k - 0.5 * jnp.sum((background - near_phi) * (dual - near_dual), axis=0)
    grads = jnp.stack([grad_k, grad_a]).reshape(2, cx, cy, n_src, slab)
    grads = jnp.transpose(grads, (3, 0, 1, 2, 4)).reshape(n_src, -1, 128)
    hv = jnp.sum(exchange(grads, "src", 3, scatter=True), axis=0).reshape(2, cx, cy, slab)
    hv_k, hv_a = hv[0], hv[1]
    cell_count = cx * lax.axis_size("gx") * cy * lax.axis_size("gy") * cz
    w_k = hv_k - beta_prev[0] * q_kappa
    w_a = hv_a - beta_prev[0] * q_absorb
    local_wv = jnp.sum(w_k * v_kappa) + jnp.sum(w_a * v_absorb)
    local_vv = jnp.sum(v_kappa * v_kappa) + jnp.sum(v_absorb * v_absorb)
    wv_sum, vv_sum = small_sum(jnp.stack([local_wv, local_vv]), ("gy", "gx", "src"), 4)
    alpha = wv_sum / cell_count / (vv_sum / cell_count + eps_norm)
    r_k = w_k - alpha * v_kappa
    r_a = w_a - alpha * v_absorb
    rr_sum = small_sum((jnp.sum(r_k * r_k) + jnp.sum(r_a * r_a))[None], ("gy", "gx", "src"), 7)[0]
    beta = jnp.sqrt(rr_sum / cell_count + eps_norm)
    return (r_k / beta, r_a / beta, jnp.stack([alpha, beta]))


def solution(mesh):
    return jax.shard_map(
        per_device,
        mesh=mesh,
        in_specs=(
            P("gx", "gy", None),
            P(),
            P(),
            P("src", "gx", "gy", None),
            P(),
            P("gx", "gy", "src"),
            P("gx", "gy", "src"),
            P("gx", "gy", "src"),
            P("gx", "gy", "src"),
            P(),
        ),
        out_specs=(P("gx", "gy", "src"), P("gx", "gy", "src"), P()),
        check_vma=False,
    )
```

```python
import functools

import jax
import jax.numpy as jnp
from jax import lax
from jax.experimental import pallas as pl
from jax.experimental.pallas import tpu as pltpu
from jax.sharding import PartitionSpec as P

ITERS = 6
MESH = pl.DeviceIdType.MESH


lam_low = 0.02
lam_high = 24.1
eps_norm = 1e-06


def _exchange_kernel(axis, n, scatter, x_ref, o_ref, slots, send_sem, recv_sem, local_sem):
    me = lax.axis_index(axis)
    barrier = pltpu.get_barrier_semaphore()
    for k in range(1, n):
        peer = lax.rem(me + k, n)
        pl.semaphore_signal(barrier, inc=1, device_id={axis: peer}, device_id_type=MESH)
    pl.semaphore_wait(barrier, n - 1)
    copies = []
    for k in range(1, n):
        peer = lax.rem(me + k, n)
        copy = pltpu.make_async_remote_copy(
            src_ref=x_ref.at[peer] if scatter else x_ref,
            dst_ref=slots.at[me],
            send_sem=send_sem.at[k - 1],
            recv_sem=recv_sem.at[k - 1],
            device_id={axis: peer},
            device_id_type=MESH,
        )
        copy.start()
        copies.append(copy)
    local = pltpu.make_async_copy(x_ref.at[me] if scatter else x_ref, slots.at[me], local_sem)
    local.start()
    local.wait()
    for copy in copies:
        copy.wait()
    o_ref[...] = slots[...]


def exchange(x, axis, cid, scatter=False):
    n = lax.axis_size(axis)
    block = x.shape[1:] if scatter else x.shape
    return pl.pallas_call(
        functools.partial(_exchange_kernel, axis, n, scatter),
        out_shape=jax.ShapeDtypeStruct((n,) + block, x.dtype),
        in_specs=[pl.BlockSpec(memory_space=pltpu.VMEM)],
        out_specs=pl.BlockSpec(memory_space=pltpu.VMEM),
        scratch_shapes=[
            pltpu.VMEM((n,) + block, x.dtype),
            pltpu.SemaphoreType.DMA((n - 1,)),
            pltpu.SemaphoreType.DMA((n - 1,)),
            pltpu.SemaphoreType.DMA,
        ],
        compiler_params=pltpu.CompilerParams(collective_id=cid, has_side_effects=True),
    )(x)


def _halo_kernel(hx, hy, x_ref, o_ref, wide, send_sem, recv_sem, local_sem):
    fields, cx, cy, cz = x_ref.shape
    ax, ay = lax.axis_index("gx"), lax.axis_index("gy")
    nx, ny = lax.axis_size("gx"), lax.axis_size("gy")
    wide[...] = jnp.zeros_like(wide)
    steps = [(dx, dy) for dx in (-1, 0, 1) for dy in (-1, 0, 1) if (dx, dy) != (0, 0)]

    def exists(dx, dy):
        return (ax + dx >= 0) & (ax + dx < nx) & (ay + dy >= 0) & (ay + dy < ny)

    def window(d, block, halo):
        if d < 0:
            return pl.ds(0, halo), pl.ds(block + halo, halo)
        if d > 0:
            return pl.ds(block - halo, halo), pl.ds(0, halo)
        return pl.ds(0, block), pl.ds(halo, block)

    barrier = pltpu.get_barrier_semaphore()
    for dx, dy in steps:
        @pl.when(exists(dx, dy))
        def _():
            pl.semaphore_signal(
                barrier, inc=1, device_id={"gx": ax + dx, "gy": ay + dy}, device_id_type=MESH
            )
    across = 1 + (ax + nx - 1) // nx + (2 * nx - 2 - ax) // nx
    along = 1 + (ay + ny - 1) // ny + (2 * ny - 2 - ay) // ny
    pl.semaphore_wait(barrier, across * along - 1)

    local = pltpu.make_async_copy(
        x_ref, wide.at[:, pl.ds(hx, cx), pl.ds(hy, cy), :], local_sem
    )
    local.start()
    copies = []
    for k, (dx, dy) in enumerate(steps):
        src_x, dst_x = window(dx, cx, hx)
        src_y, dst_y = window(dy, cy, hy)
        tx = jnp.clip(ax + dx, 0, nx - 1)
        ty = jnp.clip(ay + dy, 0, ny - 1)
        copy = pltpu.make_async_remote_copy(
            src_ref=x_ref.at[:, src_x, src_y, :],
            dst_ref=wide.at[:, dst_x, dst_y, :],
            send_sem=send_sem.at[k],
            recv_sem=recv_sem.at[k],
            device_id={"gx": tx, "gy": ty},
            device_id_type=MESH,
        )
        copies.append(copy)

        @pl.when(exists(dx, dy))
        def _():
            copy.start()

    local.wait()
    for copy, (dx, dy) in zip(copies, steps):
        @pl.when(exists(dx, dy))
        def _():
            copy.wait_send()

        @pl.when(exists(-dx, -dy))
        def _():
            copy.wait_recv()

    o_ref[...] = wide[...]


def halo_block(x, hx, hy, cid):
    fields, cx, cy, cz = x.shape
    shape = (fields, cx + 2 * hx, cy + 2 * hy, cz)
    return pl.pallas_call(
        functools.partial(_halo_kernel, hx, hy),
        out_shape=jax.ShapeDtypeStruct(shape, x.dtype),
        in_specs=[pl.BlockSpec(memory_space=pltpu.VMEM)],
        out_specs=pl.BlockSpec(memory_space=pltpu.VMEM),
        scratch_shapes=[
            pltpu.VMEM(shape, x.dtype),
            pltpu.SemaphoreType.DMA((8,)),
            pltpu.SemaphoreType.DMA((8,)),
            pltpu.SemaphoreType.DMA,
        ],
        compiler_params=pltpu.CompilerParams(
            collective_id=cid, has_side_effects=True, vmem_limit_bytes=48 * 1024 * 1024
        ),
    )(x)


def _reduce_kernel(axes, x_ref, o_ref, *scratch):
    stages = len(axes)
    slots, sends, recvs = scratch[:stages], scratch[stages : 2 * stages], scratch[2 * stages : 3 * stages]
    held = scratch[3 * stages :]
    barrier = pltpu.get_barrier_semaphore()
    peers = 0
    for axis in axes:
        n = lax.axis_size(axis)
        me = lax.axis_index(axis)
        for k in range(1, n):
            pl.semaphore_signal(
                barrier, inc=1, device_id={axis: lax.rem(me + k, n)}, device_id_type=MESH
            )
        peers += n - 1
    pl.semaphore_wait(barrier, peers)
    value = x_ref
    for i, axis in enumerate(axes):
        n = lax.axis_size(axis)
        me = lax.axis_index(axis)
        copies = []
        for k in range(1, n):
            copy = pltpu.make_async_remote_copy(
                src_ref=value,
                dst_ref=slots[i].at[me],
                send_sem=sends[i].at[k - 1],
                recv_sem=recvs[i].at[k - 1],
                device_id={axis: lax.rem(me + k, n)},
                device_id_type=MESH,
            )
            copy.start()
            copies.append(copy)
        slots[i][me] = value[...]
        for copy in copies:
            copy.wait()
        total = slots[i][0]
        for j in range(1, n):
            total = total + slots[i][j]
        if i + 1 < stages:
            held[i][...] = total
            value = held[i]
        else:
            o_ref[...] = total


def small_sum(values, axes, cid):
    count = values.shape[0]
    packed = jnp.pad(values, (0, 1024 - count)).reshape(8, 128)
    sizes = [lax.axis_size(axis) for axis in axes]
    scratch = (
        [pltpu.VMEM((n, 8, 128), jnp.float32) for n in sizes]
        + [pltpu.SemaphoreType.DMA((n - 1,)) for n in sizes]
        + [pltpu.SemaphoreType.DMA((n - 1,)) for n in sizes]
        + [pltpu.VMEM((8, 128), jnp.float32) for n in sizes[:-1]]
    )
    total = pl.pallas_call(
        functools.partial(_reduce_kernel, tuple(axes)),
        out_shape=jax.ShapeDtypeStruct((8, 128), jnp.float32),
        in_specs=[pl.BlockSpec(memory_space=pltpu.VMEM)],
        out_specs=pl.BlockSpec(memory_space=pltpu.VMEM),
        scratch_shapes=scratch,
        compiler_params=pltpu.CompilerParams(collective_id=cid, has_side_effects=True),
    )(packed)
    return total.reshape(-1)[:count]


def padded_2(block, sides, width):
    for axis, dim in sides:
        count = lax.axis_size(axis)
        forward = [(i, i + 1) for i in range(count - 1)]
        backward = [(target, source) for source, target in forward]
        low = lax.ppermute(
            lax.slice_in_dim(block, block.shape[dim] - width, None, axis=dim), axis, forward
        )
        high = lax.ppermute(lax.slice_in_dim(block, 0, width, axis=dim), axis, backward)
        block = jnp.concatenate([low, block, high], axis=dim)
    return block


def regional(labels, table):
    field = jnp.zeros(labels.shape, jnp.float32)
    for region in range(table.shape[0]):
        field = field + jnp.where(labels == region, table[region], 0.0)
    return field


def beside(padded):
    widths = [(0, 0)] * (padded.ndim - 1) + [(1, 1)]
    full = jnp.pad(padded, widths)
    return [
        full[..., 2:, 1:-1, 1:-1],
        full[..., :-2, 1:-1, 1:-1],
        full[..., 1:-1, 2:, 1:-1],
        full[..., 1:-1, :-2, 1:-1],
        full[..., 1:-1, 1:-1, 2:],
        full[..., 1:-1, 1:-1, :-2],
    ]


def around(field):
    widths = [(0, 0)] * (field.ndim - 3) + [(1, 1)] * 3
    full = jnp.pad(field, widths)
    return [
        full[..., 2:, 1:-1, 1:-1],
        full[..., :-2, 1:-1, 1:-1],
        full[..., 1:-1, 2:, 1:-1],
        full[..., 1:-1, :-2, 1:-1],
        full[..., 1:-1, 1:-1, 2:],
        full[..., 1:-1, 1:-1, :-2],
    ]


def trim(field):
    return field[:, 1:-1]


def chebyshev_trimmed(rhs, apply_at, lo):
    theta = 0.5 * (lam_high + lam_low)
    delta = 0.5 * (lam_high - lam_low)
    sigma = theta / delta
    rho = 1.0 / sigma
    solution = jnp.zeros_like(rhs)
    remain = rhs
    step_dir = rhs / theta
    for step in range(ITERS):
        solution = solution + step_dir
        if step + 1 < ITERS:
            applied = apply_at(step_dir, lo)
            lo += 1
            remain = trim(remain) - trim(applied)
            rho_next = 1.0 / (2.0 * sigma - rho)
            step_dir = rho_next * rho * trim(step_dir) + 2.0 * rho_next / delta * remain
            rho = rho_next
            solution = trim(solution)
    return solution


def chebyshev(rhs, apply_op):
    theta = 0.5 * (lam_high + lam_low)
    delta = 0.5 * (lam_high - lam_low)
    sigma = theta / delta
    rho = 1.0 / sigma
    solution = jnp.zeros_like(rhs)
    remain = rhs
    step_dir = rhs / theta
    for step in range(ITERS):
        solution = solution + step_dir
        if step + 1 < ITERS:
            remain = remain - apply_op(step_dir)
            rho_next = 1.0 / (2.0 * sigma - rho)
            step_dir = rho_next * rho * step_dir + 2.0 * rho_next / delta * remain
            rho = rho_next
    return solution


def per_device(
    labels,
    kappa_table,
    absorb_table,
    background,
    det_cells,
    v_kappa,
    v_absorb,
    q_kappa,
    q_absorb,
    beta_prev,
):
    sources, cx, cy, cz = background.shape
    n_src = lax.axis_size("src")
    slab = v_kappa.shape[2]
    pair = jnp.stack([v_kappa, v_absorb]).reshape(-1, 128)
    gathered = exchange(pair, "src", 0).reshape((n_src, 2, cx, cy, slab))
    full_k, full_a = jnp.transpose(gathered, (1, 2, 3, 0, 4)).reshape(2, cx, cy, cz)
    width = ITERS
    width_y = 8
    region_of = labels.astype(jnp.float32)[None]
    stacked = jnp.concatenate([background, region_of, full_k[None], full_a[None]], axis=0)
    wide = halo_block(stacked, width, width_y, 10)
    phi_w, region_w, vk_w, va_w = wide[:sources], wide[sources], wide[sources + 1], wide[sources + 2]
    wx = cx + 2 * width
    wy = cy + 2 * width_y
    gx_at = lax.axis_index("gx") * cx - width + jnp.arange(wx)
    gy_at = lax.axis_index("gy") * cy - width_y + jnp.arange(wy)
    inside = ((gx_at >= 0) & (gx_at < cx * lax.axis_size("gx")))[:, None, None] & (
        (gy_at >= 0) & (gy_at < cy * lax.axis_size("gy"))
    )[None, :, None]
    mask = inside.astype(jnp.float32)
    regions = kappa_table.shape[0]
    label_hot = (region_w.reshape(1, -1) == jnp.arange(regions, dtype=jnp.float32)[:, None]).astype(jnp.float32)
    tables = jnp.stack([kappa_table, absorb_table])
    fields = jnp.dot(tables, label_hot, precision=lax.Precision.HIGHEST).reshape(2, wx, wy, cz)
    kappa_w, absorb_w = mask * fields[0], mask * fields[1]
    kappa_faces = [mask * (0.5 * (kappa_w + near)) for near in around(kappa_w)]
    vk_faces = [mask * (0.5 * (vk_w + near)) for near in around(vk_w)]

    def apply_at(field, lo):
        hi = wx - lo
        result = absorb_w[lo:hi] * field
        for face, near in zip(kappa_faces, around(field)):
            result = result + face[lo:hi] * (field - near)
        return result

    rhs = va_w * phi_w
    for face, near in zip(vk_faces, around(phi_w)):
        rhs = rhs + face * (phi_w - near)
    rhs = -rhs
    change = chebyshev_trimmed(trim(rhs), apply_at, 1)[:, :, width_y : width_y + cy, :]
    span_y = cy * lax.axis_size("gy")
    ix = det_cells // (span_y * cz)
    iy = det_cells // cz % span_y
    iz = det_cells % cz
    anchor_x = lax.axis_index("gx") * cx
    anchor_y = lax.axis_index("gy") * cy
    owned = (ix >= anchor_x) & (ix < anchor_x + cx) & (iy >= anchor_y) & (iy < anchor_y + cy)
    plane = (ix - anchor_x) * cy + (iy - anchor_y)
    plane_hot = (jnp.arange(cx * cy)[:, None] == plane[None, :]) & owned[None, :]
    depth_hot = (jnp.arange(cz)[:, None] == iz[None, :]).astype(jnp.float32)
    both = jnp.concatenate([change, background], axis=0).reshape(-1, cz)
    picked = jnp.dot(both, depth_hot, precision=lax.Precision.HIGHEST).reshape(2 * sources, cx * cy, -1)
    picked = jnp.sum(jnp.where(plane_hot[None], picked, 0.0), axis=1)
    seen, base = picked[:sources], picked[sources:]
    partial = jnp.stack(
        [
            jnp.sum(base, axis=1),
            jnp.sum(seen, axis=1),
            jnp.sum(base * seen, axis=1),
            jnp.sum(base * base, axis=1),
        ],
        axis=1,
    )
    sums = small_sum(partial.reshape(-1), ("gy", "gx"), 1).reshape(sources, 4, 1)
    total, seen_sum, cross, square = sums[:, 0], sums[:, 1], sums[:, 2], sums[:, 3]
    mean_base = total / det_cells.shape[0]
    ratio = base / total
    jv_vals = (seen - ratio * seen_sum) / mean_base
    ratio_jv = (cross / total - seen_sum * (square / (total * total))) / mean_base
    weight = (jv_vals - ratio_jv) / mean_base
    spread = jnp.where(plane_hot[None], weight[:, None, :], 0.0).reshape(sources * cx * cy, -1)
    source = jnp.dot(spread, depth_hot.T, precision=lax.Precision.HIGHEST).reshape(change.shape)
    dual_w = chebyshev_trimmed(halo_block(source, width, width_y, 11), apply_at, 0)
    ring = (slice(None), slice(width - 1, width + cx + 1), slice(width_y - 1, width_y + cy + 1))
    phi_near = beside(phi_w[ring])
    dual_near = beside(dual_w[:, :, width_y - 1 : width_y + cy + 1])
    dual = dual_w[:, 1 : 1 + cx, width_y : width_y + cy, :]
    grad_a = -jnp.sum(background * dual, axis=0)
    grad_k = jnp.zeros_like(background[0])
    for near_phi, near_dual in zip(phi_near, dual_near):
        grad_k = grad_k - 0.5 * jnp.sum((background - near_phi) * (dual - near_dual), axis=0)
    grads = jnp.stack([grad_k, grad_a]).reshape(2, cx, cy, n_src, slab)
    grads = jnp.transpose(grads, (3, 0, 1, 2, 4)).reshape(n_src, -1, 128)
    hv = jnp.sum(exchange(grads, "src", 3, scatter=True), axis=0).reshape(2, cx, cy, slab)
    hv_k, hv_a = hv[0], hv[1]
    cell_count = cx * lax.axis_size("gx") * cy * lax.axis_size("gy") * cz
    w_k = hv_k - beta_prev[0] * q_kappa
    w_a = hv_a - beta_prev[0] * q_absorb
    local_wv = jnp.sum(w_k * v_kappa) + jnp.sum(w_a * v_absorb)
    local_vv = jnp.sum(v_kappa * v_kappa) + jnp.sum(v_absorb * v_absorb)
    wv_sum, vv_sum = small_sum(jnp.stack([local_wv, local_vv]), ("gy", "gx", "src"), 4)
    alpha = wv_sum / cell_count / (vv_sum / cell_count + eps_norm)
    r_k = w_k - alpha * v_kappa
    r_a = w_a - alpha * v_absorb
    rr_sum = small_sum((jnp.sum(r_k * r_k) + jnp.sum(r_a * r_a))[None], ("gy", "gx", "src"), 7)[0]
    beta = jnp.sqrt(rr_sum / cell_count + eps_norm)
    return (r_k / beta, r_a / beta, jnp.stack([alpha, beta]))


def solution(mesh):
    return jax.shard_map(
        per_device,
        mesh=mesh,
        in_specs=(
            P("gx", "gy", None),
            P(),
            P(),
            P("src", "gx", "gy", None),
            P(),
            P("gx", "gy", "src"),
            P("gx", "gy", "src"),
            P("gx", "gy", "src"),
            P("gx", "gy", "src"),
            P(),
        ),
        out_specs=(P("gx", "gy", "src"), P("gx", "gy", "src"), P()),
        check_vma=False,
    )
```

```python
import functools

import jax
import jax.numpy as jnp
from jax import lax
from jax.experimental import pallas as pl
from jax.experimental.pallas import tpu as pltpu
from jax.sharding import PartitionSpec as P

ITERS = 6
MESH = pl.DeviceIdType.MESH


lam_low = 0.02
lam_high = 24.1
eps_norm = 1e-06


def _exchange_kernel(axis, n, scatter, x_ref, o_ref, slots, send_sem, recv_sem, local_sem):
    me = lax.axis_index(axis)
    barrier = pltpu.get_barrier_semaphore()
    for k in range(1, n):
        peer = lax.rem(me + k, n)
        pl.semaphore_signal(barrier, inc=1, device_id={axis: peer}, device_id_type=MESH)
    pl.semaphore_wait(barrier, n - 1)
    copies = []
    for k in range(1, n):
        peer = lax.rem(me + k, n)
        copy = pltpu.make_async_remote_copy(
            src_ref=x_ref.at[peer] if scatter else x_ref,
            dst_ref=slots.at[me],
            send_sem=send_sem.at[k - 1],
            recv_sem=recv_sem.at[k - 1],
            device_id={axis: peer},
            device_id_type=MESH,
        )
        copy.start()
        copies.append(copy)
    local = pltpu.make_async_copy(x_ref.at[me] if scatter else x_ref, slots.at[me], local_sem)
    local.start()
    local.wait()
    for copy in copies:
        copy.wait()
    o_ref[...] = slots[...]


def exchange(x, axis, cid, scatter=False):
    n = lax.axis_size(axis)
    block = x.shape[1:] if scatter else x.shape
    return pl.pallas_call(
        functools.partial(_exchange_kernel, axis, n, scatter),
        out_shape=jax.ShapeDtypeStruct((n,) + block, x.dtype),
        in_specs=[pl.BlockSpec(memory_space=pltpu.VMEM)],
        out_specs=pl.BlockSpec(memory_space=pltpu.VMEM),
        scratch_shapes=[
            pltpu.VMEM((n,) + block, x.dtype),
            pltpu.SemaphoreType.DMA((n - 1,)),
            pltpu.SemaphoreType.DMA((n - 1,)),
            pltpu.SemaphoreType.DMA,
        ],
        compiler_params=pltpu.CompilerParams(collective_id=cid, has_side_effects=True),
    )(x)


def _halo_kernel(hx, hy, x_ref, o_ref, wide, send_sem, recv_sem, local_sem):
    fields, cx, cy, cz = x_ref.shape
    ax, ay = lax.axis_index("gx"), lax.axis_index("gy")
    nx, ny = lax.axis_size("gx"), lax.axis_size("gy")
    wide[...] = jnp.zeros_like(wide)
    steps = [(dx, dy) for dx in (-1, 0, 1) for dy in (-1, 0, 1) if (dx, dy) != (0, 0)]

    def exists(dx, dy):
        return (ax + dx >= 0) & (ax + dx < nx) & (ay + dy >= 0) & (ay + dy < ny)

    def window(d, block, halo):
        if d < 0:
            return pl.ds(0, halo), pl.ds(block + halo, halo)
        if d > 0:
            return pl.ds(block - halo, halo), pl.ds(0, halo)
        return pl.ds(0, block), pl.ds(halo, block)

    barrier = pltpu.get_barrier_semaphore()
    for dx, dy in steps:
        @pl.when(exists(dx, dy))
        def _():
            pl.semaphore_signal(
                barrier, inc=1, device_id={"gx": ax + dx, "gy": ay + dy}, device_id_type=MESH
            )
    across = 1 + (ax + nx - 1) // nx + (2 * nx - 2 - ax) // nx
    along = 1 + (ay + ny - 1) // ny + (2 * ny - 2 - ay) // ny
    pl.semaphore_wait(barrier, across * along - 1)

    local = pltpu.make_async_copy(
        x_ref, wide.at[:, pl.ds(hx, cx), pl.ds(hy, cy), :], local_sem
    )
    local.start()
    copies = []
    for k, (dx, dy) in enumerate(steps):
        src_x, dst_x = window(dx, cx, hx)
        src_y, dst_y = window(dy, cy, hy)
        tx = jnp.clip(ax + dx, 0, nx - 1)
        ty = jnp.clip(ay + dy, 0, ny - 1)
        copy = pltpu.make_async_remote_copy(
            src_ref=x_ref.at[:, src_x, src_y, :],
            dst_ref=wide.at[:, dst_x, dst_y, :],
            send_sem=send_sem.at[k],
            recv_sem=recv_sem.at[k],
            device_id={"gx": tx, "gy": ty},
            device_id_type=MESH,
        )
        copies.append(copy)

        @pl.when(exists(dx, dy))
        def _():
            copy.start()

    local.wait()
    for copy, (dx, dy) in zip(copies, steps):
        @pl.when(exists(dx, dy))
        def _():
            copy.wait_send()

        @pl.when(exists(-dx, -dy))
        def _():
            copy.wait_recv()

    o_ref[...] = wide[...]


def halo_block(x, hx, hy, cid):
    fields, cx, cy, cz = x.shape
    shape = (fields, cx + 2 * hx, cy + 2 * hy, cz)
    return pl.pallas_call(
        functools.partial(_halo_kernel, hx, hy),
        out_shape=jax.ShapeDtypeStruct(shape, x.dtype),
        in_specs=[pl.BlockSpec(memory_space=pltpu.VMEM)],
        out_specs=pl.BlockSpec(memory_space=pltpu.VMEM),
        scratch_shapes=[
            pltpu.VMEM(shape, x.dtype),
            pltpu.SemaphoreType.DMA((8,)),
            pltpu.SemaphoreType.DMA((8,)),
            pltpu.SemaphoreType.DMA,
        ],
        compiler_params=pltpu.CompilerParams(
            collective_id=cid, has_side_effects=True, vmem_limit_bytes=48 * 1024 * 1024
        ),
    )(x)


def _reduce_kernel(axes, scatter, *refs):
    stages = len(axes)
    if scatter:
        g_ref, x_ref, h_ref, o_ref, g_slots, g_send, g_recv, g_local = refs[:8]
        scratch = refs[8:]
    else:
        x_ref, o_ref = refs[:2]
        scratch = refs[2:]
    slots, sends, recvs = scratch[:stages], scratch[stages : 2 * stages], scratch[2 * stages : 3 * stages]
    held = scratch[3 * stages :]
    barrier = pltpu.get_barrier_semaphore()
    peers = 0
    for axis in axes:
        n = lax.axis_size(axis)
        me = lax.axis_index(axis)
        for k in range(1, n):
            pl.semaphore_signal(
                barrier, inc=1, device_id={axis: lax.rem(me + k, n)}, device_id_type=MESH
            )
        peers += n - 1
    pl.semaphore_wait(barrier, peers)
    if scatter:
        n = lax.axis_size("src")
        me = lax.axis_index("src")
        parts = []
        for k in range(1, n):
            peer = lax.rem(me + k, n)
            copy = pltpu.make_async_remote_copy(
                src_ref=g_ref.at[peer],
                dst_ref=g_slots.at[me],
                send_sem=g_send.at[k - 1],
                recv_sem=g_recv.at[k - 1],
                device_id={"src": peer},
                device_id_type=MESH,
            )
            copy.start()
            parts.append(copy)
        own = pltpu.make_async_copy(g_ref.at[me], g_slots.at[me], g_local)
        own.start()
    value = x_ref
    for i, axis in enumerate(axes):
        n = lax.axis_size(axis)
        me = lax.axis_index(axis)
        copies = []
        for k in range(1, n):
            copy = pltpu.make_async_remote_copy(
                src_ref=value,
                dst_ref=slots[i].at[me],
                send_sem=sends[i].at[k - 1],
                recv_sem=recvs[i].at[k - 1],
                device_id={axis: lax.rem(me + k, n)},
                device_id_type=MESH,
            )
            copy.start()
            copies.append(copy)
        slots[i][me] = value[...]
        for copy in copies:
            copy.wait()
        total = slots[i][0]
        for j in range(1, n):
            total = total + slots[i][j]
        if i + 1 < stages:
            held[i][...] = total
            value = held[i]
        else:
            o_ref[...] = total
    if scatter:
        own.wait()
        for copy in parts:
            copy.wait()
        total = g_slots[0]
        for j in range(1, lax.axis_size("src")):
            total = total + g_slots[j]
        h_ref[...] = total


def small_sum(values, axes, cid, spread=None):
    count = values.shape[0]
    packed = jnp.pad(values, (0, 1024 - count)).reshape(8, 128)
    sizes = [lax.axis_size(axis) for axis in axes]
    scratch = (
        [pltpu.VMEM((n, 8, 128), jnp.float32) for n in sizes]
        + [pltpu.SemaphoreType.DMA((n - 1,)) for n in sizes]
        + [pltpu.SemaphoreType.DMA((n - 1,)) for n in sizes]
        + [pltpu.VMEM((8, 128), jnp.float32) for n in sizes[:-1]]
    )
    small = jax.ShapeDtypeStruct((8, 128), jnp.float32)
    operands = (packed,)
    out_shape = small
    if spread is not None:
        n = spread.shape[0]
        scratch = [
            pltpu.VMEM(spread.shape, jnp.float32),
            pltpu.SemaphoreType.DMA((n - 1,)),
            pltpu.SemaphoreType.DMA((n - 1,)),
            pltpu.SemaphoreType.DMA,
        ] + scratch
        operands = (spread, packed)
        out_shape = (jax.ShapeDtypeStruct(spread.shape[1:], jnp.float32), small)
    result = pl.pallas_call(
        functools.partial(_reduce_kernel, tuple(axes), spread is not None),
        out_shape=out_shape,
        in_specs=[pl.BlockSpec(memory_space=pltpu.VMEM)] * len(operands),
        out_specs=(
            (pl.BlockSpec(memory_space=pltpu.VMEM),) * 2
            if spread is not None
            else pl.BlockSpec(memory_space=pltpu.VMEM)
        ),
        scratch_shapes=scratch,
        compiler_params=pltpu.CompilerParams(collective_id=cid, has_side_effects=True),
    )(*operands)
    if spread is not None:
        return result[0], result[1].reshape(-1)[:count]
    return result.reshape(-1)[:count]

def padded_2(block, sides, width):
    for axis, dim in sides:
        count = lax.axis_size(axis)
        forward = [(i, i + 1) for i in range(count - 1)]
        backward = [(target, source) for source, target in forward]
        low = lax.ppermute(
            lax.slice_in_dim(block, block.shape[dim] - width, None, axis=dim), axis, forward
        )
        high = lax.ppermute(lax.slice_in_dim(block, 0, width, axis=dim), axis, backward)
        block = jnp.concatenate([low, block, high], axis=dim)
    return block


def regional(labels, table):
    field = jnp.zeros(labels.shape, jnp.float32)
    for region in range(table.shape[0]):
        field = field + jnp.where(labels == region, table[region], 0.0)
    return field


def beside(padded):
    widths = [(0, 0)] * (padded.ndim - 1) + [(1, 1)]
    full = jnp.pad(padded, widths)
    return [
        full[..., 2:, 1:-1, 1:-1],
        full[..., :-2, 1:-1, 1:-1],
        full[..., 1:-1, 2:, 1:-1],
        full[..., 1:-1, :-2, 1:-1],
        full[..., 1:-1, 1:-1, 2:],
        full[..., 1:-1, 1:-1, :-2],
    ]


def around(field):
    widths = [(0, 0)] * (field.ndim - 3) + [(1, 1)] * 3
    full = jnp.pad(field, widths)
    return [
        full[..., 2:, 1:-1, 1:-1],
        full[..., :-2, 1:-1, 1:-1],
        full[..., 1:-1, 2:, 1:-1],
        full[..., 1:-1, :-2, 1:-1],
        full[..., 1:-1, 1:-1, 2:],
        full[..., 1:-1, 1:-1, :-2],
    ]


def chebyshev(rhs, apply_op):
    theta = 0.5 * (lam_high + lam_low)
    delta = 0.5 * (lam_high - lam_low)
    sigma = theta / delta
    rho = 1.0 / sigma
    solution = jnp.zeros_like(rhs)
    remain = rhs
    step_dir = rhs / theta
    for step in range(ITERS):
        solution = solution + step_dir
        if step + 1 < ITERS:
            remain = remain - apply_op(step_dir)
            rho_next = 1.0 / (2.0 * sigma - rho)
            step_dir = rho_next * rho * step_dir + 2.0 * rho_next / delta * remain
            rho = rho_next
    return solution


def per_device(
    labels,
    kappa_table,
    absorb_table,
    background,
    det_cells,
    v_kappa,
    v_absorb,
    q_kappa,
    q_absorb,
    beta_prev,
):
    sources, cx, cy, cz = background.shape
    n_src = lax.axis_size("src")
    slab = v_kappa.shape[2]
    quad = jnp.stack([v_kappa, v_absorb, q_kappa, q_absorb]).reshape(-1, 128)
    gathered = exchange(quad, "src", 0).reshape((n_src, 4, cx, cy, slab))
    full_k, full_a, full_qk, full_qa = jnp.transpose(gathered, (1, 2, 3, 0, 4)).reshape(4, cx, cy, cz)
    width = ITERS
    width_y = 8
    region_of = labels.astype(jnp.float32)[None]
    stacked = jnp.concatenate([background, region_of, full_k[None], full_a[None]], axis=0)
    wide = halo_block(stacked, width, width_y, 10)
    phi_w, region_w, vk_w, va_w = wide[:sources], wide[sources], wide[sources + 1], wide[sources + 2]
    wx = cx + 2 * width
    wy = cy + 2 * width_y
    gx_at = lax.axis_index("gx") * cx - width + jnp.arange(wx)
    gy_at = lax.axis_index("gy") * cy - width_y + jnp.arange(wy)
    inside = ((gx_at >= 0) & (gx_at < cx * lax.axis_size("gx")))[:, None, None] & (
        (gy_at >= 0) & (gy_at < cy * lax.axis_size("gy"))
    )[None, :, None]
    mask = inside.astype(jnp.float32)
    regions = kappa_table.shape[0]
    label_hot = (region_w.reshape(1, -1) == jnp.arange(regions, dtype=jnp.float32)[:, None]).astype(jnp.float32)
    tables = jnp.stack([kappa_table, absorb_table])
    fields = jnp.dot(tables, label_hot, precision=lax.Precision.HIGHEST).reshape(2, wx, wy, cz)
    kappa_w, absorb_w = mask * fields[0], mask * fields[1]
    kappa_faces = [mask * (0.5 * (kappa_w + near)) for near in around(kappa_w)]
    vk_faces = [mask * (0.5 * (vk_w + near)) for near in around(vk_w)]

    def apply_op(field):
        result = absorb_w * field
        for face, near in zip(kappa_faces, around(field)):
            result = result + face * (field - near)
        return result

    rhs = va_w * phi_w
    for face, near in zip(vk_faces, around(phi_w)):
        rhs = rhs + face * (phi_w - near)
    rhs = -rhs
    change = chebyshev(rhs, apply_op)[:, width : width + cx, width_y : width_y + cy, :]
    span_y = cy * lax.axis_size("gy")
    ix = det_cells // (span_y * cz)
    iy = det_cells // cz % span_y
    iz = det_cells % cz
    anchor_x = lax.axis_index("gx") * cx
    anchor_y = lax.axis_index("gy") * cy
    owned = (ix >= anchor_x) & (ix < anchor_x + cx) & (iy >= anchor_y) & (iy < anchor_y + cy)
    plane = (ix - anchor_x) * cy + (iy - anchor_y)
    plane_hot = (jnp.arange(cx * cy)[:, None] == plane[None, :]) & owned[None, :]
    depth_hot = (jnp.arange(cz)[:, None] == iz[None, :]).astype(jnp.float32)
    both = jnp.concatenate([change, background], axis=0).reshape(-1, cz)
    picked = jnp.dot(both, depth_hot, precision=lax.Precision.HIGHEST).reshape(2 * sources, cx * cy, -1)
    picked = jnp.sum(jnp.where(plane_hot[None], picked, 0.0), axis=1)
    seen, base = picked[:sources], picked[sources:]
    partial = jnp.stack(
        [
            jnp.sum(base, axis=1),
            jnp.sum(seen, axis=1),
            jnp.sum(base * seen, axis=1),
            jnp.sum(base * base, axis=1),
        ],
        axis=1,
    )
    block_vv = jnp.sum(full_k * full_k) + jnp.sum(full_a * full_a)
    block_qv = jnp.sum(full_qk * full_k) + jnp.sum(full_qa * full_a)
    partial = jnp.concatenate([partial.reshape(-1), jnp.stack([block_vv, block_qv])])
    sums = small_sum(partial, ("gy", "gx"), 1)
    vv_sum, qv_sum = sums[4 * sources], sums[4 * sources + 1]
    sums = sums[: 4 * sources].reshape(sources, 4, 1)
    total, seen_sum, cross, square = sums[:, 0], sums[:, 1], sums[:, 2], sums[:, 3]
    mean_base = total / det_cells.shape[0]
    ratio = base / total
    jv_vals = (seen - ratio * seen_sum) / mean_base
    ratio_jv = (cross / total - seen_sum * (square / (total * total))) / mean_base
    weight = (jv_vals - ratio_jv) / mean_base
    spread = jnp.where(plane_hot[None], weight[:, None, :], 0.0).reshape(sources * cx * cy, -1)
    source = jnp.dot(spread, depth_hot.T, precision=lax.Precision.HIGHEST).reshape(change.shape)
    dual_w = chebyshev(halo_block(source, width, width_y, 11), apply_op)
    ring = (slice(None), slice(width - 1, width + cx + 1), slice(width_y - 1, width_y + cy + 1))
    phi_near = beside(phi_w[ring])
    dual_near = beside(dual_w[ring])
    dual = dual_w[:, width : width + cx, width_y : width_y + cy, :]
    grad_a = -jnp.sum(background * dual, axis=0)
    grad_k = jnp.zeros_like(background[0])
    for near_phi, near_dual in zip(phi_near, dual_near):
        grad_k = grad_k - 0.5 * jnp.sum((background - near_phi) * (dual - near_dual), axis=0)
    grads = jnp.stack([grad_k, grad_a]).reshape(2, cx, cy, n_src, slab)
    grads = jnp.transpose(grads, (3, 0, 1, 2, 4)).reshape(n_src, -1, 128)
    block_hv = jnp.sum(grad_k * full_k) + jnp.sum(grad_a * full_a)
    hv, hv_sum = small_sum(block_hv[None], ("gy", "gx", "src"), 3, spread=grads)
    hv = hv.reshape(2, cx, cy, slab)
    hv_k, hv_a = hv[0], hv[1]
    cell_count = cx * lax.axis_size("gx") * cy * lax.axis_size("gy") * cz
    w_k = hv_k - beta_prev[0] * q_kappa
    w_a = hv_a - beta_prev[0] * q_absorb
    wv_sum = hv_sum[0] - beta_prev[0] * qv_sum
    alpha = wv_sum / cell_count / (vv_sum / cell_count + eps_norm)
    r_k = w_k - alpha * v_kappa
    r_a = w_a - alpha * v_absorb
    rr_sum = small_sum((jnp.sum(r_k * r_k) + jnp.sum(r_a * r_a))[None], ("gy", "gx", "src"), 7)[0]
    beta = jnp.sqrt(rr_sum / cell_count + eps_norm)
    return (r_k / beta, r_a / beta, jnp.stack([alpha, beta]))


def solution(mesh):
    return jax.shard_map(
        per_device,
        mesh=mesh,
        in_specs=(
            P("gx", "gy", None),
            P(),
            P(),
            P("src", "gx", "gy", None),
            P(),
            P("gx", "gy", "src"),
            P("gx", "gy", "src"),
            P("gx", "gy", "src"),
            P("gx", "gy", "src"),
            P(),
        ),
        out_specs=(P("gx", "gy", "src"), P("gx", "gy", "src"), P()),
        check_vma=False,
    )
```

```python
import functools

import jax
import jax.numpy as jnp
from jax import lax
from jax.experimental import pallas as pl
from jax.experimental.pallas import tpu as pltpu
from jax.sharding import PartitionSpec as P

ITERS = 6
MESH = pl.DeviceIdType.MESH


lam_low = 0.02
lam_high = 24.1
eps_norm = 1e-06


def _exchange_kernel(axis, n, scatter, x_ref, o_ref, slots, send_sem, recv_sem, local_sem):
    me = lax.axis_index(axis)
    barrier = pltpu.get_barrier_semaphore()
    for k in range(1, n):
        peer = lax.rem(me + k, n)
        pl.semaphore_signal(barrier, inc=1, device_id={axis: peer}, device_id_type=MESH)
    pl.semaphore_wait(barrier, n - 1)
    copies = []
    for k in range(1, n):
        peer = lax.rem(me + k, n)
        copy = pltpu.make_async_remote_copy(
            src_ref=x_ref.at[peer] if scatter else x_ref,
            dst_ref=slots.at[me],
            send_sem=send_sem.at[k - 1],
            recv_sem=recv_sem.at[k - 1],
            device_id={axis: peer},
            device_id_type=MESH,
        )
        copy.start()
        copies.append(copy)
    local = pltpu.make_async_copy(x_ref.at[me] if scatter else x_ref, slots.at[me], local_sem)
    local.start()
    local.wait()
    for copy in copies:
        copy.wait()
    o_ref[...] = slots[...]


def exchange(x, axis, cid, scatter=False):
    n = lax.axis_size(axis)
    block = x.shape[1:] if scatter else x.shape
    return pl.pallas_call(
        functools.partial(_exchange_kernel, axis, n, scatter),
        out_shape=jax.ShapeDtypeStruct((n,) + block, x.dtype),
        in_specs=[pl.BlockSpec(memory_space=pltpu.VMEM)],
        out_specs=pl.BlockSpec(memory_space=pltpu.VMEM),
        scratch_shapes=[
            pltpu.VMEM((n,) + block, x.dtype),
            pltpu.SemaphoreType.DMA((n - 1,)),
            pltpu.SemaphoreType.DMA((n - 1,)),
            pltpu.SemaphoreType.DMA,
        ],
        compiler_params=pltpu.CompilerParams(collective_id=cid, has_side_effects=True),
    )(x)


def _halo_kernel(hx, hy, x_ref, o_ref, wide, send_sem, recv_sem, local_sem):
    fields, cx, cy, cz = x_ref.shape
    ax, ay = lax.axis_index("gx"), lax.axis_index("gy")
    nx, ny = lax.axis_size("gx"), lax.axis_size("gy")
    wide[...] = jnp.zeros_like(wide)
    steps = [(dx, dy) for dx in (-1, 0, 1) for dy in (-1, 0, 1) if (dx, dy) != (0, 0)]

    def exists(dx, dy):
        return (ax + dx >= 0) & (ax + dx < nx) & (ay + dy >= 0) & (ay + dy < ny)

    def window(d, block, halo):
        if d < 0:
            return pl.ds(0, halo), pl.ds(block + halo, halo)
        if d > 0:
            return pl.ds(block - halo, halo), pl.ds(0, halo)
        return pl.ds(0, block), pl.ds(halo, block)

    barrier = pltpu.get_barrier_semaphore()
    for dx, dy in steps:
        @pl.when(exists(dx, dy))
        def _():
            pl.semaphore_signal(
                barrier, inc=1, device_id={"gx": ax + dx, "gy": ay + dy}, device_id_type=MESH
            )
    across = 1 + (ax + nx - 1) // nx + (2 * nx - 2 - ax) // nx
    along = 1 + (ay + ny - 1) // ny + (2 * ny - 2 - ay) // ny
    pl.semaphore_wait(barrier, across * along - 1)

    local = pltpu.make_async_copy(
        x_ref, wide.at[:, pl.ds(hx, cx), pl.ds(hy, cy), :], local_sem
    )
    local.start()
    copies = []
    for k, (dx, dy) in enumerate(steps):
        src_x, dst_x = window(dx, cx, hx)
        src_y, dst_y = window(dy, cy, hy)
        tx = jnp.clip(ax + dx, 0, nx - 1)
        ty = jnp.clip(ay + dy, 0, ny - 1)
        copy = pltpu.make_async_remote_copy(
            src_ref=x_ref.at[:, src_x, src_y, :],
            dst_ref=wide.at[:, dst_x, dst_y, :],
            send_sem=send_sem.at[k],
            recv_sem=recv_sem.at[k],
            device_id={"gx": tx, "gy": ty},
            device_id_type=MESH,
        )
        copies.append(copy)

        @pl.when(exists(dx, dy))
        def _():
            copy.start()

    local.wait()
    for copy, (dx, dy) in zip(copies, steps):
        @pl.when(exists(dx, dy))
        def _():
            copy.wait_send()

        @pl.when(exists(-dx, -dy))
        def _():
            copy.wait_recv()

    o_ref[...] = wide[...]


def halo_block(x, hx, hy, cid):
    fields, cx, cy, cz = x.shape
    shape = (fields, cx + 2 * hx, cy + 2 * hy, cz)
    return pl.pallas_call(
        functools.partial(_halo_kernel, hx, hy),
        out_shape=jax.ShapeDtypeStruct(shape, x.dtype),
        in_specs=[pl.BlockSpec(memory_space=pltpu.VMEM)],
        out_specs=pl.BlockSpec(memory_space=pltpu.VMEM),
        scratch_shapes=[
            pltpu.VMEM(shape, x.dtype),
            pltpu.SemaphoreType.DMA((8,)),
            pltpu.SemaphoreType.DMA((8,)),
            pltpu.SemaphoreType.DMA,
        ],
        compiler_params=pltpu.CompilerParams(
            collective_id=cid, has_side_effects=True, vmem_limit_bytes=48 * 1024 * 1024
        ),
    )(x)


def _reduce_kernel(axes, x_ref, o_ref, *scratch):
    stages = len(axes)
    slots, sends, recvs = scratch[:stages], scratch[stages : 2 * stages], scratch[2 * stages : 3 * stages]
    held = scratch[3 * stages :]
    barrier = pltpu.get_barrier_semaphore()
    peers = 0
    for axis in axes:
        n = lax.axis_size(axis)
        me = lax.axis_index(axis)
        for k in range(1, n):
            pl.semaphore_signal(
                barrier, inc=1, device_id={axis: lax.rem(me + k, n)}, device_id_type=MESH
            )
        peers += n - 1
    pl.semaphore_wait(barrier, peers)
    value = x_ref
    for i, axis in enumerate(axes):
        n = lax.axis_size(axis)
        me = lax.axis_index(axis)
        copies = []
        for k in range(1, n):
            copy = pltpu.make_async_remote_copy(
                src_ref=value,
                dst_ref=slots[i].at[me],
                send_sem=sends[i].at[k - 1],
                recv_sem=recvs[i].at[k - 1],
                device_id={axis: lax.rem(me + k, n)},
                device_id_type=MESH,
            )
            copy.start()
            copies.append(copy)
        slots[i][me] = value[...]
        for copy in copies:
            copy.wait()
        total = slots[i][0]
        for j in range(1, n):
            total = total + slots[i][j]
        if i + 1 < stages:
            held[i][...] = total
            value = held[i]
        else:
            o_ref[...] = total


def small_sum(values, axes, cid):
    count = values.shape[0]
    rows = -(-count // 1024) * 8
    packed = jnp.pad(values, (0, rows * 128 - count)).reshape(rows, 128)
    sizes = [lax.axis_size(axis) for axis in axes]
    scratch = (
        [pltpu.VMEM((n, rows, 128), jnp.float32) for n in sizes]
        + [pltpu.SemaphoreType.DMA((n - 1,)) for n in sizes]
        + [pltpu.SemaphoreType.DMA((n - 1,)) for n in sizes]
        + [pltpu.VMEM((rows, 128), jnp.float32) for n in sizes[:-1]]
    )
    total = pl.pallas_call(
        functools.partial(_reduce_kernel, tuple(axes)),
        out_shape=jax.ShapeDtypeStruct((rows, 128), jnp.float32),
        in_specs=[pl.BlockSpec(memory_space=pltpu.VMEM)],
        out_specs=pl.BlockSpec(memory_space=pltpu.VMEM),
        scratch_shapes=scratch,
        compiler_params=pltpu.CompilerParams(collective_id=cid, has_side_effects=True),
    )(packed)
    return total.reshape(-1)[:count]


def padded_2(block, sides, width):
    for axis, dim in sides:
        count = lax.axis_size(axis)
        forward = [(i, i + 1) for i in range(count - 1)]
        backward = [(target, source) for source, target in forward]
        low = lax.ppermute(
            lax.slice_in_dim(block, block.shape[dim] - width, None, axis=dim), axis, forward
        )
        high = lax.ppermute(lax.slice_in_dim(block, 0, width, axis=dim), axis, backward)
        block = jnp.concatenate([low, block, high], axis=dim)
    return block


def regional(labels, table):
    field = jnp.zeros(labels.shape, jnp.float32)
    for region in range(table.shape[0]):
        field = field + jnp.where(labels == region, table[region], 0.0)
    return field


def beside(padded):
    widths = [(0, 0)] * (padded.ndim - 1) + [(1, 1)]
    full = jnp.pad(padded, widths)
    return [
        full[..., 2:, 1:-1, 1:-1],
        full[..., :-2, 1:-1, 1:-1],
        full[..., 1:-1, 2:, 1:-1],
        full[..., 1:-1, :-2, 1:-1],
        full[..., 1:-1, 1:-1, 2:],
        full[..., 1:-1, 1:-1, :-2],
    ]


def around(field):
    widths = [(0, 0)] * (field.ndim - 3) + [(1, 1)] * 3
    full = jnp.pad(field, widths)
    return [
        full[..., 2:, 1:-1, 1:-1],
        full[..., :-2, 1:-1, 1:-1],
        full[..., 1:-1, 2:, 1:-1],
        full[..., 1:-1, :-2, 1:-1],
        full[..., 1:-1, 1:-1, 2:],
        full[..., 1:-1, 1:-1, :-2],
    ]


def chebyshev(rhs, apply_op):
    theta = 0.5 * (lam_high + lam_low)
    delta = 0.5 * (lam_high - lam_low)
    sigma = theta / delta
    rho = 1.0 / sigma
    solution = jnp.zeros_like(rhs)
    remain = rhs
    step_dir = rhs / theta
    for step in range(ITERS):
        solution = solution + step_dir
        if step + 1 < ITERS:
            remain = remain - apply_op(step_dir)
            rho_next = 1.0 / (2.0 * sigma - rho)
            step_dir = rho_next * rho * step_dir + 2.0 * rho_next / delta * remain
            rho = rho_next
    return solution


def per_device(
    labels,
    kappa_table,
    absorb_table,
    background,
    det_cells,
    v_kappa,
    v_absorb,
    q_kappa,
    q_absorb,
    beta_prev,
):
    sources, cx, cy, cz = background.shape
    n_src = lax.axis_size("src")
    slab = v_kappa.shape[2]
    pair = jnp.stack([v_kappa, v_absorb]).reshape(-1, 128)
    gathered = exchange(pair, "src", 0).reshape((n_src, 2, cx, cy, slab))
    full_k, full_a = jnp.transpose(gathered, (1, 2, 3, 0, 4)).reshape(2, cx, cy, cz)
    width = ITERS
    width_y = 8
    region_of = labels.astype(jnp.float32)[None]
    stacked = jnp.concatenate([background, region_of, full_k[None], full_a[None]], axis=0)
    wide = halo_block(stacked, width, width_y, 10)
    phi_w, region_w, vk_w, va_w = wide[:sources], wide[sources], wide[sources + 1], wide[sources + 2]
    wx = cx + 2 * width
    wy = cy + 2 * width_y
    gx_at = lax.axis_index("gx") * cx - width + jnp.arange(wx)
    gy_at = lax.axis_index("gy") * cy - width_y + jnp.arange(wy)
    inside = ((gx_at >= 0) & (gx_at < cx * lax.axis_size("gx")))[:, None, None] & (
        (gy_at >= 0) & (gy_at < cy * lax.axis_size("gy"))
    )[None, :, None]
    mask = inside.astype(jnp.float32)
    regions = kappa_table.shape[0]
    label_hot = (region_w.reshape(1, -1) == jnp.arange(regions, dtype=jnp.float32)[:, None]).astype(jnp.float32)
    tables = jnp.stack([kappa_table, absorb_table])
    fields = jnp.dot(tables, label_hot, precision=lax.Precision.HIGHEST).reshape(2, wx, wy, cz)
    kappa_w, absorb_w = mask * fields[0], mask * fields[1]
    kappa_faces = [mask * (0.5 * (kappa_w + near)) for near in around(kappa_w)]
    vk_faces = [mask * (0.5 * (vk_w + near)) for near in around(vk_w)]

    def apply_op(field):
        result = absorb_w * field
        for face, near in zip(kappa_faces, around(field)):
            result = result + face * (field - near)
        return result

    rhs = va_w * phi_w
    for face, near in zip(vk_faces, around(phi_w)):
        rhs = rhs + face * (phi_w - near)
    rhs = -rhs
    change = chebyshev(rhs, apply_op)[:, width : width + cx, width_y : width_y + cy, :]
    span_y = cy * lax.axis_size("gy")
    ix = det_cells // (span_y * cz)
    iy = det_cells // cz % span_y
    iz = det_cells % cz
    anchor_x = lax.axis_index("gx") * cx
    anchor_y = lax.axis_index("gy") * cy
    owned = (ix >= anchor_x) & (ix < anchor_x + cx) & (iy >= anchor_y) & (iy < anchor_y + cy)
    plane = (ix - anchor_x) * cy + (iy - anchor_y)
    plane_hot = (jnp.arange(cx * cy)[:, None] == plane[None, :]) & owned[None, :]
    depth_hot = (jnp.arange(cz)[:, None] == iz[None, :]).astype(jnp.float32)
    both = jnp.concatenate([change, background], axis=0).reshape(-1, cz)
    picked = jnp.dot(both, depth_hot, precision=lax.Precision.HIGHEST).reshape(2 * sources, cx * cy, -1)
    picked = jnp.sum(jnp.where(plane_hot[None], picked, 0.0), axis=1)
    picks = small_sum(picked.reshape(-1), ("gy", "gx"), 1).reshape(2 * sources, -1)
    seen, base = picks[:sources], picks[sources:]
    total = jnp.sum(base, axis=1, keepdims=True)
    mean_base = total / det_cells.shape[0]
    ratio = base / total
    jv_vals = (seen - ratio * jnp.sum(seen, axis=1, keepdims=True)) / mean_base
    weight = (jv_vals - jnp.sum(ratio * jv_vals, axis=1, keepdims=True)) / mean_base
    near_x = ix - (anchor_x - width)
    near_y = iy - (anchor_y - width_y)
    held = (near_x >= 0) & (near_x < wx) & (near_y >= 0) & (near_y < wy)
    wide_hot = (jnp.arange(wx * wy)[:, None] == (near_x * wy + near_y)[None, :]) & held[None, :]
    wide_hot = wide_hot.astype(jnp.float32)
    source_w = jnp.stack(
        [
            jnp.dot(wide_hot, weight[i][:, None] * depth_hot.T, precision=lax.Precision.HIGHEST)
            for i in range(sources)
        ]
    ).reshape(sources, wx, wy, cz)
    dual_w = chebyshev(source_w, apply_op)
    ring = (slice(None), slice(width - 1, width + cx + 1), slice(width_y - 1, width_y + cy + 1))
    phi_near = beside(phi_w[ring])
    dual_near = beside(dual_w[ring])
    dual = dual_w[:, width : width + cx, width_y : width_y + cy, :]
    grad_a = -jnp.sum(background * dual, axis=0)
    grad_k = jnp.zeros_like(background[0])
    for near_phi, near_dual in zip(phi_near, dual_near):
        grad_k = grad_k - 0.5 * jnp.sum((background - near_phi) * (dual - near_dual), axis=0)
    grads = jnp.stack([grad_k, grad_a]).reshape(2, cx, cy, n_src, slab)
    grads = jnp.transpose(grads, (3, 0, 1, 2, 4)).reshape(n_src, -1, 128)
    hv = jnp.sum(exchange(grads, "src", 3, scatter=True), axis=0).reshape(2, cx, cy, slab)
    hv_k, hv_a = hv[0], hv[1]
    cell_count = cx * lax.axis_size("gx") * cy * lax.axis_size("gy") * cz
    w_k = hv_k - beta_prev[0] * q_kappa
    w_a = hv_a - beta_prev[0] * q_absorb
    local_wv = jnp.sum(w_k * v_kappa) + jnp.sum(w_a * v_absorb)
    local_vv = jnp.sum(v_kappa * v_kappa) + jnp.sum(v_absorb * v_absorb)
    wv_sum, vv_sum = small_sum(jnp.stack([local_wv, local_vv]), ("gy", "gx", "src"), 4)
    alpha = wv_sum / cell_count / (vv_sum / cell_count + eps_norm)
    r_k = w_k - alpha * v_kappa
    r_a = w_a - alpha * v_absorb
    rr_sum = small_sum((jnp.sum(r_k * r_k) + jnp.sum(r_a * r_a))[None], ("gy", "gx", "src"), 7)[0]
    beta = jnp.sqrt(rr_sum / cell_count + eps_norm)
    return (r_k / beta, r_a / beta, jnp.stack([alpha, beta]))


def solution(mesh):
    return jax.shard_map(
        per_device,
        mesh=mesh,
        in_specs=(
            P("gx", "gy", None),
            P(),
            P(),
            P("src", "gx", "gy", None),
            P(),
            P("gx", "gy", "src"),
            P("gx", "gy", "src"),
            P("gx", "gy", "src"),
            P("gx", "gy", "src"),
            P(),
        ),
        out_specs=(P("gx", "gy", "src"), P("gx", "gy", "src"), P()),
        check_vma=False,
    )
```

```python
import functools

import jax
import jax.numpy as jnp
from jax import lax
from jax.experimental import pallas as pl
from jax.experimental.pallas import tpu as pltpu
from jax.sharding import PartitionSpec as P

ITERS = 6
MESH = pl.DeviceIdType.MESH


lam_low = 0.02
lam_high = 24.1
eps_norm = 1e-06


def _exchange_kernel(axis, n, scatter, x_ref, o_ref, slots, send_sem, recv_sem, local_sem):
    me = lax.axis_index(axis)
    barrier = pltpu.get_barrier_semaphore()
    for k in range(1, n):
        peer = lax.rem(me + k, n)
        pl.semaphore_signal(barrier, inc=1, device_id={axis: peer}, device_id_type=MESH)
    pl.semaphore_wait(barrier, n - 1)
    copies = []
    for k in range(1, n):
        peer = lax.rem(me + k, n)
        copy = pltpu.make_async_remote_copy(
            src_ref=x_ref.at[peer] if scatter else x_ref,
            dst_ref=slots.at[me],
            send_sem=send_sem.at[k - 1],
            recv_sem=recv_sem.at[k - 1],
            device_id={axis: peer},
            device_id_type=MESH,
        )
        copy.start()
        copies.append(copy)
    local = pltpu.make_async_copy(x_ref.at[me] if scatter else x_ref, slots.at[me], local_sem)
    local.start()
    local.wait()
    for copy in copies:
        copy.wait()
    o_ref[...] = slots[...]


def exchange(x, axis, cid, scatter=False):
    n = lax.axis_size(axis)
    block = x.shape[1:] if scatter else x.shape
    return pl.pallas_call(
        functools.partial(_exchange_kernel, axis, n, scatter),
        out_shape=jax.ShapeDtypeStruct((n,) + block, x.dtype),
        in_specs=[pl.BlockSpec(memory_space=pltpu.VMEM)],
        out_specs=pl.BlockSpec(memory_space=pltpu.VMEM),
        scratch_shapes=[
            pltpu.VMEM((n,) + block, x.dtype),
            pltpu.SemaphoreType.DMA((n - 1,)),
            pltpu.SemaphoreType.DMA((n - 1,)),
            pltpu.SemaphoreType.DMA,
        ],
        compiler_params=pltpu.CompilerParams(collective_id=cid, has_side_effects=True),
    )(x)


def _halo_kernel(hx, hy, x_ref, o_ref, wide, send_sem, recv_sem, local_sem):
    fields, cx, cy, cz = x_ref.shape
    ax, ay = lax.axis_index("gx"), lax.axis_index("gy")
    nx, ny = lax.axis_size("gx"), lax.axis_size("gy")
    wide[...] = jnp.zeros_like(wide)
    steps = [(dx, dy) for dx in (-1, 0, 1) for dy in (-1, 0, 1) if (dx, dy) != (0, 0)]

    def exists(dx, dy):
        return (ax + dx >= 0) & (ax + dx < nx) & (ay + dy >= 0) & (ay + dy < ny)

    def window(d, block, halo):
        if d < 0:
            return pl.ds(0, halo), pl.ds(block + halo, halo)
        if d > 0:
            return pl.ds(block - halo, halo), pl.ds(0, halo)
        return pl.ds(0, block), pl.ds(halo, block)

    barrier = pltpu.get_barrier_semaphore()
    for dx, dy in steps:
        @pl.when(exists(dx, dy))
        def _():
            pl.semaphore_signal(
                barrier, inc=1, device_id={"gx": ax + dx, "gy": ay + dy}, device_id_type=MESH
            )
    across = 1 + (ax + nx - 1) // nx + (2 * nx - 2 - ax) // nx
    along = 1 + (ay + ny - 1) // ny + (2 * ny - 2 - ay) // ny
    pl.semaphore_wait(barrier, across * along - 1)

    local = pltpu.make_async_copy(
        x_ref, wide.at[:, pl.ds(hx, cx), pl.ds(hy, cy), :], local_sem
    )
    local.start()
    copies = []
    for k, (dx, dy) in enumerate(steps):
        src_x, dst_x = window(dx, cx, hx)
        src_y, dst_y = window(dy, cy, hy)
        tx = jnp.clip(ax + dx, 0, nx - 1)
        ty = jnp.clip(ay + dy, 0, ny - 1)
        copy = pltpu.make_async_remote_copy(
            src_ref=x_ref.at[:, src_x, src_y, :],
            dst_ref=wide.at[:, dst_x, dst_y, :],
            send_sem=send_sem.at[k],
            recv_sem=recv_sem.at[k],
            device_id={"gx": tx, "gy": ty},
            device_id_type=MESH,
        )
        copies.append(copy)

        @pl.when(exists(dx, dy))
        def _():
            copy.start()

    local.wait()
    for copy, (dx, dy) in zip(copies, steps):
        @pl.when(exists(dx, dy))
        def _():
            copy.wait_send()

        @pl.when(exists(-dx, -dy))
        def _():
            copy.wait_recv()

    o_ref[...] = wide[...]


def halo_block(x, hx, hy, cid):
    fields, cx, cy, cz = x.shape
    shape = (fields, cx + 2 * hx, cy + 2 * hy, cz)
    return pl.pallas_call(
        functools.partial(_halo_kernel, hx, hy),
        out_shape=jax.ShapeDtypeStruct(shape, x.dtype),
        in_specs=[pl.BlockSpec(memory_space=pltpu.VMEM)],
        out_specs=pl.BlockSpec(memory_space=pltpu.VMEM),
        scratch_shapes=[
            pltpu.VMEM(shape, x.dtype),
            pltpu.SemaphoreType.DMA((8,)),
            pltpu.SemaphoreType.DMA((8,)),
            pltpu.SemaphoreType.DMA,
        ],
        compiler_params=pltpu.CompilerParams(
            collective_id=cid, has_side_effects=True, vmem_limit_bytes=48 * 1024 * 1024
        ),
    )(x)


def _group(axes):
    sizes = [lax.axis_size(axis) for axis in axes]
    n = 1
    for size in sizes:
        n *= size
    me = 0
    for axis, size in zip(axes, sizes):
        me = me * size + lax.axis_index(axis)

    def member(index):
        ids = {}
        for axis, size in reversed(list(zip(axes, sizes))):
            ids[axis] = index % size
            index = index // size
        return ids

    return n, me, member


def _reduce_kernel(stages, x_ref, o_ref, *scratch):
    count = len(stages)
    slots, sends, recvs = scratch[:count], scratch[count : 2 * count], scratch[2 * count : 3 * count]
    held = scratch[3 * count :]
    barrier = pltpu.get_barrier_semaphore()
    peers = 0
    for axes in stages:
        n, me, member = _group(axes)
        for k in range(1, n):
            pl.semaphore_signal(
                barrier, inc=1, device_id=member(lax.rem(me + k, n)), device_id_type=MESH
            )
        peers += n - 1
    pl.semaphore_wait(barrier, peers)
    value = x_ref
    for i, axes in enumerate(stages):
        n, me, member = _group(axes)
        copies = []
        for k in range(1, n):
            copy = pltpu.make_async_remote_copy(
                src_ref=value,
                dst_ref=slots[i].at[me],
                send_sem=sends[i].at[k - 1],
                recv_sem=recvs[i].at[k - 1],
                device_id=member(lax.rem(me + k, n)),
                device_id_type=MESH,
            )
            copy.start()
            copies.append(copy)
        slots[i][me] = value[...]
        for copy in copies:
            copy.wait()
        total = slots[i][0]
        for j in range(1, n):
            total = total + slots[i][j]
        if i + 1 < count:
            held[i][...] = total
            value = held[i]
        else:
            o_ref[...] = total

def small_sum(values, axes, cid):
    count = values.shape[0]
    rows = -(-count // 1024) * 8
    packed = jnp.pad(values, (0, rows * 128 - count)).reshape(rows, 128)
    stages = tuple(tuple(axis) if isinstance(axis, tuple) else (axis,) for axis in axes)
    sizes = [_group(axis)[0] for axis in stages]
    scratch = (
        [pltpu.VMEM((n, rows, 128), jnp.float32) for n in sizes]
        + [pltpu.SemaphoreType.DMA((n - 1,)) for n in sizes]
        + [pltpu.SemaphoreType.DMA((n - 1,)) for n in sizes]
        + [pltpu.VMEM((rows, 128), jnp.float32) for n in sizes[:-1]]
    )
    total = pl.pallas_call(
        functools.partial(_reduce_kernel, stages),
        out_shape=jax.ShapeDtypeStruct((rows, 128), jnp.float32),
        in_specs=[pl.BlockSpec(memory_space=pltpu.VMEM)],
        out_specs=pl.BlockSpec(memory_space=pltpu.VMEM),
        scratch_shapes=scratch,
        compiler_params=pltpu.CompilerParams(collective_id=cid, has_side_effects=True),
    )(packed)
    return total.reshape(-1)[:count]


def padded_2(block, sides, width):
    for axis, dim in sides:
        count = lax.axis_size(axis)
        forward = [(i, i + 1) for i in range(count - 1)]
        backward = [(target, source) for source, target in forward]
        low = lax.ppermute(
            lax.slice_in_dim(block, block.shape[dim] - width, None, axis=dim), axis, forward
        )
        high = lax.ppermute(lax.slice_in_dim(block, 0, width, axis=dim), axis, backward)
        block = jnp.concatenate([low, block, high], axis=dim)
    return block


def regional(labels, table):
    field = jnp.zeros(labels.shape, jnp.float32)
    for region in range(table.shape[0]):
        field = field + jnp.where(labels == region, table[region], 0.0)
    return field


def beside(padded):
    widths = [(0, 0)] * (padded.ndim - 1) + [(1, 1)]
    full = jnp.pad(padded, widths)
    return [
        full[..., 2:, 1:-1, 1:-1],
        full[..., :-2, 1:-1, 1:-1],
        full[..., 1:-1, 2:, 1:-1],
        full[..., 1:-1, :-2, 1:-1],
        full[..., 1:-1, 1:-1, 2:],
        full[..., 1:-1, 1:-1, :-2],
    ]


def around(field):
    widths = [(0, 0)] * (field.ndim - 3) + [(1, 1)] * 3
    full = jnp.pad(field, widths)
    return [
        full[..., 2:, 1:-1, 1:-1],
        full[..., :-2, 1:-1, 1:-1],
        full[..., 1:-1, 2:, 1:-1],
        full[..., 1:-1, :-2, 1:-1],
        full[..., 1:-1, 1:-1, 2:],
        full[..., 1:-1, 1:-1, :-2],
    ]


def chebyshev(rhs, apply_op):
    theta = 0.5 * (lam_high + lam_low)
    delta = 0.5 * (lam_high - lam_low)
    sigma = theta / delta
    rho = 1.0 / sigma
    solution = jnp.zeros_like(rhs)
    remain = rhs
    step_dir = rhs / theta
    for step in range(ITERS):
        solution = solution + step_dir
        if step + 1 < ITERS:
            remain = remain - apply_op(step_dir)
            rho_next = 1.0 / (2.0 * sigma - rho)
            step_dir = rho_next * rho * step_dir + 2.0 * rho_next / delta * remain
            rho = rho_next
    return solution


def per_device(
    labels,
    kappa_table,
    absorb_table,
    background,
    det_cells,
    v_kappa,
    v_absorb,
    q_kappa,
    q_absorb,
    beta_prev,
):
    sources, cx, cy, cz = background.shape
    n_src = lax.axis_size("src")
    slab = v_kappa.shape[2]
    pair = jnp.stack([v_kappa, v_absorb]).reshape(-1, 128)
    gathered = exchange(pair, "src", 0).reshape((n_src, 2, cx, cy, slab))
    full_k, full_a = jnp.transpose(gathered, (1, 2, 3, 0, 4)).reshape(2, cx, cy, cz)
    width = ITERS
    width_y = 8
    region_of = labels.astype(jnp.float32)[None]
    stacked = jnp.concatenate([background, region_of, full_k[None], full_a[None]], axis=0)
    wide = halo_block(stacked, width, width_y, 10)
    phi_w, region_w, vk_w, va_w = wide[:sources], wide[sources], wide[sources + 1], wide[sources + 2]
    wx = cx + 2 * width
    wy = cy + 2 * width_y
    gx_at = lax.axis_index("gx") * cx - width + jnp.arange(wx)
    gy_at = lax.axis_index("gy") * cy - width_y + jnp.arange(wy)
    inside = ((gx_at >= 0) & (gx_at < cx * lax.axis_size("gx")))[:, None, None] & (
        (gy_at >= 0) & (gy_at < cy * lax.axis_size("gy"))
    )[None, :, None]
    mask = inside.astype(jnp.float32)
    regions = kappa_table.shape[0]
    label_hot = (region_w.reshape(1, -1) == jnp.arange(regions, dtype=jnp.float32)[:, None]).astype(jnp.float32)
    tables = jnp.stack([kappa_table, absorb_table])
    fields = jnp.dot(tables, label_hot, precision=lax.Precision.HIGHEST).reshape(2, wx, wy, cz)
    kappa_w, absorb_w = mask * fields[0], mask * fields[1]
    kappa_faces = [mask * (0.5 * (kappa_w + near)) for near in around(kappa_w)]
    vk_faces = [mask * (0.5 * (vk_w + near)) for near in around(vk_w)]

    def apply_op(field):
        result = absorb_w * field
        for face, near in zip(kappa_faces, around(field)):
            result = result + face * (field - near)
        return result

    rhs = va_w * phi_w
    for face, near in zip(vk_faces, around(phi_w)):
        rhs = rhs + face * (phi_w - near)
    rhs = -rhs
    change = chebyshev(rhs, apply_op)[:, width : width + cx, width_y : width_y + cy, :]
    span_y = cy * lax.axis_size("gy")
    ix = det_cells // (span_y * cz)
    iy = det_cells // cz % span_y
    iz = det_cells % cz
    anchor_x = lax.axis_index("gx") * cx
    anchor_y = lax.axis_index("gy") * cy
    owned = (ix >= anchor_x) & (ix < anchor_x + cx) & (iy >= anchor_y) & (iy < anchor_y + cy)
    plane = (ix - anchor_x) * cy + (iy - anchor_y)
    plane_hot = (jnp.arange(cx * cy)[:, None] == plane[None, :]) & owned[None, :]
    depth_hot = (jnp.arange(cz)[:, None] == iz[None, :]).astype(jnp.float32)
    both = jnp.concatenate([change, background], axis=0).reshape(-1, cz)
    picked = jnp.dot(both, depth_hot, precision=lax.Precision.HIGHEST).reshape(2 * sources, cx * cy, -1)
    picked = jnp.sum(jnp.where(plane_hot[None], picked, 0.0), axis=1)
    picks = small_sum(picked.reshape(-1), ("gy", "gx"), 1).reshape(2 * sources, -1)
    seen, base = picks[:sources], picks[sources:]
    total = jnp.sum(base, axis=1, keepdims=True)
    mean_base = total / det_cells.shape[0]
    ratio = base / total
    jv_vals = (seen - ratio * jnp.sum(seen, axis=1, keepdims=True)) / mean_base
    weight = (jv_vals - jnp.sum(ratio * jv_vals, axis=1, keepdims=True)) / mean_base
    near_x = ix - (anchor_x - width)
    near_y = iy - (anchor_y - width_y)
    held = (near_x >= 0) & (near_x < wx) & (near_y >= 0) & (near_y < wy)
    wide_hot = (jnp.arange(wx * wy)[:, None] == (near_x * wy + near_y)[None, :]) & held[None, :]
    wide_hot = wide_hot.astype(jnp.float32)
    spread = (weight[:, :, None] * depth_hot.T[None]).transpose(1, 0, 2).reshape(det_cells.shape[0], -1)
    source_w = jnp.dot(wide_hot, spread, precision=lax.Precision.HIGHEST).reshape(wx * wy, sources, cz)
    source_w = source_w.transpose(1, 0, 2).reshape(sources, wx, wy, cz)
    dual_w = chebyshev(source_w, apply_op)
    ring = (slice(None), slice(width - 1, width + cx + 1), slice(width_y - 1, width_y + cy + 1))
    phi_near = beside(phi_w[ring])
    dual_near = beside(dual_w[ring])
    dual = dual_w[:, width : width + cx, width_y : width_y + cy, :]
    grad_a = -jnp.sum(background * dual, axis=0)
    grad_k = jnp.zeros_like(background[0])
    for near_phi, near_dual in zip(phi_near, dual_near):
        grad_k = grad_k - 0.5 * jnp.sum((background - near_phi) * (dual - near_dual), axis=0)
    grads = jnp.stack([grad_k, grad_a]).reshape(2, cx, cy, n_src, slab)
    grads = jnp.transpose(grads, (3, 0, 1, 2, 4)).reshape(n_src, -1, 128)
    hv = jnp.sum(exchange(grads, "src", 3, scatter=True), axis=0).reshape(2, cx, cy, slab)
    hv_k, hv_a = hv[0], hv[1]
    cell_count = cx * lax.axis_size("gx") * cy * lax.axis_size("gy") * cz
    w_k = hv_k - beta_prev[0] * q_kappa
    w_a = hv_a - beta_prev[0] * q_absorb
    local_wv = jnp.sum(w_k * v_kappa) + jnp.sum(w_a * v_absorb)
    local_vv = jnp.sum(v_kappa * v_kappa) + jnp.sum(v_absorb * v_absorb)
    wv_sum, vv_sum = small_sum(jnp.stack([local_wv, local_vv]), (("gx", "gy"), "src"), 4)
    alpha = wv_sum / cell_count / (vv_sum / cell_count + eps_norm)
    r_k = w_k - alpha * v_kappa
    r_a = w_a - alpha * v_absorb
    rr_sum = small_sum((jnp.sum(r_k * r_k) + jnp.sum(r_a * r_a))[None], (("gx", "gy"), "src"), 7)[0]
    beta = jnp.sqrt(rr_sum / cell_count + eps_norm)
    return (r_k / beta, r_a / beta, jnp.stack([alpha, beta]))


def solution(mesh):
    return jax.shard_map(
        per_device,
        mesh=mesh,
        in_specs=(
            P("gx", "gy", None),
            P(),
            P(),
            P("src", "gx", "gy", None),
            P(),
            P("gx", "gy", "src"),
            P("gx", "gy", "src"),
            P("gx", "gy", "src"),
            P("gx", "gy", "src"),
            P(),
        ),
        out_specs=(P("gx", "gy", "src"), P("gx", "gy", "src"), P()),
        check_vma=False,
    )
```

```python
import functools

import jax
import jax.numpy as jnp
from jax import lax
from jax.experimental import pallas as pl
from jax.experimental.pallas import tpu as pltpu
from jax.sharding import PartitionSpec as P

ITERS = 6
MESH = pl.DeviceIdType.MESH


lam_low = 0.02
lam_high = 24.1
eps_norm = 1e-06


def _exchange_kernel(axis, n, scatter, x_ref, o_ref, slots, send_sem, recv_sem, local_sem):
    me = lax.axis_index(axis)
    barrier = pltpu.get_barrier_semaphore()
    for k in range(1, n):
        peer = lax.rem(me + k, n)
        pl.semaphore_signal(barrier, inc=1, device_id={axis: peer}, device_id_type=MESH)
    pl.semaphore_wait(barrier, n - 1)
    copies = []
    for k in range(1, n):
        peer = lax.rem(me + k, n)
        copy = pltpu.make_async_remote_copy(
            src_ref=x_ref.at[peer] if scatter else x_ref,
            dst_ref=slots.at[me],
            send_sem=send_sem.at[k - 1],
            recv_sem=recv_sem.at[k - 1],
            device_id={axis: peer},
            device_id_type=MESH,
        )
        copy.start()
        copies.append(copy)
    local = pltpu.make_async_copy(x_ref.at[me] if scatter else x_ref, slots.at[me], local_sem)
    local.start()
    local.wait()
    for copy in copies:
        copy.wait()
    o_ref[...] = slots[...]


def exchange(x, axis, cid, scatter=False):
    n = lax.axis_size(axis)
    block = x.shape[1:] if scatter else x.shape
    return pl.pallas_call(
        functools.partial(_exchange_kernel, axis, n, scatter),
        out_shape=jax.ShapeDtypeStruct((n,) + block, x.dtype),
        in_specs=[pl.BlockSpec(memory_space=pltpu.VMEM)],
        out_specs=pl.BlockSpec(memory_space=pltpu.VMEM),
        scratch_shapes=[
            pltpu.VMEM((n,) + block, x.dtype),
            pltpu.SemaphoreType.DMA((n - 1,)),
            pltpu.SemaphoreType.DMA((n - 1,)),
            pltpu.SemaphoreType.DMA,
        ],
        compiler_params=pltpu.CompilerParams(collective_id=cid, has_side_effects=True),
    )(x)


def _halo_kernel(hx, hy, gather, *refs):
    if gather:
        x_ref, g_ref, o_ref, go_ref, wide, send_sem, recv_sem, local_sem = refs[:8]
        g_slots, g_send, g_recv, g_local = refs[8:]
    else:
        x_ref, o_ref, wide, send_sem, recv_sem, local_sem = refs
    fields, cx, cy, cz = x_ref.shape
    ax, ay = lax.axis_index("gx"), lax.axis_index("gy")
    nx, ny = lax.axis_size("gx"), lax.axis_size("gy")
    wide[...] = jnp.zeros_like(wide)
    steps = [(dx, dy) for dx in (-1, 0, 1) for dy in (-1, 0, 1) if (dx, dy) != (0, 0)]

    def exists(dx, dy):
        return (ax + dx >= 0) & (ax + dx < nx) & (ay + dy >= 0) & (ay + dy < ny)

    def window(d, block, halo):
        if d < 0:
            return pl.ds(0, halo), pl.ds(block + halo, halo)
        if d > 0:
            return pl.ds(block - halo, halo), pl.ds(0, halo)
        return pl.ds(0, block), pl.ds(halo, block)

    barrier = pltpu.get_barrier_semaphore()
    for dx, dy in steps:
        @pl.when(exists(dx, dy))
        def _():
            pl.semaphore_signal(
                barrier, inc=1, device_id={"gx": ax + dx, "gy": ay + dy}, device_id_type=MESH
            )
    across = 1 + (ax + nx - 1) // nx + (2 * nx - 2 - ax) // nx
    along = 1 + (ay + ny - 1) // ny + (2 * ny - 2 - ay) // ny
    if gather:
        n = lax.axis_size("src")
        me = lax.axis_index("src")
        for k in range(1, n):
            pl.semaphore_signal(
                barrier, inc=1, device_id={"src": lax.rem(me + k, n)}, device_id_type=MESH
            )
        pl.semaphore_wait(barrier, across * along - 1 + n - 1)
        pulls = []
        for k in range(1, n):
            pull = pltpu.make_async_remote_copy(
                src_ref=g_ref,
                dst_ref=g_slots.at[me],
                send_sem=g_send.at[k - 1],
                recv_sem=g_recv.at[k - 1],
                device_id={"src": lax.rem(me + k, n)},
                device_id_type=MESH,
            )
            pull.start()
            pulls.append(pull)
        own = pltpu.make_async_copy(g_ref, g_slots.at[me], g_local)
        own.start()
    else:
        pl.semaphore_wait(barrier, across * along - 1)

    local = pltpu.make_async_copy(
        x_ref, wide.at[:, pl.ds(hx, cx), pl.ds(hy, cy), :], local_sem
    )
    local.start()
    copies = []
    for k, (dx, dy) in enumerate(steps):
        src_x, dst_x = window(dx, cx, hx)
        src_y, dst_y = window(dy, cy, hy)
        tx = jnp.clip(ax + dx, 0, nx - 1)
        ty = jnp.clip(ay + dy, 0, ny - 1)
        copy = pltpu.make_async_remote_copy(
            src_ref=x_ref.at[:, src_x, src_y, :],
            dst_ref=wide.at[:, dst_x, dst_y, :],
            send_sem=send_sem.at[k],
            recv_sem=recv_sem.at[k],
            device_id={"gx": tx, "gy": ty},
            device_id_type=MESH,
        )
        copies.append(copy)

        @pl.when(exists(dx, dy))
        def _():
            copy.start()

    local.wait()
    for copy, (dx, dy) in zip(copies, steps):
        @pl.when(exists(dx, dy))
        def _():
            copy.wait_send()

        @pl.when(exists(-dx, -dy))
        def _():
            copy.wait_recv()

    if gather:
        own.wait()
        for pull in pulls:
            pull.wait()
        go_ref[...] = g_slots[...]
    o_ref[...] = wide[...]


def halo_block(x, hx, hy, cid, gather=None):
    fields, cx, cy, cz = x.shape
    shape = (fields, cx + 2 * hx, cy + 2 * hy, cz)
    vmem = pl.BlockSpec(memory_space=pltpu.VMEM)
    scratch = [
        pltpu.VMEM(shape, x.dtype),
        pltpu.SemaphoreType.DMA((8,)),
        pltpu.SemaphoreType.DMA((8,)),
        pltpu.SemaphoreType.DMA,
    ]
    operands = (x,)
    out_shape = jax.ShapeDtypeStruct(shape, x.dtype)
    out_specs = vmem
    if gather is not None:
        n = lax.axis_size("src")
        slots = (n,) + gather.shape
        scratch += [
            pltpu.VMEM(slots, gather.dtype),
            pltpu.SemaphoreType.DMA((n - 1,)),
            pltpu.SemaphoreType.DMA((n - 1,)),
            pltpu.SemaphoreType.DMA,
        ]
        operands = (x, gather)
        out_shape = (out_shape, jax.ShapeDtypeStruct(slots, gather.dtype))
        out_specs = (vmem, vmem)
    return pl.pallas_call(
        functools.partial(_halo_kernel, hx, hy, gather is not None),
        out_shape=out_shape,
        in_specs=[vmem] * len(operands),
        out_specs=out_specs,
        scratch_shapes=scratch,
        compiler_params=pltpu.CompilerParams(
            collective_id=cid, has_side_effects=True, vmem_limit_bytes=48 * 1024 * 1024
        ),
    )(*operands)


def _group(axes):
    sizes = [lax.axis_size(axis) for axis in axes]
    n = 1
    for size in sizes:
        n *= size
    me = 0
    for axis, size in zip(axes, sizes):
        me = me * size + lax.axis_index(axis)

    def member(index):
        ids = {}
        for axis, size in reversed(list(zip(axes, sizes))):
            ids[axis] = index % size
            index = index // size
        return ids

    return n, me, member


def _reduce_kernel(stages, x_ref, o_ref, *scratch):
    count = len(stages)
    slots, sends, recvs = scratch[:count], scratch[count : 2 * count], scratch[2 * count : 3 * count]
    held = scratch[3 * count :]
    barrier = pltpu.get_barrier_semaphore()
    peers = 0
    for axes in stages:
        n, me, member = _group(axes)
        for k in range(1, n):
            pl.semaphore_signal(
                barrier, inc=1, device_id=member(lax.rem(me + k, n)), device_id_type=MESH
            )
        peers += n - 1
    pl.semaphore_wait(barrier, peers)
    value = x_ref
    for i, axes in enumerate(stages):
        n, me, member = _group(axes)
        copies = []
        for k in range(1, n):
            copy = pltpu.make_async_remote_copy(
                src_ref=value,
                dst_ref=slots[i].at[me],
                send_sem=sends[i].at[k - 1],
                recv_sem=recvs[i].at[k - 1],
                device_id=member(lax.rem(me + k, n)),
                device_id_type=MESH,
            )
            copy.start()
            copies.append(copy)
        slots[i][me] = value[...]
        for copy in copies:
            copy.wait()
        total = slots[i][0]
        for j in range(1, n):
            total = total + slots[i][j]
        if i + 1 < count:
            held[i][...] = total
            value = held[i]
        else:
            o_ref[...] = total

def small_sum(values, axes, cid):
    count = values.shape[0]
    rows = -(-count // 1024) * 8
    packed = jnp.pad(values, (0, rows * 128 - count)).reshape(rows, 128)
    stages = tuple(tuple(axis) if isinstance(axis, tuple) else (axis,) for axis in axes)
    sizes = [_group(axis)[0] for axis in stages]
    scratch = (
        [pltpu.VMEM((n, rows, 128), jnp.float32) for n in sizes]
        + [pltpu.SemaphoreType.DMA((n - 1,)) for n in sizes]
        + [pltpu.SemaphoreType.DMA((n - 1,)) for n in sizes]
        + [pltpu.VMEM((rows, 128), jnp.float32) for n in sizes[:-1]]
    )
    total = pl.pallas_call(
        functools.partial(_reduce_kernel, stages),
        out_shape=jax.ShapeDtypeStruct((rows, 128), jnp.float32),
        in_specs=[pl.BlockSpec(memory_space=pltpu.VMEM)],
        out_specs=pl.BlockSpec(memory_space=pltpu.VMEM),
        scratch_shapes=scratch,
        compiler_params=pltpu.CompilerParams(collective_id=cid, has_side_effects=True),
    )(packed)
    return total.reshape(-1)[:count]


def padded_2(block, sides, width):
    for axis, dim in sides:
        count = lax.axis_size(axis)
        forward = [(i, i + 1) for i in range(count - 1)]
        backward = [(target, source) for source, target in forward]
        low = lax.ppermute(
            lax.slice_in_dim(block, block.shape[dim] - width, None, axis=dim), axis, forward
        )
        high = lax.ppermute(lax.slice_in_dim(block, 0, width, axis=dim), axis, backward)
        block = jnp.concatenate([low, block, high], axis=dim)
    return block


def regional(labels, table):
    field = jnp.zeros(labels.shape, jnp.float32)
    for region in range(table.shape[0]):
        field = field + jnp.where(labels == region, table[region], 0.0)
    return field


def beside(padded):
    widths = [(0, 0)] * (padded.ndim - 1) + [(1, 1)]
    full = jnp.pad(padded, widths)
    return [
        full[..., 2:, 1:-1, 1:-1],
        full[..., :-2, 1:-1, 1:-1],
        full[..., 1:-1, 2:, 1:-1],
        full[..., 1:-1, :-2, 1:-1],
        full[..., 1:-1, 1:-1, 2:],
        full[..., 1:-1, 1:-1, :-2],
    ]


def around(field):
    widths = [(0, 0)] * (field.ndim - 3) + [(1, 1)] * 3
    full = jnp.pad(field, widths)
    return [
        full[..., 2:, 1:-1, 1:-1],
        full[..., :-2, 1:-1, 1:-1],
        full[..., 1:-1, 2:, 1:-1],
        full[..., 1:-1, :-2, 1:-1],
        full[..., 1:-1, 1:-1, 2:],
        full[..., 1:-1, 1:-1, :-2],
    ]


def chebyshev(rhs, apply_op):
    theta = 0.5 * (lam_high + lam_low)
    delta = 0.5 * (lam_high - lam_low)
    sigma = theta / delta
    rho = 1.0 / sigma
    solution = jnp.zeros_like(rhs)
    remain = rhs
    step_dir = rhs / theta
    for step in range(ITERS):
        solution = solution + step_dir
        if step + 1 < ITERS:
            remain = remain - apply_op(step_dir)
            rho_next = 1.0 / (2.0 * sigma - rho)
            step_dir = rho_next * rho * step_dir + 2.0 * rho_next / delta * remain
            rho = rho_next
    return solution


def per_device(
    labels,
    kappa_table,
    absorb_table,
    background,
    det_cells,
    v_kappa,
    v_absorb,
    q_kappa,
    q_absorb,
    beta_prev,
):
    sources, cx, cy, cz = background.shape
    n_src = lax.axis_size("src")
    slab = v_kappa.shape[2]
    pair = jnp.stack([v_kappa, v_absorb]).reshape(-1, 128)
    width = ITERS
    width_y = 8
    region_of = labels.astype(jnp.float32)[None]
    stacked = jnp.concatenate([background, region_of], axis=0)
    wide, gathered = halo_block(stacked, width, width_y, 10, gather=pair)
    gathered = gathered.reshape((n_src, 2, cx, cy, slab))
    full_k, full_a = jnp.transpose(gathered, (1, 2, 3, 0, 4)).reshape(2, cx, cy, cz)
    wide_v = halo_block(jnp.stack([full_k, full_a]), width, width_y, 11)
    phi_w, region_w, vk_w, va_w = wide[:sources], wide[sources], wide_v[0], wide_v[1]
    wx = cx + 2 * width
    wy = cy + 2 * width_y
    gx_at = lax.axis_index("gx") * cx - width + jnp.arange(wx)
    gy_at = lax.axis_index("gy") * cy - width_y + jnp.arange(wy)
    inside = ((gx_at >= 0) & (gx_at < cx * lax.axis_size("gx")))[:, None, None] & (
        (gy_at >= 0) & (gy_at < cy * lax.axis_size("gy"))
    )[None, :, None]
    mask = inside.astype(jnp.float32)
    regions = kappa_table.shape[0]
    label_hot = (region_w.reshape(1, -1) == jnp.arange(regions, dtype=jnp.float32)[:, None]).astype(jnp.float32)
    tables = jnp.stack([kappa_table, absorb_table])
    fields = jnp.dot(tables, label_hot, precision=lax.Precision.HIGHEST).reshape(2, wx, wy, cz)
    kappa_w, absorb_w = mask * fields[0], mask * fields[1]
    kappa_faces = [mask * (0.5 * (kappa_w + near)) for near in around(kappa_w)]
    vk_faces = [mask * (0.5 * (vk_w + near)) for near in around(vk_w)]

    def apply_op(field):
        result = absorb_w * field
        for face, near in zip(kappa_faces, around(field)):
            result = result + face * (field - near)
        return result

    rhs = va_w * phi_w
    for face, near in zip(vk_faces, around(phi_w)):
        rhs = rhs + face * (phi_w - near)
    rhs = -rhs
    change = chebyshev(rhs, apply_op)[:, width : width + cx, width_y : width_y + cy, :]
    span_y = cy * lax.axis_size("gy")
    ix = det_cells // (span_y * cz)
    iy = det_cells // cz % span_y
    iz = det_cells % cz
    anchor_x = lax.axis_index("gx") * cx
    anchor_y = lax.axis_index("gy") * cy
    owned = (ix >= anchor_x) & (ix < anchor_x + cx) & (iy >= anchor_y) & (iy < anchor_y + cy)
    plane = (ix - anchor_x) * cy + (iy - anchor_y)
    plane_hot = (jnp.arange(cx * cy)[:, None] == plane[None, :]) & owned[None, :]
    depth_hot = (jnp.arange(cz)[:, None] == iz[None, :]).astype(jnp.float32)
    both = jnp.concatenate([change, background], axis=0).reshape(-1, cz)
    picked = jnp.dot(both, depth_hot, precision=lax.Precision.HIGHEST).reshape(2 * sources, cx * cy, -1)
    picked = jnp.sum(jnp.where(plane_hot[None], picked, 0.0), axis=1)
    picks = small_sum(picked.reshape(-1), ("gy", "gx"), 1).reshape(2 * sources, -1)
    seen, base = picks[:sources], picks[sources:]
    total = jnp.sum(base, axis=1, keepdims=True)
    mean_base = total / det_cells.shape[0]
    ratio = base / total
    jv_vals = (seen - ratio * jnp.sum(seen, axis=1, keepdims=True)) / mean_base
    weight = (jv_vals - jnp.sum(ratio * jv_vals, axis=1, keepdims=True)) / mean_base
    near_x = ix - (anchor_x - width)
    near_y = iy - (anchor_y - width_y)
    held = (near_x >= 0) & (near_x < wx) & (near_y >= 0) & (near_y < wy)
    wide_hot = (jnp.arange(wx * wy)[:, None] == (near_x * wy + near_y)[None, :]) & held[None, :]
    wide_hot = wide_hot.astype(jnp.float32)
    spread = (weight[:, :, None] * depth_hot.T[None]).transpose(1, 0, 2).reshape(det_cells.shape[0], -1)
    source_w = jnp.dot(wide_hot, spread, precision=lax.Precision.HIGHEST).reshape(wx * wy, sources, cz)
    source_w = source_w.transpose(1, 0, 2).reshape(sources, wx, wy, cz)
    dual_w = chebyshev(source_w, apply_op)
    ring = (slice(None), slice(width - 1, width + cx + 1), slice(width_y - 1, width_y + cy + 1))
    phi_near = beside(phi_w[ring])
    dual_near = beside(dual_w[ring])
    dual = dual_w[:, width : width + cx, width_y : width_y + cy, :]
    grad_a = -jnp.sum(background * dual, axis=0)
    grad_k = jnp.zeros_like(background[0])
    for near_phi, near_dual in zip(phi_near, dual_near):
        grad_k = grad_k - 0.5 * jnp.sum((background - near_phi) * (dual - near_dual), axis=0)
    grads = jnp.stack([grad_k, grad_a]).reshape(2, cx, cy, n_src, slab)
    grads = jnp.transpose(grads, (3, 0, 1, 2, 4)).reshape(n_src, -1, 128)
    hv = jnp.sum(exchange(grads, "src", 3, scatter=True), axis=0).reshape(2, cx, cy, slab)
    hv_k, hv_a = hv[0], hv[1]
    cell_count = cx * lax.axis_size("gx") * cy * lax.axis_size("gy") * cz
    w_k = hv_k - beta_prev[0] * q_kappa
    w_a = hv_a - beta_prev[0] * q_absorb
    local_wv = jnp.sum(w_k * v_kappa) + jnp.sum(w_a * v_absorb)
    local_vv = jnp.sum(v_kappa * v_kappa) + jnp.sum(v_absorb * v_absorb)
    wv_sum, vv_sum = small_sum(jnp.stack([local_wv, local_vv]), (("gx", "gy"), "src"), 4)
    alpha = wv_sum / cell_count / (vv_sum / cell_count + eps_norm)
    r_k = w_k - alpha * v_kappa
    r_a = w_a - alpha * v_absorb
    rr_sum = small_sum((jnp.sum(r_k * r_k) + jnp.sum(r_a * r_a))[None], (("gx", "gy"), "src"), 7)[0]
    beta = jnp.sqrt(rr_sum / cell_count + eps_norm)
    return (r_k / beta, r_a / beta, jnp.stack([alpha, beta]))


def solution(mesh):
    return jax.shard_map(
        per_device,
        mesh=mesh,
        in_specs=(
            P("gx", "gy", None),
            P(),
            P(),
            P("src", "gx", "gy", None),
            P(),
            P("gx", "gy", "src"),
            P("gx", "gy", "src"),
            P("gx", "gy", "src"),
            P("gx", "gy", "src"),
            P(),
        ),
        out_specs=(P("gx", "gy", "src"), P("gx", "gy", "src"), P()),
        check_vma=False,
    )
```

```python
import functools

import jax
import jax.numpy as jnp
from jax import lax
from jax.experimental import pallas as pl
from jax.experimental.pallas import tpu as pltpu
from jax.sharding import PartitionSpec as P

ITERS = 6
MESH = pl.DeviceIdType.MESH


lam_low = 0.02
lam_high = 24.1
eps_norm = 1e-06


def _exchange_kernel(axis, n, scatter, x_ref, o_ref, slots, send_sem, recv_sem, local_sem):
    me = lax.axis_index(axis)
    barrier = pltpu.get_barrier_semaphore()
    for k in range(1, n):
        peer = lax.rem(me + k, n)
        pl.semaphore_signal(barrier, inc=1, device_id={axis: peer}, device_id_type=MESH)
    pl.semaphore_wait(barrier, n - 1)
    copies = []
    for k in range(1, n):
        peer = lax.rem(me + k, n)
        copy = pltpu.make_async_remote_copy(
            src_ref=x_ref.at[peer] if scatter else x_ref,
            dst_ref=slots.at[me],
            send_sem=send_sem.at[k - 1],
            recv_sem=recv_sem.at[k - 1],
            device_id={axis: peer},
            device_id_type=MESH,
        )
        copy.start()
        copies.append(copy)
    local = pltpu.make_async_copy(x_ref.at[me] if scatter else x_ref, slots.at[me], local_sem)
    local.start()
    local.wait()
    for copy in copies:
        copy.wait()
    o_ref[...] = slots[...]


def exchange(x, axis, cid, scatter=False):
    n = lax.axis_size(axis)
    block = x.shape[1:] if scatter else x.shape
    return pl.pallas_call(
        functools.partial(_exchange_kernel, axis, n, scatter),
        out_shape=jax.ShapeDtypeStruct((n,) + block, x.dtype),
        in_specs=[pl.BlockSpec(memory_space=pltpu.VMEM)],
        out_specs=pl.BlockSpec(memory_space=pltpu.VMEM),
        scratch_shapes=[
            pltpu.VMEM((n,) + block, x.dtype),
            pltpu.SemaphoreType.DMA((n - 1,)),
            pltpu.SemaphoreType.DMA((n - 1,)),
            pltpu.SemaphoreType.DMA,
        ],
        compiler_params=pltpu.CompilerParams(collective_id=cid, has_side_effects=True),
    )(x)


def _halo_kernel(hx, hy, x_ref, o_ref, wide, send_sem, recv_sem, local_sem):
    fields, cx, cy, cz = x_ref.shape
    ax, ay = lax.axis_index("gx"), lax.axis_index("gy")
    nx, ny = lax.axis_size("gx"), lax.axis_size("gy")
    wide[...] = jnp.zeros_like(wide)
    steps = [(-1, 0), (1, 0), (0, -1), (0, 1), (-1, -1), (-1, 1), (1, -1), (1, 1)]

    def exists(dx, dy):
        return (ax + dx >= 0) & (ax + dx < nx) & (ay + dy >= 0) & (ay + dy < ny)

    def window(d, block, halo):
        if d < 0:
            return pl.ds(0, halo), pl.ds(block + halo, halo)
        if d > 0:
            return pl.ds(block - halo, halo), pl.ds(0, halo)
        return pl.ds(0, block), pl.ds(halo, block)

    barrier = pltpu.get_barrier_semaphore()
    for dx, dy in steps:
        @pl.when(exists(dx, dy))
        def _():
            pl.semaphore_signal(
                barrier, inc=1, device_id={"gx": ax + dx, "gy": ay + dy}, device_id_type=MESH
            )
    across = 1 + (ax + nx - 1) // nx + (2 * nx - 2 - ax) // nx
    along = 1 + (ay + ny - 1) // ny + (2 * ny - 2 - ay) // ny
    pl.semaphore_wait(barrier, across * along - 1)

    local = pltpu.make_async_copy(
        x_ref, wide.at[:, pl.ds(hx, cx), pl.ds(hy, cy), :], local_sem
    )
    local.start()
    copies = []
    for k, (dx, dy) in enumerate(steps):
        src_x, dst_x = window(dx, cx, hx)
        src_y, dst_y = window(dy, cy, hy)
        tx = jnp.clip(ax + dx, 0, nx - 1)
        ty = jnp.clip(ay + dy, 0, ny - 1)
        for f in range(fields):
            copy = pltpu.make_async_remote_copy(
                src_ref=x_ref.at[f, src_x, src_y, :],
                dst_ref=wide.at[f, dst_x, dst_y, :],
                send_sem=send_sem.at[k * fields + f],
                recv_sem=recv_sem.at[k * fields + f],
                device_id={"gx": tx, "gy": ty},
                device_id_type=MESH,
            )
            copies.append((copy, dx, dy))

            @pl.when(exists(dx, dy))
            def _():
                copy.start()

    local.wait()
    for copy, dx, dy in copies:
        @pl.when(exists(dx, dy))
        def _():
            copy.wait_send()

        @pl.when(exists(-dx, -dy))
        def _():
            copy.wait_recv()

    o_ref[...] = wide[...]


def halo_block(x, hx, hy, cid):
    fields, cx, cy, cz = x.shape
    shape = (fields, cx + 2 * hx, cy + 2 * hy, cz)
    return pl.pallas_call(
        functools.partial(_halo_kernel, hx, hy),
        out_shape=jax.ShapeDtypeStruct(shape, x.dtype),
        in_specs=[pl.BlockSpec(memory_space=pltpu.VMEM)],
        out_specs=pl.BlockSpec(memory_space=pltpu.VMEM),
        scratch_shapes=[
            pltpu.VMEM(shape, x.dtype),
            pltpu.SemaphoreType.DMA((8 * fields,)),
            pltpu.SemaphoreType.DMA((8 * fields,)),
            pltpu.SemaphoreType.DMA,
        ],
        compiler_params=pltpu.CompilerParams(
            collective_id=cid, has_side_effects=True, vmem_limit_bytes=48 * 1024 * 1024
        ),
    )(x)


def _group(axes):
    sizes = [lax.axis_size(axis) for axis in axes]
    n = 1
    for size in sizes:
        n *= size
    me = 0
    for axis, size in zip(axes, sizes):
        me = me * size + lax.axis_index(axis)

    def member(index):
        ids = {}
        for axis, size in reversed(list(zip(axes, sizes))):
            ids[axis] = index % size
            index = index // size
        return ids

    return n, me, member


def _reduce_kernel(stages, x_ref, o_ref, *scratch):
    count = len(stages)
    slots, sends, recvs = scratch[:count], scratch[count : 2 * count], scratch[2 * count : 3 * count]
    held = scratch[3 * count :]
    barrier = pltpu.get_barrier_semaphore()
    peers = 0
    for axes in stages:
        n, me, member = _group(axes)
        for k in range(1, n):
            pl.semaphore_signal(
                barrier, inc=1, device_id=member(lax.rem(me + k, n)), device_id_type=MESH
            )
        peers += n - 1
    pl.semaphore_wait(barrier, peers)
    value = x_ref
    for i, axes in enumerate(stages):
        n, me, member = _group(axes)
        copies = []
        for k in range(1, n):
            copy = pltpu.make_async_remote_copy(
                src_ref=value,
                dst_ref=slots[i].at[me],
                send_sem=sends[i].at[k - 1],
                recv_sem=recvs[i].at[k - 1],
                device_id=member(lax.rem(me + k, n)),
                device_id_type=MESH,
            )
            copy.start()
            copies.append(copy)
        slots[i][me] = value[...]
        for copy in copies:
            copy.wait()
        total = slots[i][0]
        for j in range(1, n):
            total = total + slots[i][j]
        if i + 1 < count:
            held[i][...] = total
            value = held[i]
        else:
            o_ref[...] = total

def small_sum(values, axes, cid):
    count = values.shape[0]
    rows = -(-count // 1024) * 8
    packed = jnp.pad(values, (0, rows * 128 - count)).reshape(rows, 128)
    stages = tuple(tuple(axis) if isinstance(axis, tuple) else (axis,) for axis in axes)
    sizes = [_group(axis)[0] for axis in stages]
    scratch = (
        [pltpu.VMEM((n, rows, 128), jnp.float32) for n in sizes]
        + [pltpu.SemaphoreType.DMA((n - 1,)) for n in sizes]
        + [pltpu.SemaphoreType.DMA((n - 1,)) for n in sizes]
        + [pltpu.VMEM((rows, 128), jnp.float32) for n in sizes[:-1]]
    )
    total = pl.pallas_call(
        functools.partial(_reduce_kernel, stages),
        out_shape=jax.ShapeDtypeStruct((rows, 128), jnp.float32),
        in_specs=[pl.BlockSpec(memory_space=pltpu.VMEM)],
        out_specs=pl.BlockSpec(memory_space=pltpu.VMEM),
        scratch_shapes=scratch,
        compiler_params=pltpu.CompilerParams(collective_id=cid, has_side_effects=True),
    )(packed)
    return total.reshape(-1)[:count]


def padded_2(block, sides, width):
    for axis, dim in sides:
        count = lax.axis_size(axis)
        forward = [(i, i + 1) for i in range(count - 1)]
        backward = [(target, source) for source, target in forward]
        low = lax.ppermute(
            lax.slice_in_dim(block, block.shape[dim] - width, None, axis=dim), axis, forward
        )
        high = lax.ppermute(lax.slice_in_dim(block, 0, width, axis=dim), axis, backward)
        block = jnp.concatenate([low, block, high], axis=dim)
    return block


def regional(labels, table):
    field = jnp.zeros(labels.shape, jnp.float32)
    for region in range(table.shape[0]):
        field = field + jnp.where(labels == region, table[region], 0.0)
    return field


def beside(padded):
    widths = [(0, 0)] * (padded.ndim - 1) + [(1, 1)]
    full = jnp.pad(padded, widths)
    return [
        full[..., 2:, 1:-1, 1:-1],
        full[..., :-2, 1:-1, 1:-1],
        full[..., 1:-1, 2:, 1:-1],
        full[..., 1:-1, :-2, 1:-1],
        full[..., 1:-1, 1:-1, 2:],
        full[..., 1:-1, 1:-1, :-2],
    ]


def around(field):
    widths = [(0, 0)] * (field.ndim - 3) + [(1, 1)] * 3
    full = jnp.pad(field, widths)
    return [
        full[..., 2:, 1:-1, 1:-1],
        full[..., :-2, 1:-1, 1:-1],
        full[..., 1:-1, 2:, 1:-1],
        full[..., 1:-1, :-2, 1:-1],
        full[..., 1:-1, 1:-1, 2:],
        full[..., 1:-1, 1:-1, :-2],
    ]


def chebyshev(rhs, apply_op):
    theta = 0.5 * (lam_high + lam_low)
    delta = 0.5 * (lam_high - lam_low)
    sigma = theta / delta
    rho = 1.0 / sigma
    solution = jnp.zeros_like(rhs)
    remain = rhs
    step_dir = rhs / theta
    for step in range(ITERS):
        solution = solution + step_dir
        if step + 1 < ITERS:
            remain = remain - apply_op(step_dir)
            rho_next = 1.0 / (2.0 * sigma - rho)
            step_dir = rho_next * rho * step_dir + 2.0 * rho_next / delta * remain
            rho = rho_next
    return solution


def per_device(
    labels,
    kappa_table,
    absorb_table,
    background,
    det_cells,
    v_kappa,
    v_absorb,
    q_kappa,
    q_absorb,
    beta_prev,
):
    sources, cx, cy, cz = background.shape
    n_src = lax.axis_size("src")
    slab = v_kappa.shape[2]
    pair = jnp.stack([v_kappa, v_absorb]).reshape(-1, 128)
    gathered = exchange(pair, "src", 0).reshape((n_src, 2, cx, cy, slab))
    full_k, full_a = jnp.transpose(gathered, (1, 2, 3, 0, 4)).reshape(2, cx, cy, cz)
    width = ITERS
    width_y = 8
    region_of = labels.astype(jnp.float32)[None]
    stacked = jnp.concatenate([background, region_of, full_k[None], full_a[None]], axis=0)
    wide = halo_block(stacked, width, width_y, 10)
    phi_w, region_w, vk_w, va_w = wide[:sources], wide[sources], wide[sources + 1], wide[sources + 2]
    wx = cx + 2 * width
    wy = cy + 2 * width_y
    gx_at = lax.axis_index("gx") * cx - width + jnp.arange(wx)
    gy_at = lax.axis_index("gy") * cy - width_y + jnp.arange(wy)
    inside = ((gx_at >= 0) & (gx_at < cx * lax.axis_size("gx")))[:, None, None] & (
        (gy_at >= 0) & (gy_at < cy * lax.axis_size("gy"))
    )[None, :, None]
    mask = inside.astype(jnp.float32)
    regions = kappa_table.shape[0]
    label_hot = (region_w.reshape(1, -1) == jnp.arange(regions, dtype=jnp.float32)[:, None]).astype(jnp.float32)
    tables = jnp.stack([kappa_table, absorb_table])
    fields = jnp.dot(tables, label_hot, precision=lax.Precision.HIGHEST).reshape(2, wx, wy, cz)
    kappa_w, absorb_w = mask * fields[0], mask * fields[1]
    kappa_faces = [mask * (0.5 * (kappa_w + near)) for near in around(kappa_w)]
    vk_faces = [mask * (0.5 * (vk_w + near)) for near in around(vk_w)]

    def apply_op(field):
        result = absorb_w * field
        for face, near in zip(kappa_faces, around(field)):
            result = result + face * (field - near)
        return result

    rhs = va_w * phi_w
    for face, near in zip(vk_faces, around(phi_w)):
        rhs = rhs + face * (phi_w - near)
    rhs = -rhs
    change = chebyshev(rhs, apply_op)[:, width : width + cx, width_y : width_y + cy, :]
    span_y = cy * lax.axis_size("gy")
    ix = det_cells // (span_y * cz)
    iy = det_cells // cz % span_y
    iz = det_cells % cz
    anchor_x = lax.axis_index("gx") * cx
    anchor_y = lax.axis_index("gy") * cy
    owned = (ix >= anchor_x) & (ix < anchor_x + cx) & (iy >= anchor_y) & (iy < anchor_y + cy)
    plane = (ix - anchor_x) * cy + (iy - anchor_y)
    plane_hot = (jnp.arange(cx * cy)[:, None] == plane[None, :]) & owned[None, :]
    depth_hot = (jnp.arange(cz)[:, None] == iz[None, :]).astype(jnp.float32)
    both = jnp.concatenate([change, background], axis=0).reshape(-1, cz)
    picked = jnp.dot(both, depth_hot, precision=lax.Precision.HIGHEST).reshape(2 * sources, cx * cy, -1)
    picked = jnp.sum(jnp.where(plane_hot[None], picked, 0.0), axis=1)
    picks = small_sum(picked.reshape(-1), ("gy", "gx"), 1).reshape(2 * sources, -1)
    seen, base = picks[:sources], picks[sources:]
    total = jnp.sum(base, axis=1, keepdims=True)
    mean_base = total / det_cells.shape[0]
    ratio = base / total
    jv_vals = (seen - ratio * jnp.sum(seen, axis=1, keepdims=True)) / mean_base
    weight = (jv_vals - jnp.sum(ratio * jv_vals, axis=1, keepdims=True)) / mean_base
    near_x = ix - (anchor_x - width)
    near_y = iy - (anchor_y - width_y)
    held = (near_x >= 0) & (near_x < wx) & (near_y >= 0) & (near_y < wy)
    wide_hot = (jnp.arange(wx * wy)[:, None] == (near_x * wy + near_y)[None, :]) & held[None, :]
    wide_hot = wide_hot.astype(jnp.float32)
    spread = (weight[:, :, None] * depth_hot.T[None]).transpose(1, 0, 2).reshape(det_cells.shape[0], -1)
    source_w = jnp.dot(wide_hot, spread, precision=lax.Precision.HIGHEST).reshape(wx * wy, sources, cz)
    source_w = source_w.transpose(1, 0, 2).reshape(sources, wx, wy, cz)
    dual_w = chebyshev(source_w, apply_op)
    ring = (slice(None), slice(width - 1, width + cx + 1), slice(width_y - 1, width_y + cy + 1))
    phi_near = beside(phi_w[ring])
    dual_near = beside(dual_w[ring])
    dual = dual_w[:, width : width + cx, width_y : width_y + cy, :]
    grad_a = -jnp.sum(background * dual, axis=0)
    grad_k = jnp.zeros_like(background[0])
    for near_phi, near_dual in zip(phi_near, dual_near):
        grad_k = grad_k - 0.5 * jnp.sum((background - near_phi) * (dual - near_dual), axis=0)
    grads = jnp.stack([grad_k, grad_a]).reshape(2, cx, cy, n_src, slab)
    grads = jnp.transpose(grads, (3, 0, 1, 2, 4)).reshape(n_src, -1, 128)
    hv = jnp.sum(exchange(grads, "src", 3, scatter=True), axis=0).reshape(2, cx, cy, slab)
    hv_k, hv_a = hv[0], hv[1]
    cell_count = cx * lax.axis_size("gx") * cy * lax.axis_size("gy") * cz
    w_k = hv_k - beta_prev[0] * q_kappa
    w_a = hv_a - beta_prev[0] * q_absorb
    local_wv = jnp.sum(w_k * v_kappa) + jnp.sum(w_a * v_absorb)
    local_vv = jnp.sum(v_kappa * v_kappa) + jnp.sum(v_absorb * v_absorb)
    wv_sum, vv_sum = small_sum(jnp.stack([local_wv, local_vv]), (("gx", "gy"), "src"), 4)
    alpha = wv_sum / cell_count / (vv_sum / cell_count + eps_norm)
    r_k = w_k - alpha * v_kappa
    r_a = w_a - alpha * v_absorb
    rr_sum = small_sum((jnp.sum(r_k * r_k) + jnp.sum(r_a * r_a))[None], (("gx", "gy"), "src"), 7)[0]
    beta = jnp.sqrt(rr_sum / cell_count + eps_norm)
    return (r_k / beta, r_a / beta, jnp.stack([alpha, beta]))


def solution(mesh):
    return jax.shard_map(
        per_device,
        mesh=mesh,
        in_specs=(
            P("gx", "gy", None),
            P(),
            P(),
            P("src", "gx", "gy", None),
            P(),
            P("gx", "gy", "src"),
            P("gx", "gy", "src"),
            P("gx", "gy", "src"),
            P("gx", "gy", "src"),
            P(),
        ),
        out_specs=(P("gx", "gy", "src"), P("gx", "gy", "src"), P()),
        check_vma=False,
    )
```

```python
import functools

import jax
import jax.numpy as jnp
from jax import lax
from jax.experimental import pallas as pl
from jax.experimental.pallas import tpu as pltpu
from jax.sharding import PartitionSpec as P

ITERS = 6
MESH = pl.DeviceIdType.MESH


lam_low = 0.02
lam_high = 24.1
eps_norm = 1e-06


def _exchange_kernel(axis, n, scatter, x_ref, o_ref, slots, send_sem, recv_sem, local_sem):
    me = lax.axis_index(axis)
    barrier = pltpu.get_barrier_semaphore()
    for k in range(1, n):
        peer = lax.rem(me + k, n)
        pl.semaphore_signal(barrier, inc=1, device_id={axis: peer}, device_id_type=MESH)
    pl.semaphore_wait(barrier, n - 1)
    copies = []
    for k in range(1, n):
        peer = lax.rem(me + k, n)
        copy = pltpu.make_async_remote_copy(
            src_ref=x_ref.at[peer] if scatter else x_ref,
            dst_ref=slots.at[me],
            send_sem=send_sem.at[k - 1],
            recv_sem=recv_sem.at[k - 1],
            device_id={axis: peer},
            device_id_type=MESH,
        )
        copy.start()
        copies.append(copy)
    local = pltpu.make_async_copy(x_ref.at[me] if scatter else x_ref, slots.at[me], local_sem)
    local.start()
    local.wait()
    for copy in copies:
        copy.wait()
    o_ref[...] = slots[...]


def exchange(x, axis, cid, scatter=False):
    n = lax.axis_size(axis)
    block = x.shape[1:] if scatter else x.shape
    return pl.pallas_call(
        functools.partial(_exchange_kernel, axis, n, scatter),
        out_shape=jax.ShapeDtypeStruct((n,) + block, x.dtype),
        in_specs=[pl.BlockSpec(memory_space=pltpu.VMEM)],
        out_specs=pl.BlockSpec(memory_space=pltpu.VMEM),
        scratch_shapes=[
            pltpu.VMEM((n,) + block, x.dtype),
            pltpu.SemaphoreType.DMA((n - 1,)),
            pltpu.SemaphoreType.DMA((n - 1,)),
            pltpu.SemaphoreType.DMA,
        ],
        compiler_params=pltpu.CompilerParams(collective_id=cid, has_side_effects=True),
    )(x)


def _halo_kernel(hx, hy, x_ref, o_ref, wide, send_sem, recv_sem, local_sem):
    fields, cx, cy, cz = x_ref.shape
    ax, ay = lax.axis_index("gx"), lax.axis_index("gy")
    nx, ny = lax.axis_size("gx"), lax.axis_size("gy")
    wide[...] = jnp.zeros_like(wide)
    steps = [(dx, dy) for dx in (-1, 0, 1) for dy in (-1, 0, 1) if (dx, dy) != (0, 0)]

    def exists(dx, dy):
        return (ax + dx >= 0) & (ax + dx < nx) & (ay + dy >= 0) & (ay + dy < ny)

    def window(d, block, halo):
        if d < 0:
            return pl.ds(0, halo), pl.ds(block + halo, halo)
        if d > 0:
            return pl.ds(block - halo, halo), pl.ds(0, halo)
        return pl.ds(0, block), pl.ds(halo, block)

    barrier = pltpu.get_barrier_semaphore()
    for dx, dy in steps:
        @pl.when(exists(dx, dy))
        def _():
            pl.semaphore_signal(
                barrier, inc=1, device_id={"gx": ax + dx, "gy": ay + dy}, device_id_type=MESH
            )
    across = 1 + (ax + nx - 1) // nx + (2 * nx - 2 - ax) // nx
    along = 1 + (ay + ny - 1) // ny + (2 * ny - 2 - ay) // ny
    pl.semaphore_wait(barrier, across * along - 1)

    local = pltpu.make_async_copy(
        x_ref, wide.at[:, pl.ds(hx, cx), pl.ds(hy, cy), :], local_sem
    )
    local.start()
    copies = []
    for k, (dx, dy) in enumerate(steps):
        src_x, dst_x = window(dx, cx, hx)
        src_y, dst_y = window(dy, cy, hy)
        tx = jnp.clip(ax + dx, 0, nx - 1)
        ty = jnp.clip(ay + dy, 0, ny - 1)
        copy = pltpu.make_async_remote_copy(
            src_ref=x_ref.at[:, src_x, src_y, :],
            dst_ref=wide.at[:, dst_x, dst_y, :],
            send_sem=send_sem.at[k],
            recv_sem=recv_sem.at[k],
            device_id={"gx": tx, "gy": ty},
            device_id_type=MESH,
        )
        copies.append(copy)

        @pl.when(exists(dx, dy))
        def _():
            copy.start()

    local.wait()
    for copy, (dx, dy) in zip(copies, steps):
        @pl.when(exists(dx, dy))
        def _():
            copy.wait_send()

        @pl.when(exists(-dx, -dy))
        def _():
            copy.wait_recv()

    o_ref[...] = wide[...]


def halo_block(x, hx, hy, cid):
    fields, cx, cy, cz = x.shape
    shape = (fields, cx + 2 * hx, cy + 2 * hy, cz)
    return pl.pallas_call(
        functools.partial(_halo_kernel, hx, hy),
        out_shape=jax.ShapeDtypeStruct(shape, x.dtype),
        in_specs=[pl.BlockSpec(memory_space=pltpu.VMEM)],
        out_specs=pl.BlockSpec(memory_space=pltpu.VMEM),
        scratch_shapes=[
            pltpu.VMEM(shape, x.dtype),
            pltpu.SemaphoreType.DMA((8,)),
            pltpu.SemaphoreType.DMA((8,)),
            pltpu.SemaphoreType.DMA,
        ],
        compiler_params=pltpu.CompilerParams(
            collective_id=cid, has_side_effects=True, vmem_limit_bytes=48 * 1024 * 1024
        ),
    )(x)


def _group(axes):
    sizes = [lax.axis_size(axis) for axis in axes]
    n = 1
    for size in sizes:
        n *= size
    me = 0
    for axis, size in zip(axes, sizes):
        me = me * size + lax.axis_index(axis)

    def member(index):
        ids = {}
        for axis, size in reversed(list(zip(axes, sizes))):
            ids[axis] = index % size
            index = index // size
        return ids

    return n, me, member


def _reduce_kernel(stages, x_ref, o_ref, *scratch):
    count = len(stages)
    slots, sends, recvs = scratch[:count], scratch[count : 2 * count], scratch[2 * count : 3 * count]
    held = scratch[3 * count :]
    barrier = pltpu.get_barrier_semaphore()
    peers = 0
    for axes in stages:
        n, me, member = _group(axes)
        for k in range(1, n):
            pl.semaphore_signal(
                barrier, inc=1, device_id=member(lax.rem(me + k, n)), device_id_type=MESH
            )
        peers += n - 1
    pl.semaphore_wait(barrier, peers)
    value = x_ref
    for i, axes in enumerate(stages):
        n, me, member = _group(axes)
        copies = []
        for k in range(1, n):
            copy = pltpu.make_async_remote_copy(
                src_ref=value,
                dst_ref=slots[i].at[me],
                send_sem=sends[i].at[k - 1],
                recv_sem=recvs[i].at[k - 1],
                device_id=member(lax.rem(me + k, n)),
                device_id_type=MESH,
            )
            copy.start()
            copies.append(copy)
        slots[i][me] = value[...]
        for copy in copies:
            copy.wait()
        total = slots[i][0]
        for j in range(1, n):
            total = total + slots[i][j]
        if i + 1 < count:
            held[i][...] = total
            value = held[i]
        else:
            o_ref[...] = total

def small_sum(values, axes, cid):
    count = values.shape[0]
    rows = -(-count // 1024) * 8
    packed = jnp.pad(values, (0, rows * 128 - count)).reshape(rows, 128)
    stages = tuple(tuple(axis) if isinstance(axis, tuple) else (axis,) for axis in axes)
    sizes = [_group(axis)[0] for axis in stages]
    scratch = (
        [pltpu.VMEM((n, rows, 128), jnp.float32) for n in sizes]
        + [pltpu.SemaphoreType.DMA((n - 1,)) for n in sizes]
        + [pltpu.SemaphoreType.DMA((n - 1,)) for n in sizes]
        + [pltpu.VMEM((rows, 128), jnp.float32) for n in sizes[:-1]]
    )
    total = pl.pallas_call(
        functools.partial(_reduce_kernel, stages),
        out_shape=jax.ShapeDtypeStruct((rows, 128), jnp.float32),
        in_specs=[pl.BlockSpec(memory_space=pltpu.VMEM)],
        out_specs=pl.BlockSpec(memory_space=pltpu.VMEM),
        scratch_shapes=scratch,
        compiler_params=pltpu.CompilerParams(collective_id=cid, has_side_effects=True),
    )(packed)
    return total.reshape(-1)[:count]


def padded_2(block, sides, width):
    for axis, dim in sides:
        count = lax.axis_size(axis)
        forward = [(i, i + 1) for i in range(count - 1)]
        backward = [(target, source) for source, target in forward]
        low = lax.ppermute(
            lax.slice_in_dim(block, block.shape[dim] - width, None, axis=dim), axis, forward
        )
        high = lax.ppermute(lax.slice_in_dim(block, 0, width, axis=dim), axis, backward)
        block = jnp.concatenate([low, block, high], axis=dim)
    return block


def regional(labels, table):
    field = jnp.zeros(labels.shape, jnp.float32)
    for region in range(table.shape[0]):
        field = field + jnp.where(labels == region, table[region], 0.0)
    return field


def beside(padded):
    widths = [(0, 0)] * (padded.ndim - 1) + [(1, 1)]
    full = jnp.pad(padded, widths)
    return [
        full[..., 2:, 1:-1, 1:-1],
        full[..., :-2, 1:-1, 1:-1],
        full[..., 1:-1, 2:, 1:-1],
        full[..., 1:-1, :-2, 1:-1],
        full[..., 1:-1, 1:-1, 2:],
        full[..., 1:-1, 1:-1, :-2],
    ]


def around(field):
    widths = [(0, 0)] * (field.ndim - 3) + [(1, 1)] * 3
    full = jnp.pad(field, widths)
    return [
        full[..., 2:, 1:-1, 1:-1],
        full[..., :-2, 1:-1, 1:-1],
        full[..., 1:-1, 2:, 1:-1],
        full[..., 1:-1, :-2, 1:-1],
        full[..., 1:-1, 1:-1, 2:],
        full[..., 1:-1, 1:-1, :-2],
    ]


def chebyshev(rhs, apply_op):
    theta = 0.5 * (lam_high + lam_low)
    delta = 0.5 * (lam_high - lam_low)
    sigma = theta / delta
    rho = 1.0 / sigma
    solution = jnp.zeros_like(rhs)
    remain = rhs
    step_dir = rhs / theta
    for step in range(ITERS):
        solution = solution + step_dir
        if step + 1 < ITERS:
            remain = remain - apply_op(step_dir)
            rho_next = 1.0 / (2.0 * sigma - rho)
            step_dir = rho_next * rho * step_dir + 2.0 * rho_next / delta * remain
            rho = rho_next
    return solution


def per_device(
    labels,
    kappa_table,
    absorb_table,
    background,
    det_cells,
    v_kappa,
    v_absorb,
    q_kappa,
    q_absorb,
    beta_prev,
):
    sources, cx, cy, cz = background.shape
    n_src = lax.axis_size("src")
    slab = v_kappa.shape[2]
    pair = jnp.stack([v_kappa, v_absorb]).reshape(-1, 128)
    gathered = exchange(pair, "src", 0).reshape((n_src, 2, cx, cy, slab))
    full_k, full_a = jnp.transpose(gathered, (1, 2, 3, 0, 4)).reshape(2, cx, cy, cz)
    width = ITERS
    width_y = 8
    region_of = labels.astype(jnp.float32)[None]
    stacked = jnp.concatenate([background, region_of, full_k[None], full_a[None]], axis=0)
    wide = halo_block(stacked, width, width_y, 10)
    phi_w, region_w, vk_w, va_w = wide[:sources], wide[sources], wide[sources + 1], wide[sources + 2]
    wx = cx + 2 * width
    wy = cy + 2 * width_y
    gx_at = lax.axis_index("gx") * cx - width + jnp.arange(wx)
    gy_at = lax.axis_index("gy") * cy - width_y + jnp.arange(wy)
    inside = ((gx_at >= 0) & (gx_at < cx * lax.axis_size("gx")))[:, None, None] & (
        (gy_at >= 0) & (gy_at < cy * lax.axis_size("gy"))
    )[None, :, None]
    mask = inside.astype(jnp.float32)
    regions = kappa_table.shape[0]
    label_hot = (region_w.reshape(1, -1) == jnp.arange(regions, dtype=jnp.float32)[:, None]).astype(jnp.float32)
    tables = jnp.stack([kappa_table, absorb_table])
    fields = jnp.dot(tables, label_hot, precision=lax.Precision.HIGHEST).reshape(2, wx, wy, cz)
    kappa_w, absorb_w = mask * fields[0], mask * fields[1]
    kappa_faces = [mask * (0.5 * (kappa_w + near)) for near in around(kappa_w)]
    vk_faces = [mask * (0.5 * (vk_w + near)) for near in around(vk_w)]

    def apply_op(field):
        result = absorb_w * field
        for face, near in zip(kappa_faces, around(field)):
            result = result + face * (field - near)
        return result

    rhs = va_w * phi_w
    for face, near in zip(vk_faces, around(phi_w)):
        rhs = rhs + face * (phi_w - near)
    rhs = -rhs
    change = chebyshev(rhs, apply_op)[:, width : width + cx, width_y : width_y + cy, :]
    span_y = cy * lax.axis_size("gy")
    ix = det_cells // (span_y * cz)
    iy = det_cells // cz % span_y
    iz = det_cells % cz
    anchor_x = lax.axis_index("gx") * cx
    anchor_y = lax.axis_index("gy") * cy
    owned = (ix >= anchor_x) & (ix < anchor_x + cx) & (iy >= anchor_y) & (iy < anchor_y + cy)
    plane = (ix - anchor_x) * cy + (iy - anchor_y)
    plane_hot = (jnp.arange(cx * cy)[:, None] == plane[None, :]) & owned[None, :]
    depth_hot = (jnp.arange(cz)[:, None] == iz[None, :]).astype(jnp.float32)
    both = jnp.concatenate([change, background], axis=0).reshape(2 * sources, cx * cy, cz)
    picked = jnp.einsum(
        "spz,pd->szd", both, plane_hot.astype(jnp.float32), precision=lax.Precision.HIGHEST
    )
    picked = jnp.sum(picked * depth_hot[None], axis=1)
    picks = small_sum(picked.reshape(-1), ("gy", "gx"), 1).reshape(2 * sources, -1)
    seen, base = picks[:sources], picks[sources:]
    total = jnp.sum(base, axis=1, keepdims=True)
    mean_base = total / det_cells.shape[0]
    ratio = base / total
    jv_vals = (seen - ratio * jnp.sum(seen, axis=1, keepdims=True)) / mean_base
    weight = (jv_vals - jnp.sum(ratio * jv_vals, axis=1, keepdims=True)) / mean_base
    near_x = ix - (anchor_x - width)
    near_y = iy - (anchor_y - width_y)
    held = (near_x >= 0) & (near_x < wx) & (near_y >= 0) & (near_y < wy)
    wide_hot = (jnp.arange(wx * wy)[:, None] == (near_x * wy + near_y)[None, :]) & held[None, :]
    wide_hot = wide_hot.astype(jnp.float32)
    spread = (weight[:, :, None] * depth_hot.T[None]).transpose(1, 0, 2).reshape(det_cells.shape[0], -1)
    source_w = jnp.dot(wide_hot, spread, precision=lax.Precision.HIGHEST).reshape(wx * wy, sources, cz)
    source_w = source_w.transpose(1, 0, 2).reshape(sources, wx, wy, cz)
    dual_w = chebyshev(source_w, apply_op)
    ring = (slice(None), slice(width - 1, width + cx + 1), slice(width_y - 1, width_y + cy + 1))
    phi_near = beside(phi_w[ring])
    dual_near = beside(dual_w[ring])
    dual = dual_w[:, width : width + cx, width_y : width_y + cy, :]
    grad_a = -jnp.sum(background * dual, axis=0)
    grad_k = jnp.zeros_like(background[0])
    for near_phi, near_dual in zip(phi_near, dual_near):
        grad_k = grad_k - 0.5 * jnp.sum((background - near_phi) * (dual - near_dual), axis=0)
    grads = jnp.stack([grad_k, grad_a]).reshape(2, cx, cy, n_src, slab)
    grads = jnp.transpose(grads, (3, 0, 1, 2, 4)).reshape(n_src, -1, 128)
    hv = jnp.sum(exchange(grads, "src", 3, scatter=True), axis=0).reshape(2, cx, cy, slab)
    hv_k, hv_a = hv[0], hv[1]
    cell_count = cx * lax.axis_size("gx") * cy * lax.axis_size("gy") * cz
    w_k = hv_k - beta_prev[0] * q_kappa
    w_a = hv_a - beta_prev[0] * q_absorb
    local_wv = jnp.sum(w_k * v_kappa) + jnp.sum(w_a * v_absorb)
    local_vv = jnp.sum(v_kappa * v_kappa) + jnp.sum(v_absorb * v_absorb)
    wv_sum, vv_sum = small_sum(jnp.stack([local_wv, local_vv]), (("gx", "gy"), "src"), 4)
    alpha = wv_sum / cell_count / (vv_sum / cell_count + eps_norm)
    r_k = w_k - alpha * v_kappa
    r_a = w_a - alpha * v_absorb
    rr_sum = small_sum((jnp.sum(r_k * r_k) + jnp.sum(r_a * r_a))[None], (("gx", "gy"), "src"), 7)[0]
    beta = jnp.sqrt(rr_sum / cell_count + eps_norm)
    return (r_k / beta, r_a / beta, jnp.stack([alpha, beta]))


def solution(mesh):
    return jax.shard_map(
        per_device,
        mesh=mesh,
        in_specs=(
            P("gx", "gy", None),
            P(),
            P(),
            P("src", "gx", "gy", None),
            P(),
            P("gx", "gy", "src"),
            P("gx", "gy", "src"),
            P("gx", "gy", "src"),
            P("gx", "gy", "src"),
            P(),
        ),
        out_specs=(P("gx", "gy", "src"), P("gx", "gy", "src"), P()),
        check_vma=False,
    )
```

```python
import functools

import jax
import jax.numpy as jnp
from jax import lax
from jax.experimental import pallas as pl
from jax.experimental.pallas import tpu as pltpu
from jax.sharding import PartitionSpec as P

ITERS = 6
MESH = pl.DeviceIdType.MESH


lam_low = 0.02
lam_high = 24.1
eps_norm = 1e-06


def _exchange_kernel(axis, n, scatter, x_ref, o_ref, slots, send_sem, recv_sem, local_sem):
    me = lax.axis_index(axis)
    barrier = pltpu.get_barrier_semaphore()
    for k in range(1, n):
        peer = lax.rem(me + k, n)
        pl.semaphore_signal(barrier, inc=1, device_id={axis: peer}, device_id_type=MESH)
    pl.semaphore_wait(barrier, n - 1)
    copies = []
    for k in range(1, n):
        peer = lax.rem(me + k, n)
        copy = pltpu.make_async_remote_copy(
            src_ref=x_ref.at[peer] if scatter else x_ref,
            dst_ref=slots.at[me],
            send_sem=send_sem.at[k - 1],
            recv_sem=recv_sem.at[k - 1],
            device_id={axis: peer},
            device_id_type=MESH,
        )
        copy.start()
        copies.append(copy)
    local = pltpu.make_async_copy(x_ref.at[me] if scatter else x_ref, slots.at[me], local_sem)
    local.start()
    local.wait()
    for copy in copies:
        copy.wait()
    o_ref[...] = slots[...]


def exchange(x, axis, cid, scatter=False):
    n = lax.axis_size(axis)
    block = x.shape[1:] if scatter else x.shape
    return pl.pallas_call(
        functools.partial(_exchange_kernel, axis, n, scatter),
        out_shape=jax.ShapeDtypeStruct((n,) + block, x.dtype),
        in_specs=[pl.BlockSpec(memory_space=pltpu.VMEM)],
        out_specs=pl.BlockSpec(memory_space=pltpu.VMEM),
        scratch_shapes=[
            pltpu.VMEM((n,) + block, x.dtype),
            pltpu.SemaphoreType.DMA((n - 1,)),
            pltpu.SemaphoreType.DMA((n - 1,)),
            pltpu.SemaphoreType.DMA,
        ],
        compiler_params=pltpu.CompilerParams(collective_id=cid, has_side_effects=True),
    )(x)


def _halo_kernel(hx, hy, x_ref, o_ref, wide, send_sem, recv_sem, local_sem):
    fields, cx, cy, cz = x_ref.shape
    ax, ay = lax.axis_index("gx"), lax.axis_index("gy")
    nx, ny = lax.axis_size("gx"), lax.axis_size("gy")
    wide[...] = jnp.zeros_like(wide)
    steps = [(dx, dy) for dx in (-1, 0, 1) for dy in (-1, 0, 1) if (dx, dy) != (0, 0)]

    def exists(dx, dy):
        return (ax + dx >= 0) & (ax + dx < nx) & (ay + dy >= 0) & (ay + dy < ny)

    def window(d, block, halo):
        if d < 0:
            return pl.ds(0, halo), pl.ds(block + halo, halo)
        if d > 0:
            return pl.ds(block - halo, halo), pl.ds(0, halo)
        return pl.ds(0, block), pl.ds(halo, block)

    barrier = pltpu.get_barrier_semaphore()
    for dx, dy in steps:
        @pl.when(exists(dx, dy))
        def _():
            pl.semaphore_signal(
                barrier, inc=1, device_id={"gx": ax + dx, "gy": ay + dy}, device_id_type=MESH
            )
    across = 1 + (ax + nx - 1) // nx + (2 * nx - 2 - ax) // nx
    along = 1 + (ay + ny - 1) // ny + (2 * ny - 2 - ay) // ny
    pl.semaphore_wait(barrier, across * along - 1)

    local = pltpu.make_async_copy(
        x_ref, wide.at[:, pl.ds(hx, cx), pl.ds(hy, cy), :], local_sem
    )
    local.start()
    copies = []
    for k, (dx, dy) in enumerate(steps):
        src_x, dst_x = window(dx, cx, hx)
        src_y, dst_y = window(dy, cy, hy)
        tx = jnp.clip(ax + dx, 0, nx - 1)
        ty = jnp.clip(ay + dy, 0, ny - 1)
        copy = pltpu.make_async_remote_copy(
            src_ref=x_ref.at[:, src_x, src_y, :],
            dst_ref=wide.at[:, dst_x, dst_y, :],
            send_sem=send_sem.at[k],
            recv_sem=recv_sem.at[k],
            device_id={"gx": tx, "gy": ty},
            device_id_type=MESH,
        )
        copies.append(copy)

        @pl.when(exists(dx, dy))
        def _():
            copy.start()

    local.wait()
    for copy, (dx, dy) in zip(copies, steps):
        @pl.when(exists(dx, dy))
        def _():
            copy.wait_send()

        @pl.when(exists(-dx, -dy))
        def _():
            copy.wait_recv()

    o_ref[...] = wide[...]


def halo_block(x, hx, hy, cid):
    fields, cx, cy, cz = x.shape
    shape = (fields, cx + 2 * hx, cy + 2 * hy, cz)
    return pl.pallas_call(
        functools.partial(_halo_kernel, hx, hy),
        out_shape=jax.ShapeDtypeStruct(shape, x.dtype),
        in_specs=[pl.BlockSpec(memory_space=pltpu.VMEM)],
        out_specs=pl.BlockSpec(memory_space=pltpu.VMEM),
        scratch_shapes=[
            pltpu.VMEM(shape, x.dtype),
            pltpu.SemaphoreType.DMA((8,)),
            pltpu.SemaphoreType.DMA((8,)),
            pltpu.SemaphoreType.DMA,
        ],
        compiler_params=pltpu.CompilerParams(
            collective_id=cid, has_side_effects=True, vmem_limit_bytes=48 * 1024 * 1024
        ),
    )(x)


def _group(axes):
    sizes = [lax.axis_size(axis) for axis in axes]
    n = 1
    for size in sizes:
        n *= size
    me = 0
    for axis, size in zip(axes, sizes):
        me = me * size + lax.axis_index(axis)

    def member(index):
        ids = {}
        for axis, size in reversed(list(zip(axes, sizes))):
            ids[axis] = index % size
            index = index // size
        return ids

    return n, me, member


def _reduce_kernel(stages, scatter, *refs):
    if scatter:
        g_ref, x_ref, h_ref, o_ref, g_slots, g_send, g_recv, g_local = refs[:8]
        scratch = refs[8:]
    else:
        x_ref, o_ref = refs[:2]
        scratch = refs[2:]
    count = len(stages)
    slots, sends, recvs = scratch[:count], scratch[count : 2 * count], scratch[2 * count : 3 * count]
    held = scratch[3 * count :]
    barrier = pltpu.get_barrier_semaphore()
    peers = 0
    for axes in stages:
        n, me, member = _group(axes)
        for k in range(1, n):
            pl.semaphore_signal(
                barrier, inc=1, device_id=member(lax.rem(me + k, n)), device_id_type=MESH
            )
        peers += n - 1
    pl.semaphore_wait(barrier, peers)
    if scatter:
        n = lax.axis_size("src")
        me = lax.axis_index("src")
        parts = []
        for k in range(1, n):
            peer = lax.rem(me + k, n)
            part = pltpu.make_async_remote_copy(
                src_ref=g_ref.at[peer],
                dst_ref=g_slots.at[me],
                send_sem=g_send.at[k - 1],
                recv_sem=g_recv.at[k - 1],
                device_id={"src": peer},
                device_id_type=MESH,
            )
            part.start()
            parts.append(part)
        own = pltpu.make_async_copy(g_ref.at[me], g_slots.at[me], g_local)
        own.start()
    value = x_ref
    for i, axes in enumerate(stages):
        n, me, member = _group(axes)
        copies = []
        for k in range(1, n):
            copy = pltpu.make_async_remote_copy(
                src_ref=value,
                dst_ref=slots[i].at[me],
                send_sem=sends[i].at[k - 1],
                recv_sem=recvs[i].at[k - 1],
                device_id=member(lax.rem(me + k, n)),
                device_id_type=MESH,
            )
            copy.start()
            copies.append(copy)
        slots[i][me] = value[...]
        for copy in copies:
            copy.wait()
        total = slots[i][0]
        for j in range(1, n):
            total = total + slots[i][j]
        if i + 1 < count:
            held[i][...] = total
            value = held[i]
        else:
            o_ref[...] = total
    if scatter:
        own.wait()
        for part in parts:
            part.wait()
        total = g_slots[0]
        for j in range(1, lax.axis_size("src")):
            total = total + g_slots[j]
        h_ref[...] = total

def small_sum(values, axes, cid, spread=None):
    count = values.shape[0]
    rows = -(-count // 1024) * 8
    packed = jnp.pad(values, (0, rows * 128 - count)).reshape(rows, 128)
    stages = tuple(tuple(axis) if isinstance(axis, tuple) else (axis,) for axis in axes)
    sizes = [_group(axis)[0] for axis in stages]
    scratch = (
        [pltpu.VMEM((n, rows, 128), jnp.float32) for n in sizes]
        + [pltpu.SemaphoreType.DMA((n - 1,)) for n in sizes]
        + [pltpu.SemaphoreType.DMA((n - 1,)) for n in sizes]
        + [pltpu.VMEM((rows, 128), jnp.float32) for n in sizes[:-1]]
    )
    vmem = pl.BlockSpec(memory_space=pltpu.VMEM)
    small = jax.ShapeDtypeStruct((rows, 128), jnp.float32)
    operands, out_shape, out_specs = (packed,), small, vmem
    if spread is not None:
        n = spread.shape[0]
        scratch = [
            pltpu.VMEM(spread.shape, jnp.float32),
            pltpu.SemaphoreType.DMA((n - 1,)),
            pltpu.SemaphoreType.DMA((n - 1,)),
            pltpu.SemaphoreType.DMA,
        ] + scratch
        operands = (spread, packed)
        out_shape = (jax.ShapeDtypeStruct(spread.shape[1:], jnp.float32), small)
        out_specs = (vmem, vmem)
    result = pl.pallas_call(
        functools.partial(_reduce_kernel, stages, spread is not None),
        out_shape=out_shape,
        in_specs=[vmem] * len(operands),
        out_specs=out_specs,
        scratch_shapes=scratch,
        compiler_params=pltpu.CompilerParams(collective_id=cid, has_side_effects=True),
    )(*operands)
    if spread is not None:
        return result[0], result[1].reshape(-1)[:count]
    return result.reshape(-1)[:count]


def padded_2(block, sides, width):
    for axis, dim in sides:
        count = lax.axis_size(axis)
        forward = [(i, i + 1) for i in range(count - 1)]
        backward = [(target, source) for source, target in forward]
        low = lax.ppermute(
            lax.slice_in_dim(block, block.shape[dim] - width, None, axis=dim), axis, forward
        )
        high = lax.ppermute(lax.slice_in_dim(block, 0, width, axis=dim), axis, backward)
        block = jnp.concatenate([low, block, high], axis=dim)
    return block


def regional(labels, table):
    field = jnp.zeros(labels.shape, jnp.float32)
    for region in range(table.shape[0]):
        field = field + jnp.where(labels == region, table[region], 0.0)
    return field


def beside(padded):
    widths = [(0, 0)] * (padded.ndim - 1) + [(1, 1)]
    full = jnp.pad(padded, widths)
    return [
        full[..., 2:, 1:-1, 1:-1],
        full[..., :-2, 1:-1, 1:-1],
        full[..., 1:-1, 2:, 1:-1],
        full[..., 1:-1, :-2, 1:-1],
        full[..., 1:-1, 1:-1, 2:],
        full[..., 1:-1, 1:-1, :-2],
    ]


def around(field):
    widths = [(0, 0)] * (field.ndim - 3) + [(1, 1)] * 3
    full = jnp.pad(field, widths)
    return [
        full[..., 2:, 1:-1, 1:-1],
        full[..., :-2, 1:-1, 1:-1],
        full[..., 1:-1, 2:, 1:-1],
        full[..., 1:-1, :-2, 1:-1],
        full[..., 1:-1, 1:-1, 2:],
        full[..., 1:-1, 1:-1, :-2],
    ]


def chebyshev(rhs, apply_op):
    theta = 0.5 * (lam_high + lam_low)
    delta = 0.5 * (lam_high - lam_low)
    sigma = theta / delta
    rho = 1.0 / sigma
    solution = jnp.zeros_like(rhs)
    remain = rhs
    step_dir = rhs / theta
    for step in range(ITERS):
        solution = solution + step_dir
        if step + 1 < ITERS:
            remain = remain - apply_op(step_dir)
            rho_next = 1.0 / (2.0 * sigma - rho)
            step_dir = rho_next * rho * step_dir + 2.0 * rho_next / delta * remain
            rho = rho_next
    return solution


def per_device(
    labels,
    kappa_table,
    absorb_table,
    background,
    det_cells,
    v_kappa,
    v_absorb,
    q_kappa,
    q_absorb,
    beta_prev,
):
    sources, cx, cy, cz = background.shape
    n_src = lax.axis_size("src")
    slab = v_kappa.shape[2]
    pair = jnp.stack([v_kappa, v_absorb]).reshape(-1, 128)
    gathered = exchange(pair, "src", 0).reshape((n_src, 2, cx, cy, slab))
    full_k, full_a = jnp.transpose(gathered, (1, 2, 3, 0, 4)).reshape(2, cx, cy, cz)
    width = ITERS
    width_y = 8
    region_of = labels.astype(jnp.float32)[None]
    stacked = jnp.concatenate([background, region_of, full_k[None], full_a[None]], axis=0)
    wide = halo_block(stacked, width, width_y, 10)
    phi_w, region_w, vk_w, va_w = wide[:sources], wide[sources], wide[sources + 1], wide[sources + 2]
    wx = cx + 2 * width
    wy = cy + 2 * width_y
    gx_at = lax.axis_index("gx") * cx - width + jnp.arange(wx)
    gy_at = lax.axis_index("gy") * cy - width_y + jnp.arange(wy)
    inside = ((gx_at >= 0) & (gx_at < cx * lax.axis_size("gx")))[:, None, None] & (
        (gy_at >= 0) & (gy_at < cy * lax.axis_size("gy"))
    )[None, :, None]
    mask = inside.astype(jnp.float32)
    regions = kappa_table.shape[0]
    label_hot = (region_w.reshape(1, -1) == jnp.arange(regions, dtype=jnp.float32)[:, None]).astype(jnp.float32)
    tables = jnp.stack([kappa_table, absorb_table])
    fields = jnp.dot(tables, label_hot, precision=lax.Precision.HIGHEST).reshape(2, wx, wy, cz)
    kappa_w, absorb_w = mask * fields[0], mask * fields[1]
    kappa_faces = [mask * (0.5 * (kappa_w + near)) for near in around(kappa_w)]
    vk_faces = [mask * (0.5 * (vk_w + near)) for near in around(vk_w)]

    def apply_op(field):
        result = absorb_w * field
        for face, near in zip(kappa_faces, around(field)):
            result = result + face * (field - near)
        return result

    rhs = va_w * phi_w
    for face, near in zip(vk_faces, around(phi_w)):
        rhs = rhs + face * (phi_w - near)
    rhs = -rhs
    change = chebyshev(rhs, apply_op)[:, width : width + cx, width_y : width_y + cy, :]
    span_y = cy * lax.axis_size("gy")
    ix = det_cells // (span_y * cz)
    iy = det_cells // cz % span_y
    iz = det_cells % cz
    anchor_x = lax.axis_index("gx") * cx
    anchor_y = lax.axis_index("gy") * cy
    owned = (ix >= anchor_x) & (ix < anchor_x + cx) & (iy >= anchor_y) & (iy < anchor_y + cy)
    plane = (ix - anchor_x) * cy + (iy - anchor_y)
    plane_hot = (jnp.arange(cx * cy)[:, None] == plane[None, :]) & owned[None, :]
    depth_hot = (jnp.arange(cz)[:, None] == iz[None, :]).astype(jnp.float32)
    both = jnp.concatenate([change, background], axis=0).reshape(2 * sources, cx * cy, cz)
    picked = jnp.einsum(
        "spz,pd->szd", both, plane_hot.astype(jnp.float32), precision=lax.Precision.HIGHEST
    )
    picked = jnp.sum(picked * depth_hot[None], axis=1)
    picks = small_sum(picked.reshape(-1), ("gy", "gx"), 1).reshape(2 * sources, -1)
    seen, base = picks[:sources], picks[sources:]
    total = jnp.sum(base, axis=1, keepdims=True)
    mean_base = total / det_cells.shape[0]
    ratio = base / total
    jv_vals = (seen - ratio * jnp.sum(seen, axis=1, keepdims=True)) / mean_base
    weight = (jv_vals - jnp.sum(ratio * jv_vals, axis=1, keepdims=True)) / mean_base
    near_x = ix - (anchor_x - width)
    near_y = iy - (anchor_y - width_y)
    held = (near_x >= 0) & (near_x < wx) & (near_y >= 0) & (near_y < wy)
    wide_hot = (jnp.arange(wx * wy)[:, None] == (near_x * wy + near_y)[None, :]) & held[None, :]
    wide_hot = wide_hot.astype(jnp.float32)
    spread = (weight[:, :, None] * depth_hot.T[None]).transpose(1, 0, 2).reshape(det_cells.shape[0], -1)
    source_w = jnp.dot(wide_hot, spread, precision=lax.Precision.HIGHEST).reshape(wx * wy, sources, cz)
    source_w = source_w.transpose(1, 0, 2).reshape(sources, wx, wy, cz)
    dual_w = chebyshev(source_w, apply_op)
    ring = (slice(None), slice(width - 1, width + cx + 1), slice(width_y - 1, width_y + cy + 1))
    phi_near = beside(phi_w[ring])
    dual_near = beside(dual_w[ring])
    dual = dual_w[:, width : width + cx, width_y : width_y + cy, :]
    grad_a = -jnp.sum(background * dual, axis=0)
    grad_k = jnp.zeros_like(background[0])
    for near_phi, near_dual in zip(phi_near, dual_near):
        grad_k = grad_k - 0.5 * jnp.sum((background - near_phi) * (dual - near_dual), axis=0)
    grads = jnp.stack([grad_k, grad_a]).reshape(2, cx, cy, n_src, slab)
    grads = jnp.transpose(grads, (3, 0, 1, 2, 4)).reshape(n_src, -1, 128)
    local_hv = jnp.sum(grad_k * full_k) + jnp.sum(grad_a * full_a)
    local_qv = jnp.sum(q_kappa * v_kappa) + jnp.sum(q_absorb * v_absorb)
    local_vv = jnp.sum(v_kappa * v_kappa) + jnp.sum(v_absorb * v_absorb)
    hv, dots = small_sum(
        jnp.stack([local_hv, local_qv, local_vv]), (("gx", "gy"), "src"), 3, spread=grads
    )
    hv = hv.reshape(2, cx, cy, slab)
    hv_k, hv_a = hv[0], hv[1]
    cell_count = cx * lax.axis_size("gx") * cy * lax.axis_size("gy") * cz
    w_k = hv_k - beta_prev[0] * q_kappa
    w_a = hv_a - beta_prev[0] * q_absorb
    wv_sum = dots[0] - beta_prev[0] * dots[1]
    vv_sum = dots[2]
    alpha = wv_sum / cell_count / (vv_sum / cell_count + eps_norm)
    r_k = w_k - alpha * v_kappa
    r_a = w_a - alpha * v_absorb
    rr_sum = small_sum((jnp.sum(r_k * r_k) + jnp.sum(r_a * r_a))[None], (("gx", "gy"), "src"), 7)[0]
    beta = jnp.sqrt(rr_sum / cell_count + eps_norm)
    return (r_k / beta, r_a / beta, jnp.stack([alpha, beta]))


def solution(mesh):
    return jax.shard_map(
        per_device,
        mesh=mesh,
        in_specs=(
            P("gx", "gy", None),
            P(),
            P(),
            P("src", "gx", "gy", None),
            P(),
            P("gx", "gy", "src"),
            P("gx", "gy", "src"),
            P("gx", "gy", "src"),
            P("gx", "gy", "src"),
            P(),
        ),
        out_specs=(P("gx", "gy", "src"), P("gx", "gy", "src"), P()),
        check_vma=False,
    )
```

```python
import functools

import jax
import jax.numpy as jnp
from jax import lax
from jax.experimental import pallas as pl
from jax.experimental.pallas import tpu as pltpu
from jax.sharding import PartitionSpec as P

ITERS = 6
MESH = pl.DeviceIdType.MESH


lam_low = 0.02
lam_high = 24.1
eps_norm = 1e-06


def _exchange_kernel(axis, n, scatter, x_ref, o_ref, slots, send_sem, recv_sem, local_sem):
    me = lax.axis_index(axis)
    barrier = pltpu.get_barrier_semaphore()
    for k in range(1, n):
        peer = lax.rem(me + k, n)
        pl.semaphore_signal(barrier, inc=1, device_id={axis: peer}, device_id_type=MESH)
    pl.semaphore_wait(barrier, n - 1)
    copies = []
    for k in range(1, n):
        peer = lax.rem(me + k, n)
        copy = pltpu.make_async_remote_copy(
            src_ref=x_ref.at[peer] if scatter else x_ref,
            dst_ref=slots.at[me],
            send_sem=send_sem.at[k - 1],
            recv_sem=recv_sem.at[k - 1],
            device_id={axis: peer},
            device_id_type=MESH,
        )
        copy.start()
        copies.append(copy)
    local = pltpu.make_async_copy(x_ref.at[me] if scatter else x_ref, slots.at[me], local_sem)
    local.start()
    local.wait()
    for copy in copies:
        copy.wait()
    o_ref[...] = slots[...]


def exchange(x, axis, cid, scatter=False):
    n = lax.axis_size(axis)
    block = x.shape[1:] if scatter else x.shape
    return pl.pallas_call(
        functools.partial(_exchange_kernel, axis, n, scatter),
        out_shape=jax.ShapeDtypeStruct((n,) + block, x.dtype),
        in_specs=[pl.BlockSpec(memory_space=pltpu.VMEM)],
        out_specs=pl.BlockSpec(memory_space=pltpu.VMEM),
        scratch_shapes=[
            pltpu.VMEM((n,) + block, x.dtype),
            pltpu.SemaphoreType.DMA((n - 1,)),
            pltpu.SemaphoreType.DMA((n - 1,)),
            pltpu.SemaphoreType.DMA,
        ],
        compiler_params=pltpu.CompilerParams(collective_id=cid, has_side_effects=True),
    )(x)


def _halo_kernel(hx, hy, own_fields, x_ref, o_ref, wide, send_sem, recv_sem, local_sem, fwd_send, fwd_recv):
    fields, cx, cy, cz = x_ref.shape
    ax, ay = lax.axis_index("gx"), lax.axis_index("gy")
    nx, ny = lax.axis_size("gx"), lax.axis_size("gy")
    me_src = lax.axis_index("src")
    half = me_src % 2
    partner = me_src + 1 - 2 * half
    wide[...] = jnp.zeros_like(wide)
    steps = [(-1, 0), (1, 0), (0, -1), (0, 1), (-1, -1), (-1, 1), (1, -1), (1, 1)]

    def exists(dx, dy):
        return (ax + dx >= 0) & (ax + dx < nx) & (ay + dy >= 0) & (ay + dy < ny)

    def window(d, block, halo):
        if d < 0:
            return pl.ds(0, halo), pl.ds(block + halo, halo)
        if d > 0:
            return pl.ds(block - halo, halo), pl.ds(0, halo)
        return pl.ds(0, block), pl.ds(halo, block)

    barrier = pltpu.get_barrier_semaphore()
    for dx, dy in steps:
        @pl.when(exists(dx, dy))
        def _():
            pl.semaphore_signal(
                barrier, inc=1, device_id={"gx": ax + dx, "gy": ay + dy}, device_id_type=MESH
            )
    pl.semaphore_signal(barrier, inc=1, device_id={"src": partner}, device_id_type=MESH)
    across = 1 + (ax + nx - 1) // nx + (2 * nx - 2 - ax) // nx
    along = 1 + (ay + ny - 1) // ny + (2 * ny - 2 - ay) // ny
    pl.semaphore_wait(barrier, across * along)

    local = pltpu.make_async_copy(
        x_ref, wide.at[:, pl.ds(hx, cx), pl.ds(hy, cy), :], local_sem
    )
    local.start()
    direct, relayed = [], []
    for k, (dx, dy) in enumerate(steps):
        src_x, dst_x = window(dx, cx, hx)
        src_y, dst_y = window(dy, cy, hy)
        tx = jnp.clip(ax + dx, 0, nx - 1)
        ty = jnp.clip(ay + dy, 0, ny - 1)
        for f in range(fields):
            slot = k * fields + f
            copy = pltpu.make_async_remote_copy(
                src_ref=x_ref.at[f, src_x, src_y, :],
                dst_ref=wide.at[f, dst_x, dst_y, :],
                send_sem=send_sem.at[slot],
                recv_sem=recv_sem.at[slot],
                device_id={"gx": tx, "gy": ty},
                device_id_type=MESH,
            )
            relay = None if f < own_fields else pltpu.make_async_remote_copy(
                src_ref=wide.at[f, dst_x, dst_y, :],
                dst_ref=wide.at[f, dst_x, dst_y, :],
                send_sem=fwd_send.at[slot],
                recv_sem=fwd_recv.at[slot],
                device_id={"src": partner},
                device_id_type=MESH,
            )
            mine = True if f < own_fields else ((f - own_fields) % 2 == half)
            direct.append((copy, relay, dx, dy, f, mine))

            @pl.when(exists(dx, dy) & mine)
            def _():
                copy.start()

    local.wait()
    for copy, relay, dx, dy, f, mine in direct:
        if f >= own_fields:
            @pl.when(exists(-dx, -dy) & mine)
            def _():
                copy.wait_recv()
                relay.start()
    for copy, relay, dx, dy, f, mine in direct:
        @pl.when(exists(dx, dy) & mine)
        def _():
            copy.wait_send()

        if f < own_fields:
            @pl.when(exists(-dx, -dy))
            def _():
                copy.wait_recv()
        else:
            @pl.when(exists(-dx, -dy) & mine)
            def _():
                relay.wait_send()

            @pl.when(exists(-dx, -dy) & jnp.logical_not(mine))
            def _():
                relay.wait_recv()

    o_ref[...] = wide[...]


def halo_block(x, hx, hy, cid, own_fields=None):
    fields, cx, cy, cz = x.shape
    own_fields = fields if own_fields is None else own_fields
    shape = (fields, cx + 2 * hx, cy + 2 * hy, cz)
    return pl.pallas_call(
        functools.partial(_halo_kernel, hx, hy, own_fields),
        out_shape=jax.ShapeDtypeStruct(shape, x.dtype),
        in_specs=[pl.BlockSpec(memory_space=pltpu.VMEM)],
        out_specs=pl.BlockSpec(memory_space=pltpu.VMEM),
        scratch_shapes=[
            pltpu.VMEM(shape, x.dtype),
            pltpu.SemaphoreType.DMA((8 * fields,)),
            pltpu.SemaphoreType.DMA((8 * fields,)),
            pltpu.SemaphoreType.DMA,
            pltpu.SemaphoreType.DMA((8 * fields,)),
            pltpu.SemaphoreType.DMA((8 * fields,)),
        ],
        compiler_params=pltpu.CompilerParams(
            collective_id=cid, has_side_effects=True, vmem_limit_bytes=48 * 1024 * 1024
        ),
    )(x)

def _group(axes):
    sizes = [lax.axis_size(axis) for axis in axes]
    n = 1
    for size in sizes:
        n *= size
    me = 0
    for axis, size in zip(axes, sizes):
        me = me * size + lax.axis_index(axis)

    def member(index):
        ids = {}
        for axis, size in reversed(list(zip(axes, sizes))):
            ids[axis] = index % size
            index = index // size
        return ids

    return n, me, member


def _reduce_kernel(stages, scatter, *refs):
    if scatter:
        g_ref, x_ref, h_ref, o_ref, g_slots, g_send, g_recv, g_local = refs[:8]
        scratch = refs[8:]
    else:
        x_ref, o_ref = refs[:2]
        scratch = refs[2:]
    count = len(stages)
    slots, sends, recvs = scratch[:count], scratch[count : 2 * count], scratch[2 * count : 3 * count]
    held = scratch[3 * count :]
    barrier = pltpu.get_barrier_semaphore()
    peers = 0
    for axes in stages:
        n, me, member = _group(axes)
        for k in range(1, n):
            pl.semaphore_signal(
                barrier, inc=1, device_id=member(lax.rem(me + k, n)), device_id_type=MESH
            )
        peers += n - 1
    pl.semaphore_wait(barrier, peers)
    if scatter:
        n = lax.axis_size("src")
        me = lax.axis_index("src")
        parts = []
        for k in range(1, n):
            peer = lax.rem(me + k, n)
            part = pltpu.make_async_remote_copy(
                src_ref=g_ref.at[peer],
                dst_ref=g_slots.at[me],
                send_sem=g_send.at[k - 1],
                recv_sem=g_recv.at[k - 1],
                device_id={"src": peer},
                device_id_type=MESH,
            )
            part.start()
            parts.append(part)
        own = pltpu.make_async_copy(g_ref.at[me], g_slots.at[me], g_local)
        own.start()
    value = x_ref
    for i, axes in enumerate(stages):
        n, me, member = _group(axes)
        copies = []
        for k in range(1, n):
            copy = pltpu.make_async_remote_copy(
                src_ref=value,
                dst_ref=slots[i].at[me],
                send_sem=sends[i].at[k - 1],
                recv_sem=recvs[i].at[k - 1],
                device_id=member(lax.rem(me + k, n)),
                device_id_type=MESH,
            )
            copy.start()
            copies.append(copy)
        slots[i][me] = value[...]
        for copy in copies:
            copy.wait()
        total = slots[i][0]
        for j in range(1, n):
            total = total + slots[i][j]
        if i + 1 < count:
            held[i][...] = total
            value = held[i]
        else:
            o_ref[...] = total
    if scatter:
        own.wait()
        for part in parts:
            part.wait()
        total = g_slots[0]
        for j in range(1, lax.axis_size("src")):
            total = total + g_slots[j]
        h_ref[...] = total

def small_sum(values, axes, cid, spread=None):
    count = values.shape[0]
    rows = -(-count // 1024) * 8
    packed = jnp.pad(values, (0, rows * 128 - count)).reshape(rows, 128)
    stages = tuple(tuple(axis) if isinstance(axis, tuple) else (axis,) for axis in axes)
    sizes = [_group(axis)[0] for axis in stages]
    scratch = (
        [pltpu.VMEM((n, rows, 128), jnp.float32) for n in sizes]
        + [pltpu.SemaphoreType.DMA((n - 1,)) for n in sizes]
        + [pltpu.SemaphoreType.DMA((n - 1,)) for n in sizes]
        + [pltpu.VMEM((rows, 128), jnp.float32) for n in sizes[:-1]]
    )
    vmem = pl.BlockSpec(memory_space=pltpu.VMEM)
    small = jax.ShapeDtypeStruct((rows, 128), jnp.float32)
    operands, out_shape, out_specs = (packed,), small, vmem
    if spread is not None:
        n = spread.shape[0]
        scratch = [
            pltpu.VMEM(spread.shape, jnp.float32),
            pltpu.SemaphoreType.DMA((n - 1,)),
            pltpu.SemaphoreType.DMA((n - 1,)),
            pltpu.SemaphoreType.DMA,
        ] + scratch
        operands = (spread, packed)
        out_shape = (jax.ShapeDtypeStruct(spread.shape[1:], jnp.float32), small)
        out_specs = (vmem, vmem)
    result = pl.pallas_call(
        functools.partial(_reduce_kernel, stages, spread is not None),
        out_shape=out_shape,
        in_specs=[vmem] * len(operands),
        out_specs=out_specs,
        scratch_shapes=scratch,
        compiler_params=pltpu.CompilerParams(collective_id=cid, has_side_effects=True),
    )(*operands)
    if spread is not None:
        return result[0], result[1].reshape(-1)[:count]
    return result.reshape(-1)[:count]


def padded_2(block, sides, width):
    for axis, dim in sides:
        count = lax.axis_size(axis)
        forward = [(i, i + 1) for i in range(count - 1)]
        backward = [(target, source) for source, target in forward]
        low = lax.ppermute(
            lax.slice_in_dim(block, block.shape[dim] - width, None, axis=dim), axis, forward
        )
        high = lax.ppermute(lax.slice_in_dim(block, 0, width, axis=dim), axis, backward)
        block = jnp.concatenate([low, block, high], axis=dim)
    return block


def regional(labels, table):
    field = jnp.zeros(labels.shape, jnp.float32)
    for region in range(table.shape[0]):
        field = field + jnp.where(labels == region, table[region], 0.0)
    return field


def beside(padded):
    widths = [(0, 0)] * (padded.ndim - 1) + [(1, 1)]
    full = jnp.pad(padded, widths)
    return [
        full[..., 2:, 1:-1, 1:-1],
        full[..., :-2, 1:-1, 1:-1],
        full[..., 1:-1, 2:, 1:-1],
        full[..., 1:-1, :-2, 1:-1],
        full[..., 1:-1, 1:-1, 2:],
        full[..., 1:-1, 1:-1, :-2],
    ]


def around(field):
    widths = [(0, 0)] * (field.ndim - 3) + [(1, 1)] * 3
    full = jnp.pad(field, widths)
    return [
        full[..., 2:, 1:-1, 1:-1],
        full[..., :-2, 1:-1, 1:-1],
        full[..., 1:-1, 2:, 1:-1],
        full[..., 1:-1, :-2, 1:-1],
        full[..., 1:-1, 1:-1, 2:],
        full[..., 1:-1, 1:-1, :-2],
    ]


def chebyshev(rhs, apply_op):
    theta = 0.5 * (lam_high + lam_low)
    delta = 0.5 * (lam_high - lam_low)
    sigma = theta / delta
    rho = 1.0 / sigma
    solution = jnp.zeros_like(rhs)
    remain = rhs
    step_dir = rhs / theta
    for step in range(ITERS):
        solution = solution + step_dir
        if step + 1 < ITERS:
            remain = remain - apply_op(step_dir)
            rho_next = 1.0 / (2.0 * sigma - rho)
            step_dir = rho_next * rho * step_dir + 2.0 * rho_next / delta * remain
            rho = rho_next
    return solution


def per_device(
    labels,
    kappa_table,
    absorb_table,
    background,
    det_cells,
    v_kappa,
    v_absorb,
    q_kappa,
    q_absorb,
    beta_prev,
):
    sources, cx, cy, cz = background.shape
    n_src = lax.axis_size("src")
    slab = v_kappa.shape[2]
    pair = jnp.stack([v_kappa, v_absorb]).reshape(-1, 128)
    gathered = exchange(pair, "src", 0).reshape((n_src, 2, cx, cy, slab))
    full_k, full_a = jnp.transpose(gathered, (1, 2, 3, 0, 4)).reshape(2, cx, cy, cz)
    width = ITERS
    width_y = 8
    region_of = labels.astype(jnp.float32)[None]
    stacked = jnp.concatenate([background, region_of, full_k[None], full_a[None]], axis=0)
    wide = halo_block(stacked, width, width_y, 10, own_fields=sources)
    phi_w, region_w, vk_w, va_w = wide[:sources], wide[sources], wide[sources + 1], wide[sources + 2]
    wx = cx + 2 * width
    wy = cy + 2 * width_y
    gx_at = lax.axis_index("gx") * cx - width + jnp.arange(wx)
    gy_at = lax.axis_index("gy") * cy - width_y + jnp.arange(wy)
    inside = ((gx_at >= 0) & (gx_at < cx * lax.axis_size("gx")))[:, None, None] & (
        (gy_at >= 0) & (gy_at < cy * lax.axis_size("gy"))
    )[None, :, None]
    mask = inside.astype(jnp.float32)
    regions = kappa_table.shape[0]
    label_hot = (region_w.reshape(1, -1) == jnp.arange(regions, dtype=jnp.float32)[:, None]).astype(jnp.float32)
    tables = jnp.stack([kappa_table, absorb_table])
    fields = jnp.dot(tables, label_hot, precision=lax.Precision.HIGHEST).reshape(2, wx, wy, cz)
    kappa_w, absorb_w = mask * fields[0], mask * fields[1]
    kappa_faces = [mask * (0.5 * (kappa_w + near)) for near in around(kappa_w)]
    vk_faces = [mask * (0.5 * (vk_w + near)) for near in around(vk_w)]

    def apply_op(field):
        result = absorb_w * field
        for face, near in zip(kappa_faces, around(field)):
            result = result + face * (field - near)
        return result

    rhs = va_w * phi_w
    for face, near in zip(vk_faces, around(phi_w)):
        rhs = rhs + face * (phi_w - near)
    rhs = -rhs
    change = chebyshev(rhs, apply_op)[:, width : width + cx, width_y : width_y + cy, :]
    span_y = cy * lax.axis_size("gy")
    ix = det_cells // (span_y * cz)
    iy = det_cells // cz % span_y
    iz = det_cells % cz
    anchor_x = lax.axis_index("gx") * cx
    anchor_y = lax.axis_index("gy") * cy
    owned = (ix >= anchor_x) & (ix < anchor_x + cx) & (iy >= anchor_y) & (iy < anchor_y + cy)
    plane = (ix - anchor_x) * cy + (iy - anchor_y)
    plane_hot = (jnp.arange(cx * cy)[:, None] == plane[None, :]) & owned[None, :]
    depth_hot = (jnp.arange(cz)[:, None] == iz[None, :]).astype(jnp.float32)
    both = jnp.concatenate([change, background], axis=0).reshape(2 * sources, cx * cy, cz)
    picked = jnp.einsum(
        "spz,pd->szd", both, plane_hot.astype(jnp.float32), precision=lax.Precision.HIGHEST
    )
    picked = jnp.sum(picked * depth_hot[None], axis=1)
    picks = small_sum(picked.reshape(-1), ("gy", "gx"), 1).reshape(2 * sources, -1)
    seen, base = picks[:sources], picks[sources:]
    total = jnp.sum(base, axis=1, keepdims=True)
    mean_base = total / det_cells.shape[0]
    ratio = base / total
    jv_vals = (seen - ratio * jnp.sum(seen, axis=1, keepdims=True)) / mean_base
    weight = (jv_vals - jnp.sum(ratio * jv_vals, axis=1, keepdims=True)) / mean_base
    near_x = ix - (anchor_x - width)
    near_y = iy - (anchor_y - width_y)
    held = (near_x >= 0) & (near_x < wx) & (near_y >= 0) & (near_y < wy)
    wide_hot = (jnp.arange(wx * wy)[:, None] == (near_x * wy + near_y)[None, :]) & held[None, :]
    wide_hot = wide_hot.astype(jnp.float32)
    spread = (weight[:, :, None] * depth_hot.T[None]).transpose(1, 0, 2).reshape(det_cells.shape[0], -1)
    source_w = jnp.dot(wide_hot, spread, precision=lax.Precision.HIGHEST).reshape(wx * wy, sources, cz)
    source_w = source_w.transpose(1, 0, 2).reshape(sources, wx, wy, cz)
    dual_w = chebyshev(source_w, apply_op)
    ring = (slice(None), slice(width - 1, width + cx + 1), slice(width_y - 1, width_y + cy + 1))
    phi_near = beside(phi_w[ring])
    dual_near = beside(dual_w[ring])
    dual = dual_w[:, width : width + cx, width_y : width_y + cy, :]
    grad_a = -jnp.sum(background * dual, axis=0)
    grad_k = jnp.zeros_like(background[0])
    for near_phi, near_dual in zip(phi_near, dual_near):
        grad_k = grad_k - 0.5 * jnp.sum((background - near_phi) * (dual - near_dual), axis=0)
    grads = jnp.stack([grad_k, grad_a]).reshape(2, cx, cy, n_src, slab)
    grads = jnp.transpose(grads, (3, 0, 1, 2, 4)).reshape(n_src, -1, 128)
    local_hv = jnp.sum(grad_k * full_k) + jnp.sum(grad_a * full_a)
    local_qv = jnp.sum(q_kappa * v_kappa) + jnp.sum(q_absorb * v_absorb)
    local_vv = jnp.sum(v_kappa * v_kappa) + jnp.sum(v_absorb * v_absorb)
    hv, dots = small_sum(
        jnp.stack([local_hv, local_qv, local_vv]), (("gx", "gy"), "src"), 3, spread=grads
    )
    hv = hv.reshape(2, cx, cy, slab)
    hv_k, hv_a = hv[0], hv[1]
    cell_count = cx * lax.axis_size("gx") * cy * lax.axis_size("gy") * cz
    w_k = hv_k - beta_prev[0] * q_kappa
    w_a = hv_a - beta_prev[0] * q_absorb
    wv_sum = dots[0] - beta_prev[0] * dots[1]
    vv_sum = dots[2]
    alpha = wv_sum / cell_count / (vv_sum / cell_count + eps_norm)
    r_k = w_k - alpha * v_kappa
    r_a = w_a - alpha * v_absorb
    rr_sum = small_sum((jnp.sum(r_k * r_k) + jnp.sum(r_a * r_a))[None], (("gx", "gy"), "src"), 7)[0]
    beta = jnp.sqrt(rr_sum / cell_count + eps_norm)
    return (r_k / beta, r_a / beta, jnp.stack([alpha, beta]))


def solution(mesh):
    return jax.shard_map(
        per_device,
        mesh=mesh,
        in_specs=(
            P("gx", "gy", None),
            P(),
            P(),
            P("src", "gx", "gy", None),
            P(),
            P("gx", "gy", "src"),
            P("gx", "gy", "src"),
            P("gx", "gy", "src"),
            P("gx", "gy", "src"),
            P(),
        ),
        out_specs=(P("gx", "gy", "src"), P("gx", "gy", "src"), P()),
        check_vma=False,
    )
```

```python
import functools

import jax
import jax.numpy as jnp
from jax import lax
from jax.experimental import pallas as pl
from jax.experimental.pallas import tpu as pltpu
from jax.sharding import PartitionSpec as P

ITERS = 6
MESH = pl.DeviceIdType.MESH


lam_low = 0.02
lam_high = 24.1
eps_norm = 1e-06


def _exchange_kernel(axis, n, scatter, x_ref, o_ref, slots, send_sem, recv_sem, local_sem):
    me = lax.axis_index(axis)
    barrier = pltpu.get_barrier_semaphore()
    for k in range(1, n):
        peer = lax.rem(me + k, n)
        pl.semaphore_signal(barrier, inc=1, device_id={axis: peer}, device_id_type=MESH)
    pl.semaphore_wait(barrier, n - 1)
    copies = []
    for k in range(1, n):
        peer = lax.rem(me + k, n)
        copy = pltpu.make_async_remote_copy(
            src_ref=x_ref.at[peer] if scatter else x_ref,
            dst_ref=slots.at[me],
            send_sem=send_sem.at[k - 1],
            recv_sem=recv_sem.at[k - 1],
            device_id={axis: peer},
            device_id_type=MESH,
        )
        copy.start()
        copies.append(copy)
    local = pltpu.make_async_copy(x_ref.at[me] if scatter else x_ref, slots.at[me], local_sem)
    local.start()
    local.wait()
    for copy in copies:
        copy.wait()
    o_ref[...] = slots[...]


def exchange(x, axis, cid, scatter=False):
    n = lax.axis_size(axis)
    block = x.shape[1:] if scatter else x.shape
    return pl.pallas_call(
        functools.partial(_exchange_kernel, axis, n, scatter),
        out_shape=jax.ShapeDtypeStruct((n,) + block, x.dtype),
        in_specs=[pl.BlockSpec(memory_space=pltpu.VMEM)],
        out_specs=pl.BlockSpec(memory_space=pltpu.VMEM),
        scratch_shapes=[
            pltpu.VMEM((n,) + block, x.dtype),
            pltpu.SemaphoreType.DMA((n - 1,)),
            pltpu.SemaphoreType.DMA((n - 1,)),
            pltpu.SemaphoreType.DMA,
        ],
        compiler_params=pltpu.CompilerParams(collective_id=cid, has_side_effects=True),
    )(x)


def _halo_kernel(hx, hy, own_fields, x_ref, o_ref, wide, send_sem, recv_sem, local_sem, fwd_send, fwd_recv):
    fields, cx, cy, cz = x_ref.shape
    ax, ay = lax.axis_index("gx"), lax.axis_index("gy")
    nx, ny = lax.axis_size("gx"), lax.axis_size("gy")
    me_src = lax.axis_index("src")
    half = me_src % 2
    partner = me_src + 1 - 2 * half
    wide[...] = jnp.zeros_like(wide)
    steps = [(-1, 0), (1, 0), (0, -1), (0, 1), (-1, -1), (-1, 1), (1, -1), (1, 1)]

    def exists(dx, dy):
        return (ax + dx >= 0) & (ax + dx < nx) & (ay + dy >= 0) & (ay + dy < ny)

    def window(d, block, halo):
        if d < 0:
            return pl.ds(0, halo), pl.ds(block + halo, halo)
        if d > 0:
            return pl.ds(block - halo, halo), pl.ds(0, halo)
        return pl.ds(0, block), pl.ds(halo, block)

    barrier = pltpu.get_barrier_semaphore()
    for dx, dy in steps:
        @pl.when(exists(dx, dy))
        def _():
            pl.semaphore_signal(
                barrier, inc=1, device_id={"gx": ax + dx, "gy": ay + dy}, device_id_type=MESH
            )
    pl.semaphore_signal(barrier, inc=1, device_id={"src": partner}, device_id_type=MESH)
    across = 1 + (ax + nx - 1) // nx + (2 * nx - 2 - ax) // nx
    along = 1 + (ay + ny - 1) // ny + (2 * ny - 2 - ay) // ny
    pl.semaphore_wait(barrier, across * along)

    local = pltpu.make_async_copy(
        x_ref, wide.at[:, pl.ds(hx, cx), pl.ds(hy, cy), :], local_sem
    )
    local.start()
    direct, relayed = [], []
    for k, (dx, dy) in enumerate(steps):
        src_x, dst_x = window(dx, cx, hx)
        if dy != 0 and dx < 0:
            src_x, dst_x = pl.ds(0, hx - 1), pl.ds(cx + hx, hx - 1)
        if dy != 0 and dx > 0:
            src_x, dst_x = pl.ds(cx - hx + 1, hx - 1), pl.ds(1, hx - 1)
        src_y, dst_y = window(dy, cy, hy)
        tx = jnp.clip(ax + dx, 0, nx - 1)
        ty = jnp.clip(ay + dy, 0, ny - 1)
        for f in range(fields):
            slot = k * fields + f
            copy = pltpu.make_async_remote_copy(
                src_ref=x_ref.at[f, src_x, src_y, :],
                dst_ref=wide.at[f, dst_x, dst_y, :],
                send_sem=send_sem.at[slot],
                recv_sem=recv_sem.at[slot],
                device_id={"gx": tx, "gy": ty},
                device_id_type=MESH,
            )
            relay = None if f < own_fields else pltpu.make_async_remote_copy(
                src_ref=wide.at[f, dst_x, dst_y, :],
                dst_ref=wide.at[f, dst_x, dst_y, :],
                send_sem=fwd_send.at[slot],
                recv_sem=fwd_recv.at[slot],
                device_id={"src": partner},
                device_id_type=MESH,
            )
            mine = True if f < own_fields else ((f - own_fields) % 2 == half)
            direct.append((copy, relay, dx, dy, f, mine))

            @pl.when(exists(dx, dy) & mine)
            def _():
                copy.start()

    local.wait()
    for copy, relay, dx, dy, f, mine in direct:
        if f >= own_fields:
            @pl.when(exists(-dx, -dy) & mine)
            def _():
                copy.wait_recv()
                relay.start()
    for copy, relay, dx, dy, f, mine in direct:
        @pl.when(exists(dx, dy) & mine)
        def _():
            copy.wait_send()

        if f < own_fields:
            @pl.when(exists(-dx, -dy))
            def _():
                copy.wait_recv()
        else:
            @pl.when(exists(-dx, -dy) & mine)
            def _():
                relay.wait_send()

            @pl.when(exists(-dx, -dy) & jnp.logical_not(mine))
            def _():
                relay.wait_recv()

    o_ref[...] = wide[...]


def halo_block(x, hx, hy, cid, own_fields=None):
    fields, cx, cy, cz = x.shape
    own_fields = fields if own_fields is None else own_fields
    shape = (fields, cx + 2 * hx, cy + 2 * hy, cz)
    return pl.pallas_call(
        functools.partial(_halo_kernel, hx, hy, own_fields),
        out_shape=jax.ShapeDtypeStruct(shape, x.dtype),
        in_specs=[pl.BlockSpec(memory_space=pltpu.VMEM)],
        out_specs=pl.BlockSpec(memory_space=pltpu.VMEM),
        scratch_shapes=[
            pltpu.VMEM(shape, x.dtype),
            pltpu.SemaphoreType.DMA((8 * fields,)),
            pltpu.SemaphoreType.DMA((8 * fields,)),
            pltpu.SemaphoreType.DMA,
            pltpu.SemaphoreType.DMA((8 * fields,)),
            pltpu.SemaphoreType.DMA((8 * fields,)),
        ],
        compiler_params=pltpu.CompilerParams(
            collective_id=cid, has_side_effects=True, vmem_limit_bytes=48 * 1024 * 1024
        ),
    )(x)

def _group(axes):
    sizes = [lax.axis_size(axis) for axis in axes]
    n = 1
    for size in sizes:
        n *= size
    me = 0
    for axis, size in zip(axes, sizes):
        me = me * size + lax.axis_index(axis)

    def member(index):
        ids = {}
        for axis, size in reversed(list(zip(axes, sizes))):
            ids[axis] = index % size
            index = index // size
        return ids

    return n, me, member


def _reduce_kernel(stages, scatter, *refs):
    if scatter:
        g_ref, x_ref, h_ref, o_ref, g_slots, g_send, g_recv, g_local = refs[:8]
        scratch = refs[8:]
    else:
        x_ref, o_ref = refs[:2]
        scratch = refs[2:]
    count = len(stages)
    slots, sends, recvs = scratch[:count], scratch[count : 2 * count], scratch[2 * count : 3 * count]
    held = scratch[3 * count :]
    barrier = pltpu.get_barrier_semaphore()
    peers = 0
    for axes in stages:
        n, me, member = _group(axes)
        for k in range(1, n):
            pl.semaphore_signal(
                barrier, inc=1, device_id=member(lax.rem(me + k, n)), device_id_type=MESH
            )
        peers += n - 1
    pl.semaphore_wait(barrier, peers)
    if scatter:
        n = lax.axis_size("src")
        me = lax.axis_index("src")
        parts = []
        for k in range(1, n):
            peer = lax.rem(me + k, n)
            part = pltpu.make_async_remote_copy(
                src_ref=g_ref.at[peer],
                dst_ref=g_slots.at[me],
                send_sem=g_send.at[k - 1],
                recv_sem=g_recv.at[k - 1],
                device_id={"src": peer},
                device_id_type=MESH,
            )
            part.start()
            parts.append(part)
        own = pltpu.make_async_copy(g_ref.at[me], g_slots.at[me], g_local)
        own.start()
    value = x_ref
    for i, axes in enumerate(stages):
        n, me, member = _group(axes)
        copies = []
        for k in range(1, n):
            copy = pltpu.make_async_remote_copy(
                src_ref=value,
                dst_ref=slots[i].at[me],
                send_sem=sends[i].at[k - 1],
                recv_sem=recvs[i].at[k - 1],
                device_id=member(lax.rem(me + k, n)),
                device_id_type=MESH,
            )
            copy.start()
            copies.append(copy)
        slots[i][me] = value[...]
        for copy in copies:
            copy.wait()
        total = slots[i][0]
        for j in range(1, n):
            total = total + slots[i][j]
        if i + 1 < count:
            held[i][...] = total
            value = held[i]
        else:
            o_ref[...] = total
    if scatter:
        own.wait()
        for part in parts:
            part.wait()
        total = g_slots[0]
        for j in range(1, lax.axis_size("src")):
            total = total + g_slots[j]
        h_ref[...] = total

def small_sum(values, axes, cid, spread=None):
    count = values.shape[0]
    rows = -(-count // 1024) * 8
    packed = jnp.pad(values, (0, rows * 128 - count)).reshape(rows, 128)
    stages = tuple(tuple(axis) if isinstance(axis, tuple) else (axis,) for axis in axes)
    sizes = [_group(axis)[0] for axis in stages]
    scratch = (
        [pltpu.VMEM((n, rows, 128), jnp.float32) for n in sizes]
        + [pltpu.SemaphoreType.DMA((n - 1,)) for n in sizes]
        + [pltpu.SemaphoreType.DMA((n - 1,)) for n in sizes]
        + [pltpu.VMEM((rows, 128), jnp.float32) for n in sizes[:-1]]
    )
    vmem = pl.BlockSpec(memory_space=pltpu.VMEM)
    small = jax.ShapeDtypeStruct((rows, 128), jnp.float32)
    operands, out_shape, out_specs = (packed,), small, vmem
    if spread is not None:
        n = spread.shape[0]
        scratch = [
            pltpu.VMEM(spread.shape, jnp.float32),
            pltpu.SemaphoreType.DMA((n - 1,)),
            pltpu.SemaphoreType.DMA((n - 1,)),
            pltpu.SemaphoreType.DMA,
        ] + scratch
        operands = (spread, packed)
        out_shape = (jax.ShapeDtypeStruct(spread.shape[1:], jnp.float32), small)
        out_specs = (vmem, vmem)
    result = pl.pallas_call(
        functools.partial(_reduce_kernel, stages, spread is not None),
        out_shape=out_shape,
        in_specs=[vmem] * len(operands),
        out_specs=out_specs,
        scratch_shapes=scratch,
        compiler_params=pltpu.CompilerParams(collective_id=cid, has_side_effects=True),
    )(*operands)
    if spread is not None:
        return result[0], result[1].reshape(-1)[:count]
    return result.reshape(-1)[:count]


def padded_2(block, sides, width):
    for axis, dim in sides:
        count = lax.axis_size(axis)
        forward = [(i, i + 1) for i in range(count - 1)]
        backward = [(target, source) for source, target in forward]
        low = lax.ppermute(
            lax.slice_in_dim(block, block.shape[dim] - width, None, axis=dim), axis, forward
        )
        high = lax.ppermute(lax.slice_in_dim(block, 0, width, axis=dim), axis, backward)
        block = jnp.concatenate([low, block, high], axis=dim)
    return block


def regional(labels, table):
    field = jnp.zeros(labels.shape, jnp.float32)
    for region in range(table.shape[0]):
        field = field + jnp.where(labels == region, table[region], 0.0)
    return field


def beside(padded):
    widths = [(0, 0)] * (padded.ndim - 1) + [(1, 1)]
    full = jnp.pad(padded, widths)
    return [
        full[..., 2:, 1:-1, 1:-1],
        full[..., :-2, 1:-1, 1:-1],
        full[..., 1:-1, 2:, 1:-1],
        full[..., 1:-1, :-2, 1:-1],
        full[..., 1:-1, 1:-1, 2:],
        full[..., 1:-1, 1:-1, :-2],
    ]


def around(field):
    widths = [(0, 0)] * (field.ndim - 3) + [(1, 1)] * 3
    full = jnp.pad(field, widths)
    return [
        full[..., 2:, 1:-1, 1:-1],
        full[..., :-2, 1:-1, 1:-1],
        full[..., 1:-1, 2:, 1:-1],
        full[..., 1:-1, :-2, 1:-1],
        full[..., 1:-1, 1:-1, 2:],
        full[..., 1:-1, 1:-1, :-2],
    ]


def chebyshev(rhs, apply_op):
    theta = 0.5 * (lam_high + lam_low)
    delta = 0.5 * (lam_high - lam_low)
    sigma = theta / delta
    rho = 1.0 / sigma
    solution = jnp.zeros_like(rhs)
    remain = rhs
    step_dir = rhs / theta
    for step in range(ITERS):
        solution = solution + step_dir
        if step + 1 < ITERS:
            remain = remain - apply_op(step_dir)
            rho_next = 1.0 / (2.0 * sigma - rho)
            step_dir = rho_next * rho * step_dir + 2.0 * rho_next / delta * remain
            rho = rho_next
    return solution


def per_device(
    labels,
    kappa_table,
    absorb_table,
    background,
    det_cells,
    v_kappa,
    v_absorb,
    q_kappa,
    q_absorb,
    beta_prev,
):
    sources, cx, cy, cz = background.shape
    n_src = lax.axis_size("src")
    slab = v_kappa.shape[2]
    pair = jnp.stack([v_kappa, v_absorb]).reshape(-1, 128)
    gathered = exchange(pair, "src", 0).reshape((n_src, 2, cx, cy, slab))
    full_k, full_a = jnp.transpose(gathered, (1, 2, 3, 0, 4)).reshape(2, cx, cy, cz)
    width = ITERS
    width_y = 8
    region_of = labels.astype(jnp.float32)[None]
    stacked = jnp.concatenate([background, region_of, full_k[None], full_a[None]], axis=0)
    wide = halo_block(stacked, width, width_y, 10, own_fields=sources)
    phi_w, region_w, vk_w, va_w = wide[:sources], wide[sources], wide[sources + 1], wide[sources + 2]
    wx = cx + 2 * width
    wy = cy + 2 * width_y
    gx_at = lax.axis_index("gx") * cx - width + jnp.arange(wx)
    gy_at = lax.axis_index("gy") * cy - width_y + jnp.arange(wy)
    inside = ((gx_at >= 0) & (gx_at < cx * lax.axis_size("gx")))[:, None, None] & (
        (gy_at >= 0) & (gy_at < cy * lax.axis_size("gy"))
    )[None, :, None]
    mask = inside.astype(jnp.float32)
    regions = kappa_table.shape[0]
    label_hot = (region_w.reshape(1, -1) == jnp.arange(regions, dtype=jnp.float32)[:, None]).astype(jnp.float32)
    tables = jnp.stack([kappa_table, absorb_table])
    fields = jnp.dot(tables, label_hot, precision=lax.Precision.HIGHEST).reshape(2, wx, wy, cz)
    kappa_w, absorb_w = mask * fields[0], mask * fields[1]
    kappa_faces = [mask * (0.5 * (kappa_w + near)) for near in around(kappa_w)]
    vk_faces = [mask * (0.5 * (vk_w + near)) for near in around(vk_w)]

    def apply_op(field):
        result = absorb_w * field
        for face, near in zip(kappa_faces, around(field)):
            result = result + face * (field - near)
        return result

    rhs = va_w * phi_w
    for face, near in zip(vk_faces, around(phi_w)):
        rhs = rhs + face * (phi_w - near)
    rhs = -rhs
    change = chebyshev(rhs, apply_op)[:, width : width + cx, width_y : width_y + cy, :]
    span_y = cy * lax.axis_size("gy")
    ix = det_cells // (span_y * cz)
    iy = det_cells // cz % span_y
    iz = det_cells % cz
    anchor_x = lax.axis_index("gx") * cx
    anchor_y = lax.axis_index("gy") * cy
    owned = (ix >= anchor_x) & (ix < anchor_x + cx) & (iy >= anchor_y) & (iy < anchor_y + cy)
    plane = (ix - anchor_x) * cy + (iy - anchor_y)
    plane_hot = (jnp.arange(cx * cy)[:, None] == plane[None, :]) & owned[None, :]
    depth_hot = (jnp.arange(cz)[:, None] == iz[None, :]).astype(jnp.float32)
    both = jnp.concatenate([change, background], axis=0).reshape(2 * sources, cx * cy, cz)
    picked = jnp.einsum(
        "spz,pd->szd", both, plane_hot.astype(jnp.float32), precision=lax.Precision.HIGHEST
    )
    picked = jnp.sum(picked * depth_hot[None], axis=1)
    picks = small_sum(picked.reshape(-1), ("gy", "gx"), 1).reshape(2 * sources, -1)
    seen, base = picks[:sources], picks[sources:]
    total = jnp.sum(base, axis=1, keepdims=True)
    mean_base = total / det_cells.shape[0]
    ratio = base / total
    jv_vals = (seen - ratio * jnp.sum(seen, axis=1, keepdims=True)) / mean_base
    weight = (jv_vals - jnp.sum(ratio * jv_vals, axis=1, keepdims=True)) / mean_base
    near_x = ix - (anchor_x - width)
    near_y = iy - (anchor_y - width_y)
    held = (near_x >= 0) & (near_x < wx) & (near_y >= 0) & (near_y < wy)
    wide_hot = (jnp.arange(wx * wy)[:, None] == (near_x * wy + near_y)[None, :]) & held[None, :]
    wide_hot = wide_hot.astype(jnp.float32)
    spread = (weight[:, :, None] * depth_hot.T[None]).transpose(1, 0, 2).reshape(det_cells.shape[0], -1)
    source_w = jnp.dot(wide_hot, spread, precision=lax.Precision.HIGHEST).reshape(wx * wy, sources, cz)
    source_w = source_w.transpose(1, 0, 2).reshape(sources, wx, wy, cz)
    dual_w = chebyshev(source_w, apply_op)
    ring = (slice(None), slice(width - 1, width + cx + 1), slice(width_y - 1, width_y + cy + 1))
    phi_near = beside(phi_w[ring])
    dual_near = beside(dual_w[ring])
    dual = dual_w[:, width : width + cx, width_y : width_y + cy, :]
    grad_a = -jnp.sum(background * dual, axis=0)
    grad_k = jnp.zeros_like(background[0])
    for near_phi, near_dual in zip(phi_near, dual_near):
        grad_k = grad_k - 0.5 * jnp.sum((background - near_phi) * (dual - near_dual), axis=0)
    grads = jnp.stack([grad_k, grad_a]).reshape(2, cx, cy, n_src, slab)
    grads = jnp.transpose(grads, (3, 0, 1, 2, 4)).reshape(n_src, -1, 128)
    local_hv = jnp.sum(grad_k * full_k) + jnp.sum(grad_a * full_a)
    local_qv = jnp.sum(q_kappa * v_kappa) + jnp.sum(q_absorb * v_absorb)
    local_vv = jnp.sum(v_kappa * v_kappa) + jnp.sum(v_absorb * v_absorb)
    hv, dots = small_sum(
        jnp.stack([local_hv, local_qv, local_vv]), (("gx", "gy"), "src"), 3, spread=grads
    )
    hv = hv.reshape(2, cx, cy, slab)
    hv_k, hv_a = hv[0], hv[1]
    cell_count = cx * lax.axis_size("gx") * cy * lax.axis_size("gy") * cz
    w_k = hv_k - beta_prev[0] * q_kappa
    w_a = hv_a - beta_prev[0] * q_absorb
    wv_sum = dots[0] - beta_prev[0] * dots[1]
    vv_sum = dots[2]
    alpha = wv_sum / cell_count / (vv_sum / cell_count + eps_norm)
    r_k = w_k - alpha * v_kappa
    r_a = w_a - alpha * v_absorb
    rr_sum = small_sum((jnp.sum(r_k * r_k) + jnp.sum(r_a * r_a))[None], (("gx", "gy"), "src"), 7)[0]
    beta = jnp.sqrt(rr_sum / cell_count + eps_norm)
    return (r_k / beta, r_a / beta, jnp.stack([alpha, beta]))


def solution(mesh):
    return jax.shard_map(
        per_device,
        mesh=mesh,
        in_specs=(
            P("gx", "gy", None),
            P(),
            P(),
            P("src", "gx", "gy", None),
            P(),
            P("gx", "gy", "src"),
            P("gx", "gy", "src"),
            P("gx", "gy", "src"),
            P("gx", "gy", "src"),
            P(),
        ),
        out_specs=(P("gx", "gy", "src"), P("gx", "gy", "src"), P()),
        check_vma=False,
    )
```

```python
import functools

import jax
import jax.numpy as jnp
from jax import lax
from jax.experimental import pallas as pl
from jax.experimental.pallas import tpu as pltpu
from jax.sharding import PartitionSpec as P

ITERS = 6
MESH = pl.DeviceIdType.MESH


lam_low = 0.02
lam_high = 24.1
eps_norm = 1e-06


def _exchange_kernel(axis, n, scatter, x_ref, o_ref, slots, send_sem, recv_sem, local_sem):
    me = lax.axis_index(axis)
    barrier = pltpu.get_barrier_semaphore()
    for k in range(1, n):
        peer = lax.rem(me + k, n)
        pl.semaphore_signal(barrier, inc=1, device_id={axis: peer}, device_id_type=MESH)
    pl.semaphore_wait(barrier, n - 1)
    copies = []
    for k in range(1, n):
        peer = lax.rem(me + k, n)
        copy = pltpu.make_async_remote_copy(
            src_ref=x_ref.at[peer] if scatter else x_ref,
            dst_ref=slots.at[me],
            send_sem=send_sem.at[k - 1],
            recv_sem=recv_sem.at[k - 1],
            device_id={axis: peer},
            device_id_type=MESH,
        )
        copy.start()
        copies.append(copy)
    local = pltpu.make_async_copy(x_ref.at[me] if scatter else x_ref, slots.at[me], local_sem)
    local.start()
    local.wait()
    for copy in copies:
        copy.wait()
    o_ref[...] = slots[...]


def exchange(x, axis, cid, scatter=False):
    n = lax.axis_size(axis)
    block = x.shape[1:] if scatter else x.shape
    return pl.pallas_call(
        functools.partial(_exchange_kernel, axis, n, scatter),
        out_shape=jax.ShapeDtypeStruct((n,) + block, x.dtype),
        in_specs=[pl.BlockSpec(memory_space=pltpu.VMEM)],
        out_specs=pl.BlockSpec(memory_space=pltpu.VMEM),
        scratch_shapes=[
            pltpu.VMEM((n,) + block, x.dtype),
            pltpu.SemaphoreType.DMA((n - 1,)),
            pltpu.SemaphoreType.DMA((n - 1,)),
            pltpu.SemaphoreType.DMA,
        ],
        compiler_params=pltpu.CompilerParams(collective_id=cid, has_side_effects=True),
    )(x)


def _halo_kernel(hx, hy, own_fields, x_ref, o_ref, wide, send_sem, recv_sem, local_sem, fwd_send, fwd_recv):
    fields, cx, cy, cz = x_ref.shape
    ax, ay = lax.axis_index("gx"), lax.axis_index("gy")
    nx, ny = lax.axis_size("gx"), lax.axis_size("gy")
    me_src = lax.axis_index("src")
    half = me_src % 2
    partner = me_src + 1 - 2 * half
    wide[...] = jnp.zeros_like(wide)
    steps = [(-1, 0), (1, 0), (0, -1), (0, 1), (-1, -1), (-1, 1), (1, -1), (1, 1)]

    def exists(dx, dy):
        return (ax + dx >= 0) & (ax + dx < nx) & (ay + dy >= 0) & (ay + dy < ny)

    def window(d, block, halo):
        if d < 0:
            return pl.ds(0, halo), pl.ds(block + halo, halo)
        if d > 0:
            return pl.ds(block - halo, halo), pl.ds(0, halo)
        return pl.ds(0, block), pl.ds(halo, block)

    barrier = pltpu.get_barrier_semaphore()
    for dx, dy in steps:
        @pl.when(exists(dx, dy))
        def _():
            pl.semaphore_signal(
                barrier, inc=1, device_id={"gx": ax + dx, "gy": ay + dy}, device_id_type=MESH
            )
    pl.semaphore_signal(barrier, inc=1, device_id={"src": partner}, device_id_type=MESH)
    across = 1 + (ax + nx - 1) // nx + (2 * nx - 2 - ax) // nx
    along = 1 + (ay + ny - 1) // ny + (2 * ny - 2 - ay) // ny
    pl.semaphore_wait(barrier, across * along)

    local = pltpu.make_async_copy(
        x_ref, wide.at[:, pl.ds(hx, cx), pl.ds(hy, cy), :], local_sem
    )
    local.start()
    direct = []
    for k, (dx, dy) in enumerate(steps):
        src_x, dst_x = window(dx, cx, hx)
        if dy != 0 and dx < 0:
            src_x, dst_x = pl.ds(0, hx - 1), pl.ds(cx + hx, hx - 1)
        if dy != 0 and dx > 0:
            src_x, dst_x = pl.ds(cx - hx + 1, hx - 1), pl.ds(1, hx - 1)
        tx = jnp.clip(ax + dx, 0, nx - 1)
        ty = jnp.clip(ay + dy, 0, ny - 1)
        for f in range(fields):
            parts = 2 if (f >= own_fields and dy == 0) else 1
            for part in range(parts):
                if parts == 2:
                    rows = cy // 2
                    src_y, dst_y = pl.ds(part * rows, rows), pl.ds(hy + part * rows, rows)
                else:
                    src_y, dst_y = window(dy, cy, hy)
                slot = (k * fields + f) * 2 + part
                copy = pltpu.make_async_remote_copy(
                    src_ref=x_ref.at[f, src_x, src_y, :],
                    dst_ref=wide.at[f, dst_x, dst_y, :],
                    send_sem=send_sem.at[slot],
                    recv_sem=recv_sem.at[slot],
                    device_id={"gx": tx, "gy": ty},
                    device_id_type=MESH,
                )
                relay = None if f < own_fields else pltpu.make_async_remote_copy(
                    src_ref=wide.at[f, dst_x, dst_y, :],
                    dst_ref=wide.at[f, dst_x, dst_y, :],
                    send_sem=fwd_send.at[slot],
                    recv_sem=fwd_recv.at[slot],
                    device_id={"src": partner},
                    device_id_type=MESH,
                )
                mine = True if f < own_fields else ((f - own_fields + part) % 2 == half)
                direct.append((copy, relay, dx, dy, f, mine))

                @pl.when(exists(dx, dy) & mine)
                def _():
                    copy.start()

    local.wait()
    for copy, relay, dx, dy, f, mine in direct:
        if f >= own_fields:
            @pl.when(exists(-dx, -dy) & mine)
            def _():
                copy.wait_recv()
                relay.start()
    for copy, relay, dx, dy, f, mine in direct:
        @pl.when(exists(dx, dy) & mine)
        def _():
            copy.wait_send()

        if f < own_fields:
            @pl.when(exists(-dx, -dy))
            def _():
                copy.wait_recv()
        else:
            @pl.when(exists(-dx, -dy) & mine)
            def _():
                relay.wait_send()

            @pl.when(exists(-dx, -dy) & jnp.logical_not(mine))
            def _():
                relay.wait_recv()

    o_ref[...] = wide[...]


def halo_block(x, hx, hy, cid, own_fields=None):
    fields, cx, cy, cz = x.shape
    own_fields = fields if own_fields is None else own_fields
    shape = (fields, cx + 2 * hx, cy + 2 * hy, cz)
    return pl.pallas_call(
        functools.partial(_halo_kernel, hx, hy, own_fields),
        out_shape=jax.ShapeDtypeStruct(shape, x.dtype),
        in_specs=[pl.BlockSpec(memory_space=pltpu.VMEM)],
        out_specs=pl.BlockSpec(memory_space=pltpu.VMEM),
        scratch_shapes=[
            pltpu.VMEM(shape, x.dtype),
            pltpu.SemaphoreType.DMA((16 * fields,)),
            pltpu.SemaphoreType.DMA((16 * fields,)),
            pltpu.SemaphoreType.DMA,
            pltpu.SemaphoreType.DMA((16 * fields,)),
            pltpu.SemaphoreType.DMA((16 * fields,)),
        ],
        compiler_params=pltpu.CompilerParams(
            collective_id=cid, has_side_effects=True, vmem_limit_bytes=48 * 1024 * 1024
        ),
    )(x)

def _group(axes):
    sizes = [lax.axis_size(axis) for axis in axes]
    n = 1
    for size in sizes:
        n *= size
    me = 0
    for axis, size in zip(axes, sizes):
        me = me * size + lax.axis_index(axis)

    def member(index):
        ids = {}
        for axis, size in reversed(list(zip(axes, sizes))):
            ids[axis] = index % size
            index = index // size
        return ids

    return n, me, member


def _reduce_kernel(stages, scatter, *refs):
    if scatter:
        g_ref, x_ref, h_ref, o_ref, g_slots, g_send, g_recv, g_local = refs[:8]
        scratch = refs[8:]
    else:
        x_ref, o_ref = refs[:2]
        scratch = refs[2:]
    count = len(stages)
    slots, sends, recvs = scratch[:count], scratch[count : 2 * count], scratch[2 * count : 3 * count]
    held = scratch[3 * count :]
    barrier = pltpu.get_barrier_semaphore()
    peers = 0
    for axes in stages:
        n, me, member = _group(axes)
        for k in range(1, n):
            pl.semaphore_signal(
                barrier, inc=1, device_id=member(lax.rem(me + k, n)), device_id_type=MESH
            )
        peers += n - 1
    pl.semaphore_wait(barrier, peers)
    if scatter:
        n = lax.axis_size("src")
        me = lax.axis_index("src")
        parts = []
        for k in range(1, n):
            peer = lax.rem(me + k, n)
            part = pltpu.make_async_remote_copy(
                src_ref=g_ref.at[peer],
                dst_ref=g_slots.at[me],
                send_sem=g_send.at[k - 1],
                recv_sem=g_recv.at[k - 1],
                device_id={"src": peer},
                device_id_type=MESH,
            )
            part.start()
            parts.append(part)
        own = pltpu.make_async_copy(g_ref.at[me], g_slots.at[me], g_local)
        own.start()
    value = x_ref
    for i, axes in enumerate(stages):
        n, me, member = _group(axes)
        copies = []
        for k in range(1, n):
            copy = pltpu.make_async_remote_copy(
                src_ref=value,
                dst_ref=slots[i].at[me],
                send_sem=sends[i].at[k - 1],
                recv_sem=recvs[i].at[k - 1],
                device_id=member(lax.rem(me + k, n)),
                device_id_type=MESH,
            )
            copy.start()
            copies.append(copy)
        slots[i][me] = value[...]
        for copy in copies:
            copy.wait()
        total = slots[i][0]
        for j in range(1, n):
            total = total + slots[i][j]
        if i + 1 < count:
            held[i][...] = total
            value = held[i]
        else:
            o_ref[...] = total
    if scatter:
        own.wait()
        for part in parts:
            part.wait()
        total = g_slots[0]
        for j in range(1, lax.axis_size("src")):
            total = total + g_slots[j]
        h_ref[...] = total

def small_sum(values, axes, cid, spread=None):
    count = values.shape[0]
    rows = -(-count // 1024) * 8
    packed = jnp.pad(values, (0, rows * 128 - count)).reshape(rows, 128)
    stages = tuple(tuple(axis) if isinstance(axis, tuple) else (axis,) for axis in axes)
    sizes = [_group(axis)[0] for axis in stages]
    scratch = (
        [pltpu.VMEM((n, rows, 128), jnp.float32) for n in sizes]
        + [pltpu.SemaphoreType.DMA((n - 1,)) for n in sizes]
        + [pltpu.SemaphoreType.DMA((n - 1,)) for n in sizes]
        + [pltpu.VMEM((rows, 128), jnp.float32) for n in sizes[:-1]]
    )
    vmem = pl.BlockSpec(memory_space=pltpu.VMEM)
    small = jax.ShapeDtypeStruct((rows, 128), jnp.float32)
    operands, out_shape, out_specs = (packed,), small, vmem
    if spread is not None:
        n = spread.shape[0]
        scratch = [
            pltpu.VMEM(spread.shape, jnp.float32),
            pltpu.SemaphoreType.DMA((n - 1,)),
            pltpu.SemaphoreType.DMA((n - 1,)),
            pltpu.SemaphoreType.DMA,
        ] + scratch
        operands = (spread, packed)
        out_shape = (jax.ShapeDtypeStruct(spread.shape[1:], jnp.float32), small)
        out_specs = (vmem, vmem)
    result = pl.pallas_call(
        functools.partial(_reduce_kernel, stages, spread is not None),
        out_shape=out_shape,
        in_specs=[vmem] * len(operands),
        out_specs=out_specs,
        scratch_shapes=scratch,
        compiler_params=pltpu.CompilerParams(collective_id=cid, has_side_effects=True),
    )(*operands)
    if spread is not None:
        return result[0], result[1].reshape(-1)[:count]
    return result.reshape(-1)[:count]


def padded_2(block, sides, width):
    for axis, dim in sides:
        count = lax.axis_size(axis)
        forward = [(i, i + 1) for i in range(count - 1)]
        backward = [(target, source) for source, target in forward]
        low = lax.ppermute(
            lax.slice_in_dim(block, block.shape[dim] - width, None, axis=dim), axis, forward
        )
        high = lax.ppermute(lax.slice_in_dim(block, 0, width, axis=dim), axis, backward)
        block = jnp.concatenate([low, block, high], axis=dim)
    return block


def regional(labels, table):
    field = jnp.zeros(labels.shape, jnp.float32)
    for region in range(table.shape[0]):
        field = field + jnp.where(labels == region, table[region], 0.0)
    return field


def beside(padded):
    widths = [(0, 0)] * (padded.ndim - 1) + [(1, 1)]
    full = jnp.pad(padded, widths)
    return [
        full[..., 2:, 1:-1, 1:-1],
        full[..., :-2, 1:-1, 1:-1],
        full[..., 1:-1, 2:, 1:-1],
        full[..., 1:-1, :-2, 1:-1],
        full[..., 1:-1, 1:-1, 2:],
        full[..., 1:-1, 1:-1, :-2],
    ]


def around(field):
    widths = [(0, 0)] * (field.ndim - 3) + [(1, 1)] * 3
    full = jnp.pad(field, widths)
    return [
        full[..., 2:, 1:-1, 1:-1],
        full[..., :-2, 1:-1, 1:-1],
        full[..., 1:-1, 2:, 1:-1],
        full[..., 1:-1, :-2, 1:-1],
        full[..., 1:-1, 1:-1, 2:],
        full[..., 1:-1, 1:-1, :-2],
    ]


def chebyshev(rhs, apply_op):
    theta = 0.5 * (lam_high + lam_low)
    delta = 0.5 * (lam_high - lam_low)
    sigma = theta / delta
    rho = 1.0 / sigma
    solution = jnp.zeros_like(rhs)
    remain = rhs
    step_dir = rhs / theta
    for step in range(ITERS):
        solution = solution + step_dir
        if step + 1 < ITERS:
            remain = remain - apply_op(step_dir)
            rho_next = 1.0 / (2.0 * sigma - rho)
            step_dir = rho_next * rho * step_dir + 2.0 * rho_next / delta * remain
            rho = rho_next
    return solution


def per_device(
    labels,
    kappa_table,
    absorb_table,
    background,
    det_cells,
    v_kappa,
    v_absorb,
    q_kappa,
    q_absorb,
    beta_prev,
):
    sources, cx, cy, cz = background.shape
    n_src = lax.axis_size("src")
    slab = v_kappa.shape[2]
    pair = jnp.stack([v_kappa, v_absorb]).reshape(-1, 128)
    gathered = exchange(pair, "src", 0).reshape((n_src, 2, cx, cy, slab))
    full_k, full_a = jnp.transpose(gathered, (1, 2, 3, 0, 4)).reshape(2, cx, cy, cz)
    width = ITERS
    width_y = 8
    region_of = labels.astype(jnp.float32)[None]
    stacked = jnp.concatenate([background, region_of, full_k[None], full_a[None]], axis=0)
    wide = halo_block(stacked, width, width_y, 10, own_fields=sources)
    phi_w, region_w, vk_w, va_w = wide[:sources], wide[sources], wide[sources + 1], wide[sources + 2]
    wx = cx + 2 * width
    wy = cy + 2 * width_y
    gx_at = lax.axis_index("gx") * cx - width + jnp.arange(wx)
    gy_at = lax.axis_index("gy") * cy - width_y + jnp.arange(wy)
    inside = ((gx_at >= 0) & (gx_at < cx * lax.axis_size("gx")))[:, None, None] & (
        (gy_at >= 0) & (gy_at < cy * lax.axis_size("gy"))
    )[None, :, None]
    mask = inside.astype(jnp.float32)
    regions = kappa_table.shape[0]
    label_hot = (region_w.reshape(1, -1) == jnp.arange(regions, dtype=jnp.float32)[:, None]).astype(jnp.float32)
    tables = jnp.stack([kappa_table, absorb_table])
    fields = jnp.dot(tables, label_hot, precision=lax.Precision.HIGHEST).reshape(2, wx, wy, cz)
    kappa_w, absorb_w = mask * fields[0], mask * fields[1]
    kappa_faces = [mask * (0.5 * (kappa_w + near)) for near in around(kappa_w)]
    vk_faces = [mask * (0.5 * (vk_w + near)) for near in around(vk_w)]

    def apply_op(field):
        result = absorb_w * field
        for face, near in zip(kappa_faces, around(field)):
            result = result + face * (field - near)
        return result

    rhs = va_w * phi_w
    for face, near in zip(vk_faces, around(phi_w)):
        rhs = rhs + face * (phi_w - near)
    rhs = -rhs
    change = chebyshev(rhs, apply_op)[:, width : width + cx, width_y : width_y + cy, :]
    span_y = cy * lax.axis_size("gy")
    ix = det_cells // (span_y * cz)
    iy = det_cells // cz % span_y
    iz = det_cells % cz
    anchor_x = lax.axis_index("gx") * cx
    anchor_y = lax.axis_index("gy") * cy
    owned = (ix >= anchor_x) & (ix < anchor_x + cx) & (iy >= anchor_y) & (iy < anchor_y + cy)
    plane = (ix - anchor_x) * cy + (iy - anchor_y)
    plane_hot = (jnp.arange(cx * cy)[:, None] == plane[None, :]) & owned[None, :]
    depth_hot = (jnp.arange(cz)[:, None] == iz[None, :]).astype(jnp.float32)
    both = jnp.concatenate([change, background], axis=0).reshape(2 * sources, cx * cy, cz)
    picked = jnp.einsum(
        "spz,pd->szd", both, plane_hot.astype(jnp.float32), precision=lax.Precision.HIGHEST
    )
    picked = jnp.sum(picked * depth_hot[None], axis=1)
    picks = small_sum(picked.reshape(-1), ("gy", "gx"), 1).reshape(2 * sources, -1)
    seen, base = picks[:sources], picks[sources:]
    total = jnp.sum(base, axis=1, keepdims=True)
    mean_base = total / det_cells.shape[0]
    ratio = base / total
    jv_vals = (seen - ratio * jnp.sum(seen, axis=1, keepdims=True)) / mean_base
    weight = (jv_vals - jnp.sum(ratio * jv_vals, axis=1, keepdims=True)) / mean_base
    near_x = ix - (anchor_x - width)
    near_y = iy - (anchor_y - width_y)
    held = (near_x >= 0) & (near_x < wx) & (near_y >= 0) & (near_y < wy)
    wide_hot = (jnp.arange(wx * wy)[:, None] == (near_x * wy + near_y)[None, :]) & held[None, :]
    wide_hot = wide_hot.astype(jnp.float32)
    spread = (weight[:, :, None] * depth_hot.T[None]).transpose(1, 0, 2).reshape(det_cells.shape[0], -1)
    source_w = jnp.dot(wide_hot, spread, precision=lax.Precision.HIGHEST).reshape(wx * wy, sources, cz)
    source_w = source_w.transpose(1, 0, 2).reshape(sources, wx, wy, cz)
    dual_w = chebyshev(source_w, apply_op)
    ring = (slice(None), slice(width - 1, width + cx + 1), slice(width_y - 1, width_y + cy + 1))
    phi_near = beside(phi_w[ring])
    dual_near = beside(dual_w[ring])
    dual = dual_w[:, width : width + cx, width_y : width_y + cy, :]
    grad_a = -jnp.sum(background * dual, axis=0)
    grad_k = jnp.zeros_like(background[0])
    for near_phi, near_dual in zip(phi_near, dual_near):
        grad_k = grad_k - 0.5 * jnp.sum((background - near_phi) * (dual - near_dual), axis=0)
    grads = jnp.stack([grad_k, grad_a]).reshape(2, cx, cy, n_src, slab)
    grads = jnp.transpose(grads, (3, 0, 1, 2, 4)).reshape(n_src, -1, 128)
    local_hv = jnp.sum(grad_k * full_k) + jnp.sum(grad_a * full_a)
    local_qv = jnp.sum(q_kappa * v_kappa) + jnp.sum(q_absorb * v_absorb)
    local_vv = jnp.sum(v_kappa * v_kappa) + jnp.sum(v_absorb * v_absorb)
    hv, dots = small_sum(
        jnp.stack([local_hv, local_qv, local_vv]), (("gx", "gy"), "src"), 3, spread=grads
    )
    hv = hv.reshape(2, cx, cy, slab)
    hv_k, hv_a = hv[0], hv[1]
    cell_count = cx * lax.axis_size("gx") * cy * lax.axis_size("gy") * cz
    w_k = hv_k - beta_prev[0] * q_kappa
    w_a = hv_a - beta_prev[0] * q_absorb
    wv_sum = dots[0] - beta_prev[0] * dots[1]
    vv_sum = dots[2]
    alpha = wv_sum / cell_count / (vv_sum / cell_count + eps_norm)
    r_k = w_k - alpha * v_kappa
    r_a = w_a - alpha * v_absorb
    rr_sum = small_sum((jnp.sum(r_k * r_k) + jnp.sum(r_a * r_a))[None], (("gx", "gy"), "src"), 7)[0]
    beta = jnp.sqrt(rr_sum / cell_count + eps_norm)
    return (r_k / beta, r_a / beta, jnp.stack([alpha, beta]))


def solution(mesh):
    return jax.shard_map(
        per_device,
        mesh=mesh,
        in_specs=(
            P("gx", "gy", None),
            P(),
            P(),
            P("src", "gx", "gy", None),
            P(),
            P("gx", "gy", "src"),
            P("gx", "gy", "src"),
            P("gx", "gy", "src"),
            P("gx", "gy", "src"),
            P(),
        ),
        out_specs=(P("gx", "gy", "src"), P("gx", "gy", "src"), P()),
        check_vma=False,
    )
```

```python
import functools

import jax
import jax.numpy as jnp
from jax import lax
from jax.experimental import pallas as pl
from jax.experimental.pallas import tpu as pltpu
from jax.sharding import PartitionSpec as P

ITERS = 6
MESH = pl.DeviceIdType.MESH


lam_low = 0.02
lam_high = 24.1
eps_norm = 1e-06


def _exchange_kernel(axis, n, scatter, x_ref, o_ref, slots, send_sem, recv_sem, local_sem):
    me = lax.axis_index(axis)
    barrier = pltpu.get_barrier_semaphore()
    for k in range(1, n):
        peer = lax.rem(me + k, n)
        pl.semaphore_signal(barrier, inc=1, device_id={axis: peer}, device_id_type=MESH)
    pl.semaphore_wait(barrier, n - 1)
    copies = []
    for k in range(1, n):
        peer = lax.rem(me + k, n)
        copy = pltpu.make_async_remote_copy(
            src_ref=x_ref.at[peer] if scatter else x_ref,
            dst_ref=slots.at[me],
            send_sem=send_sem.at[k - 1],
            recv_sem=recv_sem.at[k - 1],
            device_id={axis: peer},
            device_id_type=MESH,
        )
        copy.start()
        copies.append(copy)
    local = pltpu.make_async_copy(x_ref.at[me] if scatter else x_ref, slots.at[me], local_sem)
    local.start()
    local.wait()
    for copy in copies:
        copy.wait()
    o_ref[...] = slots[...]


def exchange(x, axis, cid, scatter=False):
    n = lax.axis_size(axis)
    block = x.shape[1:] if scatter else x.shape
    return pl.pallas_call(
        functools.partial(_exchange_kernel, axis, n, scatter),
        out_shape=jax.ShapeDtypeStruct((n,) + block, x.dtype),
        in_specs=[pl.BlockSpec(memory_space=pltpu.VMEM)],
        out_specs=pl.BlockSpec(memory_space=pltpu.VMEM),
        scratch_shapes=[
            pltpu.VMEM((n,) + block, x.dtype),
            pltpu.SemaphoreType.DMA((n - 1,)),
            pltpu.SemaphoreType.DMA((n - 1,)),
            pltpu.SemaphoreType.DMA,
        ],
        compiler_params=pltpu.CompilerParams(collective_id=cid, has_side_effects=True),
    )(x)


def _halo_kernel(hx, hy, own_fields, trim_last, x_ref, o_ref, wide, send_sem, recv_sem, local_sem, fwd_send, fwd_recv):
    fields, cx, cy, cz = x_ref.shape
    ax, ay = lax.axis_index("gx"), lax.axis_index("gy")
    nx, ny = lax.axis_size("gx"), lax.axis_size("gy")
    me_src = lax.axis_index("src")
    half = me_src % 2
    partner = me_src + 1 - 2 * half
    wide[...] = jnp.zeros_like(wide)
    steps = [(-1, 0), (1, 0), (0, -1), (0, 1), (-1, -1), (-1, 1), (1, -1), (1, 1)]

    def exists(dx, dy):
        return (ax + dx >= 0) & (ax + dx < nx) & (ay + dy >= 0) & (ay + dy < ny)

    def window(d, block, halo):
        if d < 0:
            return pl.ds(0, halo), pl.ds(block + halo, halo)
        if d > 0:
            return pl.ds(block - halo, halo), pl.ds(0, halo)
        return pl.ds(0, block), pl.ds(halo, block)

    barrier = pltpu.get_barrier_semaphore()
    for dx, dy in steps:
        @pl.when(exists(dx, dy))
        def _():
            pl.semaphore_signal(
                barrier, inc=1, device_id={"gx": ax + dx, "gy": ay + dy}, device_id_type=MESH
            )
    pl.semaphore_signal(barrier, inc=1, device_id={"src": partner}, device_id_type=MESH)
    across = 1 + (ax + nx - 1) // nx + (2 * nx - 2 - ax) // nx
    along = 1 + (ay + ny - 1) // ny + (2 * ny - 2 - ay) // ny
    pl.semaphore_wait(barrier, across * along)

    local = pltpu.make_async_copy(
        x_ref, wide.at[:, pl.ds(hx, cx), pl.ds(hy, cy), :], local_sem
    )
    local.start()
    direct, relayed = [], []
    for k, (dx, dy) in enumerate(steps):
        src_x, dst_x = window(dx, cx, hx)
        if dy != 0 and dx < 0:
            src_x, dst_x = pl.ds(0, hx - 1), pl.ds(cx + hx, hx - 1)
        if dy != 0 and dx > 0:
            src_x, dst_x = pl.ds(cx - hx + 1, hx - 1), pl.ds(1, hx - 1)
        src_y, dst_y = window(dy, cy, hy)
        tx = jnp.clip(ax + dx, 0, nx - 1)
        ty = jnp.clip(ay + dy, 0, ny - 1)
        for f in range(fields):
            slot = k * fields + f
            if trim_last and f == fields - 1 and dx != 0:
                depth = hx - 1 if dy == 0 else hx - 2
                if dx < 0:
                    src_x, dst_x = pl.ds(0, depth), pl.ds(cx + hx, depth)
                else:
                    src_x, dst_x = pl.ds(cx - depth, depth), pl.ds(hx - depth, depth)
            copy = pltpu.make_async_remote_copy(
                src_ref=x_ref.at[f, src_x, src_y, :],
                dst_ref=wide.at[f, dst_x, dst_y, :],
                send_sem=send_sem.at[slot],
                recv_sem=recv_sem.at[slot],
                device_id={"gx": tx, "gy": ty},
                device_id_type=MESH,
            )
            relay = None if f < own_fields else pltpu.make_async_remote_copy(
                src_ref=wide.at[f, dst_x, dst_y, :],
                dst_ref=wide.at[f, dst_x, dst_y, :],
                send_sem=fwd_send.at[slot],
                recv_sem=fwd_recv.at[slot],
                device_id={"src": partner},
                device_id_type=MESH,
            )
            mine = True if f < own_fields else ((f - own_fields) % 2 == half)
            direct.append((copy, relay, dx, dy, f, mine))

            @pl.when(exists(dx, dy) & mine)
            def _():
                copy.start()

    local.wait()
    for copy, relay, dx, dy, f, mine in direct:
        if f >= own_fields:
            @pl.when(exists(-dx, -dy) & mine)
            def _():
                copy.wait_recv()
                relay.start()
    for copy, relay, dx, dy, f, mine in direct:
        @pl.when(exists(dx, dy) & mine)
        def _():
            copy.wait_send()

        if f < own_fields:
            @pl.when(exists(-dx, -dy))
            def _():
                copy.wait_recv()
        else:
            @pl.when(exists(-dx, -dy) & mine)
            def _():
                relay.wait_send()

            @pl.when(exists(-dx, -dy) & jnp.logical_not(mine))
            def _():
                relay.wait_recv()

    o_ref[...] = wide[...]


def halo_block(x, hx, hy, cid, own_fields=None, trim_last=False):
    fields, cx, cy, cz = x.shape
    own_fields = fields if own_fields is None else own_fields
    shape = (fields, cx + 2 * hx, cy + 2 * hy, cz)
    return pl.pallas_call(
        functools.partial(_halo_kernel, hx, hy, own_fields, trim_last),
        out_shape=jax.ShapeDtypeStruct(shape, x.dtype),
        in_specs=[pl.BlockSpec(memory_space=pltpu.VMEM)],
        out_specs=pl.BlockSpec(memory_space=pltpu.VMEM),
        scratch_shapes=[
            pltpu.VMEM(shape, x.dtype),
            pltpu.SemaphoreType.DMA((8 * fields,)),
            pltpu.SemaphoreType.DMA((8 * fields,)),
            pltpu.SemaphoreType.DMA,
            pltpu.SemaphoreType.DMA((8 * fields,)),
            pltpu.SemaphoreType.DMA((8 * fields,)),
        ],
        compiler_params=pltpu.CompilerParams(
            collective_id=cid, has_side_effects=True, vmem_limit_bytes=48 * 1024 * 1024
        ),
    )(x)

def _group(axes):
    sizes = [lax.axis_size(axis) for axis in axes]
    n = 1
    for size in sizes:
        n *= size
    me = 0
    for axis, size in zip(axes, sizes):
        me = me * size + lax.axis_index(axis)

    def member(index):
        ids = {}
        for axis, size in reversed(list(zip(axes, sizes))):
            ids[axis] = index % size
            index = index // size
        return ids

    return n, me, member


def _reduce_kernel(stages, scatter, *refs):
    if scatter:
        g_ref, x_ref, h_ref, o_ref, g_slots, g_send, g_recv, g_local = refs[:8]
        scratch = refs[8:]
    else:
        x_ref, o_ref = refs[:2]
        scratch = refs[2:]
    count = len(stages)
    slots, sends, recvs = scratch[:count], scratch[count : 2 * count], scratch[2 * count : 3 * count]
    held = scratch[3 * count :]
    barrier = pltpu.get_barrier_semaphore()
    peers = 0
    for axes in stages:
        n, me, member = _group(axes)
        for k in range(1, n):
            pl.semaphore_signal(
                barrier, inc=1, device_id=member(lax.rem(me + k, n)), device_id_type=MESH
            )
        peers += n - 1
    pl.semaphore_wait(barrier, peers)
    if scatter:
        n = lax.axis_size("src")
        me = lax.axis_index("src")
        parts = []
        for k in range(1, n):
            peer = lax.rem(me + k, n)
            part = pltpu.make_async_remote_copy(
                src_ref=g_ref.at[peer],
                dst_ref=g_slots.at[me],
                send_sem=g_send.at[k - 1],
                recv_sem=g_recv.at[k - 1],
                device_id={"src": peer},
                device_id_type=MESH,
            )
            part.start()
            parts.append(part)
        own = pltpu.make_async_copy(g_ref.at[me], g_slots.at[me], g_local)
        own.start()
    value = x_ref
    for i, axes in enumerate(stages):
        n, me, member = _group(axes)
        copies = []
        for k in range(1, n):
            copy = pltpu.make_async_remote_copy(
                src_ref=value,
                dst_ref=slots[i].at[me],
                send_sem=sends[i].at[k - 1],
                recv_sem=recvs[i].at[k - 1],
                device_id=member(lax.rem(me + k, n)),
                device_id_type=MESH,
            )
            copy.start()
            copies.append(copy)
        slots[i][me] = value[...]
        for copy in copies:
            copy.wait()
        total = slots[i][0]
        for j in range(1, n):
            total = total + slots[i][j]
        if i + 1 < count:
            held[i][...] = total
            value = held[i]
        else:
            o_ref[...] = total
    if scatter:
        own.wait()
        for part in parts:
            part.wait()
        total = g_slots[0]
        for j in range(1, lax.axis_size("src")):
            total = total + g_slots[j]
        h_ref[...] = total

def small_sum(values, axes, cid, spread=None):
    count = values.shape[0]
    rows = -(-count // 1024) * 8
    packed = jnp.pad(values, (0, rows * 128 - count)).reshape(rows, 128)
    stages = tuple(tuple(axis) if isinstance(axis, tuple) else (axis,) for axis in axes)
    sizes = [_group(axis)[0] for axis in stages]
    scratch = (
        [pltpu.VMEM((n, rows, 128), jnp.float32) for n in sizes]
        + [pltpu.SemaphoreType.DMA((n - 1,)) for n in sizes]
        + [pltpu.SemaphoreType.DMA((n - 1,)) for n in sizes]
        + [pltpu.VMEM((rows, 128), jnp.float32) for n in sizes[:-1]]
    )
    vmem = pl.BlockSpec(memory_space=pltpu.VMEM)
    small = jax.ShapeDtypeStruct((rows, 128), jnp.float32)
    operands, out_shape, out_specs = (packed,), small, vmem
    if spread is not None:
        n = spread.shape[0]
        scratch = [
            pltpu.VMEM(spread.shape, jnp.float32),
            pltpu.SemaphoreType.DMA((n - 1,)),
            pltpu.SemaphoreType.DMA((n - 1,)),
            pltpu.SemaphoreType.DMA,
        ] + scratch
        operands = (spread, packed)
        out_shape = (jax.ShapeDtypeStruct(spread.shape[1:], jnp.float32), small)
        out_specs = (vmem, vmem)
    result = pl.pallas_call(
        functools.partial(_reduce_kernel, stages, spread is not None),
        out_shape=out_shape,
        in_specs=[vmem] * len(operands),
        out_specs=out_specs,
        scratch_shapes=scratch,
        compiler_params=pltpu.CompilerParams(collective_id=cid, has_side_effects=True),
    )(*operands)
    if spread is not None:
        return result[0], result[1].reshape(-1)[:count]
    return result.reshape(-1)[:count]


def padded_2(block, sides, width):
    for axis, dim in sides:
        count = lax.axis_size(axis)
        forward = [(i, i + 1) for i in range(count - 1)]
        backward = [(target, source) for source, target in forward]
        low = lax.ppermute(
            lax.slice_in_dim(block, block.shape[dim] - width, None, axis=dim), axis, forward
        )
        high = lax.ppermute(lax.slice_in_dim(block, 0, width, axis=dim), axis, backward)
        block = jnp.concatenate([low, block, high], axis=dim)
    return block


def regional(labels, table):
    field = jnp.zeros(labels.shape, jnp.float32)
    for region in range(table.shape[0]):
        field = field + jnp.where(labels == region, table[region], 0.0)
    return field


def beside(padded):
    widths = [(0, 0)] * (padded.ndim - 1) + [(1, 1)]
    full = jnp.pad(padded, widths)
    return [
        full[..., 2:, 1:-1, 1:-1],
        full[..., :-2, 1:-1, 1:-1],
        full[..., 1:-1, 2:, 1:-1],
        full[..., 1:-1, :-2, 1:-1],
        full[..., 1:-1, 1:-1, 2:],
        full[..., 1:-1, 1:-1, :-2],
    ]


def around(field):
    widths = [(0, 0)] * (field.ndim - 3) + [(1, 1)] * 3
    full = jnp.pad(field, widths)
    return [
        full[..., 2:, 1:-1, 1:-1],
        full[..., :-2, 1:-1, 1:-1],
        full[..., 1:-1, 2:, 1:-1],
        full[..., 1:-1, :-2, 1:-1],
        full[..., 1:-1, 1:-1, 2:],
        full[..., 1:-1, 1:-1, :-2],
    ]


def chebyshev(rhs, apply_op):
    theta = 0.5 * (lam_high + lam_low)
    delta = 0.5 * (lam_high - lam_low)
    sigma = theta / delta
    rho = 1.0 / sigma
    solution = jnp.zeros_like(rhs)
    remain = rhs
    step_dir = rhs / theta
    for step in range(ITERS):
        solution = solution + step_dir
        if step + 1 < ITERS:
            remain = remain - apply_op(step_dir)
            rho_next = 1.0 / (2.0 * sigma - rho)
            step_dir = rho_next * rho * step_dir + 2.0 * rho_next / delta * remain
            rho = rho_next
    return solution


def per_device(
    labels,
    kappa_table,
    absorb_table,
    background,
    det_cells,
    v_kappa,
    v_absorb,
    q_kappa,
    q_absorb,
    beta_prev,
):
    sources, cx, cy, cz = background.shape
    n_src = lax.axis_size("src")
    slab = v_kappa.shape[2]
    pair = jnp.stack([v_kappa, v_absorb]).reshape(-1, 128)
    gathered = exchange(pair, "src", 0).reshape((n_src, 2, cx, cy, slab))
    full_k, full_a = jnp.transpose(gathered, (1, 2, 3, 0, 4)).reshape(2, cx, cy, cz)
    width = ITERS
    width_y = 8
    region_of = labels.astype(jnp.float32)[None]
    stacked = jnp.concatenate([background, region_of, full_k[None], full_a[None]], axis=0)
    wide = halo_block(stacked, width, width_y, 10, own_fields=sources, trim_last=True)
    phi_w, region_w, vk_w, va_w = wide[:sources], wide[sources], wide[sources + 1], wide[sources + 2]
    wx = cx + 2 * width
    wy = cy + 2 * width_y
    gx_at = lax.axis_index("gx") * cx - width + jnp.arange(wx)
    gy_at = lax.axis_index("gy") * cy - width_y + jnp.arange(wy)
    inside = ((gx_at >= 0) & (gx_at < cx * lax.axis_size("gx")))[:, None, None] & (
        (gy_at >= 0) & (gy_at < cy * lax.axis_size("gy"))
    )[None, :, None]
    mask = inside.astype(jnp.float32)
    regions = kappa_table.shape[0]
    label_hot = (region_w.reshape(1, -1) == jnp.arange(regions, dtype=jnp.float32)[:, None]).astype(jnp.float32)
    tables = jnp.stack([kappa_table, absorb_table])
    fields = jnp.dot(tables, label_hot, precision=lax.Precision.HIGHEST).reshape(2, wx, wy, cz)
    kappa_w, absorb_w = mask * fields[0], mask * fields[1]
    kappa_faces = [mask * (0.5 * (kappa_w + near)) for near in around(kappa_w)]
    vk_faces = [mask * (0.5 * (vk_w + near)) for near in around(vk_w)]

    def apply_op(field):
        result = absorb_w * field
        for face, near in zip(kappa_faces, around(field)):
            result = result + face * (field - near)
        return result

    rhs = va_w * phi_w
    for face, near in zip(vk_faces, around(phi_w)):
        rhs = rhs + face * (phi_w - near)
    rhs = -rhs
    change = chebyshev(rhs, apply_op)[:, width : width + cx, width_y : width_y + cy, :]
    span_y = cy * lax.axis_size("gy")
    ix = det_cells // (span_y * cz)
    iy = det_cells // cz % span_y
    iz = det_cells % cz
    anchor_x = lax.axis_index("gx") * cx
    anchor_y = lax.axis_index("gy") * cy
    owned = (ix >= anchor_x) & (ix < anchor_x + cx) & (iy >= anchor_y) & (iy < anchor_y + cy)
    plane = (ix - anchor_x) * cy + (iy - anchor_y)
    plane_hot = (jnp.arange(cx * cy)[:, None] == plane[None, :]) & owned[None, :]
    depth_hot = (jnp.arange(cz)[:, None] == iz[None, :]).astype(jnp.float32)
    both = jnp.concatenate([change, background], axis=0).reshape(2 * sources, cx * cy, cz)
    picked = jnp.einsum(
        "spz,pd->szd", both, plane_hot.astype(jnp.float32), precision=lax.Precision.HIGHEST
    )
    picked = jnp.sum(picked * depth_hot[None], axis=1)
    picks = small_sum(picked.reshape(-1), ("gy", "gx"), 1).reshape(2 * sources, -1)
    seen, base = picks[:sources], picks[sources:]
    total = jnp.sum(base, axis=1, keepdims=True)
    mean_base = total / det_cells.shape[0]
    ratio = base / total
    jv_vals = (seen - ratio * jnp.sum(seen, axis=1, keepdims=True)) / mean_base
    weight = (jv_vals - jnp.sum(ratio * jv_vals, axis=1, keepdims=True)) / mean_base
    near_x = ix - (anchor_x - width)
    near_y = iy - (anchor_y - width_y)
    held = (near_x >= 0) & (near_x < wx) & (near_y >= 0) & (near_y < wy)
    wide_hot = (jnp.arange(wx * wy)[:, None] == (near_x * wy + near_y)[None, :]) & held[None, :]
    wide_hot = wide_hot.astype(jnp.float32)
    spread = (weight[:, :, None] * depth_hot.T[None]).transpose(1, 0, 2).reshape(det_cells.shape[0], -1)
    source_w = jnp.dot(wide_hot, spread, precision=lax.Precision.HIGHEST).reshape(wx * wy, sources, cz)
    source_w = source_w.transpose(1, 0, 2).reshape(sources, wx, wy, cz)
    dual_w = chebyshev(source_w, apply_op)
    ring = (slice(None), slice(width - 1, width + cx + 1), slice(width_y - 1, width_y + cy + 1))
    phi_near = beside(phi_w[ring])
    dual_near = beside(dual_w[ring])
    dual = dual_w[:, width : width + cx, width_y : width_y + cy, :]
    grad_a = -jnp.sum(background * dual, axis=0)
    grad_k = jnp.zeros_like(background[0])
    for near_phi, near_dual in zip(phi_near, dual_near):
        grad_k = grad_k - 0.5 * jnp.sum((background - near_phi) * (dual - near_dual), axis=0)
    grads = jnp.stack([grad_k, grad_a]).reshape(2, cx, cy, n_src, slab)
    grads = jnp.transpose(grads, (3, 0, 1, 2, 4)).reshape(n_src, -1, 128)
    local_hv = jnp.sum(grad_k * full_k) + jnp.sum(grad_a * full_a)
    local_qv = jnp.sum(q_kappa * v_kappa) + jnp.sum(q_absorb * v_absorb)
    local_vv = jnp.sum(v_kappa * v_kappa) + jnp.sum(v_absorb * v_absorb)
    hv, dots = small_sum(
        jnp.stack([local_hv, local_qv, local_vv]), (("gx", "gy"), "src"), 3, spread=grads
    )
    hv = hv.reshape(2, cx, cy, slab)
    hv_k, hv_a = hv[0], hv[1]
    cell_count = cx * lax.axis_size("gx") * cy * lax.axis_size("gy") * cz
    w_k = hv_k - beta_prev[0] * q_kappa
    w_a = hv_a - beta_prev[0] * q_absorb
    wv_sum = dots[0] - beta_prev[0] * dots[1]
    vv_sum = dots[2]
    alpha = wv_sum / cell_count / (vv_sum / cell_count + eps_norm)
    r_k = w_k - alpha * v_kappa
    r_a = w_a - alpha * v_absorb
    rr_sum = small_sum((jnp.sum(r_k * r_k) + jnp.sum(r_a * r_a))[None], (("gx", "gy"), "src"), 7)[0]
    beta = jnp.sqrt(rr_sum / cell_count + eps_norm)
    return (r_k / beta, r_a / beta, jnp.stack([alpha, beta]))


def solution(mesh):
    return jax.shard_map(
        per_device,
        mesh=mesh,
        in_specs=(
            P("gx", "gy", None),
            P(),
            P(),
            P("src", "gx", "gy", None),
            P(),
            P("gx", "gy", "src"),
            P("gx", "gy", "src"),
            P("gx", "gy", "src"),
            P("gx", "gy", "src"),
            P(),
        ),
        out_specs=(P("gx", "gy", "src"), P("gx", "gy", "src"), P()),
        check_vma=False,
    )
```
